32 devices in a mesh: band: 4 (over z), tile: 8 (over y, x, core).
Axes of the slice: x: 2, y: 2, z: 4, core: 2. Of those that a mesh axis runs over, the one named last changes fastest.
Arguments:
- anomalies: bfloat16 [4, 8, 18, 80, 256], P('band', 'tile'), may hold values from -6 to 6
- forcing: float32 [4, 8, 18, 256], P('band', 'tile'), may hold values from -6 to 6
- pair_code: int32 [4, 8, 8], P('band', 'tile'), may hold values from 0 to 4, as said below
- kernel: float32 [63, 63], replicated, may hold values from 0 to 1
- tile_taper: float32 [4], replicated, may hold values from 0.03 to 0.22
Outputs:
- increment: float32 [4, 8, 18, 256], P('band', 'tile')
- residual: float32 [4, 8, 18, 256], P('band', 'tile')
The draws below stay inside these ranges and needn't reach their ends.
Inputs may be any that keep to these rules, and one draw needn't show every extreme that they name: pair_code[b, l, k] names the pair of tile (b, l) with its neighbour in direction k; the partner's entry for the opposite direction holds the same code; no listed pair crosses the first or the last band.
All inputs are finite; a program needn't handle non-finite values.
Results may differ from the reference program's by a relative error of at most 0.014.
Values may be sent and summed in bfloat16 or wider, within the bound.
No kernel may reach another device: no remote copies, remote signals or barrier semaphores. Data moves between devices by JAX's collectives and lax.ppermute only.
A program may use at most 64 MiB of HBM per device.

```python
import math
import jax
import jax.numpy as jnp
import numpy as np
from jax import lax

SIDE = 16
COLS = 256
MEMBERS = 80
LEVS = 18
TAPERS = 4
ITERS = 2
BANDS = 4
LONS = 8


def shift_south(values):
    return jnp.concatenate([jnp.zeros((1, values.shape[1]), jnp.int32), values[:-1]], axis=0)


def draw_pair_code(key, part):
    subkeys = jax.random.split(key, 2)
    band_rows = jnp.arange(BANDS, dtype=jnp.int32)[:, None]
    distance = jnp.abs(2 * band_rows - (BANDS - 1))
    rolled = jax.random.randint(subkeys[0], (4, BANDS, LONS), 0, BANDS)
    listed = (rolled <= distance[None]).astype(jnp.int32)
    chosen = jax.random.randint(subkeys[1], (4, BANDS, LONS), 1, TAPERS + 1)
    forward = listed * chosen
    north_ok = (band_rows < BANDS - 1).astype(jnp.int32)
    east_code = forward[0]
    northwest = forward[1] * north_ok
    north_code = forward[2] * north_ok
    northeast = forward[3] * north_ok
    west_code = jnp.roll(east_code, 1, axis=1)
    south_code = shift_south(north_code)
    southwest = shift_south(jnp.roll(northeast, 1, axis=1))
    southeast = shift_south(jnp.roll(northwest, -1, axis=1))
    return jnp.stack([southwest, south_code, southeast, west_code, east_code, northwest, north_code, northeast], axis=-1)


def draw_kernel(key, part):
    subkeys = jax.random.split(key, 5)
    span = 2 * SIDE - 1
    offsets = jnp.arange(-span, span + 1).astype(jnp.float32)
    circle = SIDE * LONS
    scale_lat = jax.random.uniform(subkeys[0], (), jnp.float32, 4.0, 12.0)
    scale_lon = jax.random.uniform(subkeys[1], (), jnp.float32, 4.0, 12.0)
    top_freq = math.pi
    top_count = circle // 2
    counts_lon = jax.random.randint(subkeys[2], (8,), 0, top_count)
    freq_lon = counts_lon.astype(jnp.float32) * (2.0 * math.pi / circle)
    freq_lat = jax.random.uniform(subkeys[3], (8,), jnp.float32, 0.0, top_freq)
    amplitude = jax.random.uniform(subkeys[4], (8,), jnp.float32, 0.2, 1.0)
    phases = freq_lat[:, None, None] * offsets[None, :, None] + freq_lon[:, None, None] * offsets[None, None, :]
    waves = jnp.sum(amplitude[:, None, None] * jnp.cos(phases), axis=0) / jnp.sum(amplitude)
    envelope = jnp.exp(-jnp.abs(offsets)[:, None] / scale_lat - jnp.abs(offsets)[None, :] / scale_lon)
    return envelope * (0.5 + 0.5 * waves)


def shard_levels(rng, shape, pieces, least, top_value):
    level, own = 1.0, jax.random.fold_in(rng, 6)
    for axis_at, parts in pieces:
        heights = jnp.exp(jax.random.uniform(jax.random.fold_in(own, axis_at), (parts,), jnp.float32, least / len(pieces), top_value / len(pieces)))
        level = level * jnp.repeat(heights, shape[axis_at] // parts).reshape([-1 if axis == axis_at else 1 for axis in range(len(shape))])
    return level


def bell_draw(stream_key, shape, scale, bound, cuts=(), kind=jnp.bfloat16):
    values = jax.random.normal(stream_key, shape, jnp.float32) * scale
    if len(cuts) > 0:
        values = shard_levels(stream_key, shape, cuts, -0.22, 0.18) * values
    return jnp.clip(values, min=-bound, max=bound).astype(kind)


def setup_inputs(seed: int = 0) -> dict:
    streams_of = jax.random.split(jax.random.key(seed), 6)
    return {
        "anomalies": bell_draw(streams_of[0], (BANDS, LONS, LEVS, MEMBERS, COLS), 1.0, 6.0, ((0, 4), (1, 8))),
        "forcing": bell_draw(streams_of[1], (BANDS, LONS, LEVS, COLS), 1.0, 6.0, ((0, 4), (1, 8)), jnp.float32),
        "pair_code": draw_pair_code(jax.random.fold_in(streams_of[5], 71), 0),
        "kernel": draw_kernel(jax.random.fold_in(streams_of[5], 71), 0),
        "tile_taper": jnp.clip(jax.random.uniform(streams_of[4], (TAPERS,), jnp.float32, 0.03, 0.22), 0.03, 0.22),
    }


DIRECTIONS = ((-1, -1), (-1, 0), (-1, 1), (0, -1), (0, 1), (1, -1), (1, 0), (1, 1))


def local_map(kernel, row_step, col_step):
    tile_side = SIDE
    centre = 2 * tile_side - 1
    first_index = np.arange(tile_side)[:, None]
    second_index = np.arange(tile_side)[None, :]
    lat_index = centre + row_step * tile_side + second_index - first_index
    lon_index = centre + col_step * tile_side + second_index - first_index
    picked = kernel[lat_index[:, None, :, None], lon_index[None, :, None, :]]
    return picked.reshape(tile_side * tile_side, tile_side * tile_side).astype(jnp.bfloat16)


def taper_lookup(tile_taper, code):
    entries = jnp.arange(1, tile_taper.shape[0] + 1, dtype=jnp.int32)
    return jnp.sum(jnp.where(entries == code, tile_taper, jnp.zeros_like(tile_taper)))


def weighted_block(block, field):
    return (block.astype(jnp.float32) * field[:, None, :]).astype(jnp.bfloat16)


def pair_term(own_block, weighted, matrix, weight):
    levels, members, columns = weighted.shape
    spread = jnp.dot(weighted.reshape(levels * members, columns), matrix.T, preferred_element_type=jnp.float32)
    summed = jnp.sum(own_block.astype(jnp.float32) * spread.reshape(levels, members, columns), axis=1)
    return summed * (weight / (members - 1))


def apply_operator(anomalies, values, pair_code, local_maps, tile_taper):
    def one_tile(tile_id):
        band_id = tile_id // LONS
        lon_id = tile_id % LONS
        own_block = anomalies[band_id, lon_id]
        summed_terms = pair_term(own_block, weighted_block(own_block, values[band_id, lon_id]), local_maps[0], 1.0)
        for position, (row_step, col_step) in enumerate(DIRECTIONS):
            other_band = (band_id + row_step) % BANDS
            other_lon = (lon_id + col_step) % LONS
            weight = taper_lookup(tile_taper, pair_code[band_id, lon_id, position])
            other_weighted = weighted_block(anomalies[other_band, other_lon], values[other_band, other_lon])
            summed_terms = summed_terms + pair_term(own_block, other_weighted, local_maps[position + 1], weight)
        return summed_terms

    result = lax.map(one_tile, jnp.arange(BANDS * LONS, dtype=jnp.int32))
    return values + result.reshape(values.shape)


def reference(anomalies, forcing, pair_code, kernel, tile_taper):
    local_maps = [local_map(kernel, 0, 0)] + [local_map(kernel, row_step, col_step) for row_step, col_step in DIRECTIONS]
    increment = jnp.zeros_like(forcing)
    residual = forcing
    direction = forcing
    norm_now = jnp.sum(residual * residual)
    for iteration in range(ITERS):
        mapped = apply_operator(anomalies, direction, pair_code, local_maps, tile_taper)
        step_length = norm_now / jnp.sum(direction * mapped)
        increment = increment + step_length * direction
        residual = residual - step_length * mapped
        norm_next = jnp.sum(residual * residual)
        direction = residual + (norm_next / norm_now) * direction
        norm_now = norm_next
    return increment, residual
```

```python
import functools

import jax
import jax.numpy as jnp
import numpy as np
from jax import lax
from jax.experimental import pallas as pl
from jax.experimental.pallas import tpu as pltpu
from jax.sharding import PartitionSpec as P

SIDE = 16
ITERS = 2
GRAIN = 8
LANES = 128
SLOT = 32

DIRECTIONS = ((-1, -1), (-1, 0), (-1, 1), (0, -1), (0, 1), (1, -1), (1, 0), (1, 1))
ALL_STEPS = ((0, 0),) + DIRECTIONS


class Plan:
    def __init__(self, bands, lons, levels, members, columns):
        self.bands, self.lons = bands, lons
        self.levels, self.members, self.columns = levels, members, columns
        self.count = bands * lons
        self.depth = members // (2 * GRAIN)
        self.rows = GRAIN * (self.depth + 1)
        self.fits = (
            members % (2 * GRAIN) == 0
            and levels % (self.depth + 1) == 0
            and levels <= SLOT
            and lons % GRAIN == 0
            and columns == 2 * LANES
            and self.rows % 16 == 0
        )
        if not self.fits:
            return
        self.groups = levels // (self.depth + 1)
        chips = self.count // 2
        used = self.groups * self.depth
        self.fits = used <= chips < 2 * used
        if not self.fits:
            return
        across = lons // 2
        inner = [i ^ (i >> 1) for i in range(across)]
        if sorted(inner) != list(range(across)):
            inner = list(range(across))
        path = []
        for band in range(bands):
            path += [band * across + c for c in (inner if band % 2 == 0 else inner[::-1])]
        self.path = path
        self.extra = 2 * self.rows
        self.height = self.extra + 16

    def device(self, group, k, core):
        return 2 * self.path[group * self.depth + k] + core

    def owners(self):
        for group in range(self.groups):
            for k in range(self.depth):
                for core in range(2):
                    low = group * (self.depth + 1) + k
                    yield self.device(group, k, core), k, core, low

    def table(self):
        out = np.zeros((self.count, 8), np.int32)
        for device, k, core, low in self.owners():
            last = k == self.depth - 1
            out[device, :5] = (self.depth - k, core, int(core == 0), int(core == 1 and last), low)
        return out

    def onward(self):
        pairs = []
        for group in range(self.groups):
            for k in range(self.depth - 1):
                for core in range(2):
                    pairs.append((self.device(group, k, core), self.device(group, k + 1, core)))
        return pairs


def in_three(x):
    high = x.astype(jnp.bfloat16).astype(jnp.float32)
    rest = x - high
    middle = rest.astype(jnp.bfloat16).astype(jnp.float32)
    return high, middle, rest - middle


def pack_kernel(plan, tapers, code_ref, taper_ref, a_ref, f_ref, out_ref, ext_ref):
    parts = in_three(f_ref[...])
    lane = lax.broadcasted_iota(jnp.int32, (1, LANES), 1)
    weights = jnp.zeros((1, LANES), jnp.float32)
    for k in range(len(DIRECTIONS)):
        code = code_ref[0, 0, k]
        weight = jnp.float32(0)
        for c in range(tapers):
            weight = jnp.where(code == c + 1, taper_ref[c], weight)
        weights = jnp.where(lane == k, weight, weights)
    weights = in_three(weights / jnp.float32(plan.members - 1))
    blank = jnp.zeros((1, LANES), jnp.float32)
    rows, depth = plan.rows, plan.depth
    taken = set()
    for device, k, core, low in plan.owners():
        taken.add(device)
        count = GRAIN * (depth - k)
        start = 2 * k * GRAIN + core * count
        other = GRAIN * (k + 1)
        for half in range(2):
            lanes = slice(half * LANES, (half + 1) * LANES)
            base = half * rows
            out_ref[device, base : base + count, :] = a_ref[low, start : start + count, lanes]
            out_ref[device, base + count : base + rows, :] = a_ref[
                low + 1, core * other : (core + 1) * other, lanes
            ]
            for level in range(2):
                for n, part in enumerate(parts):
                    row = 6 * half + 3 * level + n
                    ext_ref[device, row : row + 1, :] = part[low + level : low + level + 1, lanes]
        for n, part in enumerate(weights):
            ext_ref[device, 12 + n : 13 + n, :] = part
        ext_ref[device, 15:16, :] = blank
    for device in range(plan.count):
        if device in taken:
            out_ref[device, plan.extra : plan.extra + 16, :] = ext_ref[device].astype(jnp.bfloat16)
        else:
            out_ref[device] = jnp.zeros((plan.height, LANES), jnp.bfloat16)


def build_maps(side, kernel_ref, lt_ref, by_lat_ref, turned_ref):
    span = 4 * side - 1
    wide = (span + 1) * side
    square = (lax.broadcasted_iota(jnp.int32, (span, span), 0)
              == lax.broadcasted_iota(jnp.int32, (span, span), 1))
    table = kernel_ref[...].astype(jnp.bfloat16)
    flipped = lax.dot_general(
        square.astype(jnp.float32).astype(jnp.bfloat16), table, (((1,), (1,)), ((), ())),
        preferred_element_type=jnp.float32,
    ).astype(jnp.bfloat16)
    block = lax.broadcasted_iota(jnp.int32, (span, wide), 1) // side
    pick = (lax.broadcasted_iota(jnp.int32, (span, wide), 0) == span - 1 - block)
    by_lat_ref[...] = jnp.dot(
        flipped, pick.astype(jnp.float32).astype(jnp.bfloat16), preferred_element_type=jnp.float32
    )
    lane = lax.broadcasted_iota(jnp.int32, (3 * side, wide), 1) % side
    base = jnp.zeros((3 * side, wide), jnp.float32)
    for x in range(side):
        base = jnp.where(lane == x, by_lat_ref[side - 1 - x : 4 * side - 1 - x, :], base)
    turns = LANES // side
    for turn in range(turns):
        moved = base if turn == 0 else pltpu.roll(base, wide - turn * side, 1)
        turned_ref[turn] = moved.astype(jnp.bfloat16)
    for k, (p, q) in enumerate(ALL_STEPS):
        for y in range(side):
            start = (2 * side - 1 - p * side - y) * side
            turn, first = (start % LANES) // side, start // LANES * LANES
            lt_ref[k, y * side : (y + 1) * side, :] = turned_ref[
                turn, (q + 1) * side : (q + 2) * side, first : first + side * side
            ]


def read_weights(plan, got_ref, wide_ref):
    extra = got_ref[:, plan.extra : plan.extra + 16, :].astype(jnp.float32)
    weights = extra[:, 12, :] + extra[:, 13, :] + extra[:, 14, :]
    for k in range(len(DIRECTIONS)):
        wide_ref[k] = jnp.broadcast_to(weights[:, k : k + 1], (plan.count, plan.columns))
    return extra


def forcing_of(extra, level):
    halves = []
    for half in range(2):
        row = 6 * half + 3 * level
        halves.append(extra[:, row, :] + extra[:, row + 1, :] + extra[:, row + 2, :])
    return jnp.concatenate(halves, axis=1)


def apply_rows(plan, low, got_ref, v_ref, lt_ref, wide_ref, w_ref, s_ref, p_ref):
    bands, lons, rows, columns = plan.bands, plan.lons, plan.rows, plan.columns
    grains = rows // GRAIN
    stride = lons + 2

    def weigh(band, carry):
        for l in range(lons):
            tile = band * lons + l
            v_low = v_ref[0, pl.ds(tile, 1), :]
            v_high = v_ref[1, pl.ds(tile, 1), :]
            halves = []
            for half in range(2):
                lanes = slice(half * LANES, (half + 1) * LANES)
                block = got_ref[tile, half * rows : (half + 1) * rows, :].astype(jnp.float32)
                pieces = []
                for g in range(grains):
                    v = jnp.where(g < low, v_low[:, lanes], v_high[:, lanes])
                    pieces.append(block[g * GRAIN : (g + 1) * GRAIN] * v)
                halves.append(jnp.concatenate(pieces, axis=0))
            weighted = jnp.concatenate(halves, axis=1).astype(jnp.bfloat16)
            places = [l + 1] + ([0] if l == lons - 1 else []) + ([lons + 1] if l == 0 else [])
            for place in places:
                at = pl.multiple_of((band * stride + place) * rows, 16)
                w_ref[pl.ds(at, rows), :] = weighted
        return carry

    lax.fori_loop(0, bands, weigh, 0)

    for k, (p, q) in enumerate(ALL_STEPS):

        def spread(band, carry, k=k, p=p, q=q):
            at = pl.multiple_of(((band + p) * stride + 1 + q) * rows, 16)
            y = jnp.dot(w_ref[pl.ds(at, lons * rows), :], lt_ref[k], preferred_element_type=jnp.float32)
            for l in range(lons):
                tile = band * lons + l
                piece = y[l * rows : (l + 1) * rows]
                if k == 0:
                    s_ref[tile] = piece * jnp.float32(1.0 / (plan.members - 1))
                else:
                    s_ref[tile] += piece * wide_ref[k - 1, pl.ds(tile, 1), :]
            return carry

        lax.fori_loop(max(0, -p), min(bands, bands - p), spread, 0)

    def gather(band, carry):
        sums = [[[], []], [[], []]]
        for l in range(lons):
            tile = band * lons + l
            for half in range(2):
                lanes = slice(half * LANES, (half + 1) * LANES)
                block = got_ref[tile, half * rows : (half + 1) * rows, :].astype(jnp.float32)
                product = block * s_ref[tile, :, lanes]
                lo = jnp.zeros((GRAIN, LANES), jnp.float32)
                hi = jnp.zeros((GRAIN, LANES), jnp.float32)
                for g in range(grains):
                    piece = product[g * GRAIN : (g + 1) * GRAIN]
                    share = jnp.where(g < low, jnp.float32(1), jnp.float32(0))
                    lo = lo + piece * share
                    hi = hi + piece * (1 - share)
                sums[0][half].append(jnp.sum(lo, axis=0, keepdims=True))
                sums[1][half].append(jnp.sum(hi, axis=0, keepdims=True))
        for level in range(2):
            p_ref[level, band] = jnp.concatenate(
                [jnp.concatenate(sums[level][half], axis=0) for half in range(2)], axis=1
            )
        return carry

    lax.fori_loop(0, bands, gather, 0)


def first_kernel(plan, side, info_ref, got_ref, kernel_ref, p_ref, lt_ref,
                 by_lat_ref, turned_ref, v_ref, wide_ref, w_ref, s_ref):
    build_maps(side, kernel_ref, lt_ref, by_lat_ref, turned_ref)
    extra = read_weights(plan, got_ref, wide_ref)
    v_ref[0] = forcing_of(extra, 0)
    v_ref[1] = forcing_of(extra, 1)
    apply_rows(plan, info_ref[0], got_ref, v_ref, lt_ref, wide_ref, w_ref, s_ref, p_ref)


def total(x):
    return jnp.sum(jnp.sum(x, axis=1, keepdims=True), axis=0, keepdims=True)


def second_kernel(plan, info_ref, got_ref, lt_ref, sum_ref, before_ref, after_ref, out_ref,
                  v_ref, wide_ref, w_ref, s_ref, p_ref):
    extra = read_weights(plan, got_ref, wide_ref)
    images = (sum_ref[0] + before_ref[...], sum_ref[1] + after_ref[...])
    lane = lax.broadcasted_iota(jnp.int32, (1, LANES), 1)
    first = jnp.zeros((1, LANES), jnp.float32)
    for level in range(2):
        b = forcing_of(extra, level)
        u = images[level]
        bb, bu = total(b * b), total(b * u)
        ratio = jnp.where(bb > 0, bu / jnp.where(bb > 0, bb, 1.0), 0.0)
        rest = ratio * b - u
        v_ref[level] = rest
        values = (bb, total(b * rest), total(rest * rest), ratio)
        speaks = jnp.where(info_ref[2 + level] > 0, jnp.float32(1), jnp.float32(0))
        for n, value in enumerate(values):
            at = lane == info_ref[4] + level + SLOT * n
            first = first + jnp.where(at, value, 0.0) * speaks
    apply_rows(plan, info_ref[0], got_ref, v_ref, lt_ref, wide_ref, w_ref, s_ref, p_ref)
    second = jnp.zeros((1, LANES), jnp.float32)
    for level in range(2):
        b = forcing_of(extra, level)
        t = p_ref[level].reshape(plan.count, plan.columns)
        for n, value in enumerate((total(v_ref[level] * t), total(b * t))):
            at = lane == info_ref[4] + level + SLOT * n
            second = second + jnp.where(at, value, 0.0)
    mine = jnp.where(info_ref[1] == 0, images[0], images[1])
    for half in range(2):
        lanes = slice(half * LANES, (half + 1) * LANES)
        out_ref[:, half, :] = mine[:, lanes]
        for level in range(2):
            share = p_ref[level, :, :, lanes].reshape(plan.count, LANES)
            out_ref[:, 2 + 2 * level + half, :] = share
    out_ref[:, 6, :] = jnp.broadcast_to(first, (plan.count, LANES))
    out_ref[:, 7, :] = jnp.broadcast_to(second, (plan.count, LANES))


def last_kernel(plan, f_ref, got_ref, inc_ref, res_ref, u_ref, t_ref):
    depth = plan.depth
    for level in range(plan.levels):
        group, j = divmod(level, depth + 1)
        speaker = plan.device(group, j, 0) if j < depth else plan.device(group, depth - 1, 1)
        for half in range(2):
            lanes = slice(half * LANES, (half + 1) * LANES)
            u_ref[level : level + 1, lanes] = got_ref[speaker, half : half + 1, :]
            t = None
            for core in range(2):
                for part in (0, 1):
                    k = j - part
                    if 0 <= k < depth:
                        row = 2 + 2 * part + half
                        term = got_ref[plan.device(group, k, core), row : row + 1, :]
                        t = term if t is None else t + term
            t_ref[level : level + 1, lanes] = t
    firsts = jnp.zeros((1, LANES), jnp.float32)
    seconds = jnp.zeros((1, LANES), jnp.float32)
    for device, _, _, _ in plan.owners():
        firsts = firsts + got_ref[device, 6:7, :]
        seconds = seconds + got_ref[device, 7:8, :]
    lane = lax.broadcasted_iota(jnp.int32, (1, LANES), 1)
    kept = lane < plan.levels

    def slot(row, n):
        moved = row if n == 0 else pltpu.roll(row, LANES - SLOT * n, 1)
        return jnp.where(kept, moved, 0.0)

    bb, bq, qq, ratio = (slot(firsts, n) for n in range(4))
    qt, bt = (slot(seconds, n) for n in range(2))

    def add(x):
        return jnp.sum(x, axis=1, keepdims=True)

    all_bb = add(bb)
    all_bu = add(ratio * bb - bq)
    whole = all_bu / all_bb
    shift = jnp.where(kept, whole - ratio, 0.0)
    q_q = add(shift * shift * bb + 2 * shift * bq + qq)
    q_bq = add(shift * shift * ratio * bb - shift * shift * bq + shift * bt
               + shift * ratio * bq - shift * qq + qt)
    b_bq = add(shift * ratio * bb - shift * bq + bt)
    q_u = add(shift * ratio * bb - shift * bq + ratio * bq - qq)
    energy = all_bb + all_bu
    step_0 = all_bb / energy
    norm_1 = step_0 * step_0 * q_q
    turn = norm_1 / all_bb
    curve = (step_0 * step_0 * (q_q + q_bq) + turn * step_0 * (q_u + b_bq) + turn * turn * energy)
    step_1 = norm_1 / curve

    rows = lax.broadcasted_iota(jnp.int32, (plan.levels, LANES), 0)
    diagonal = rows == lax.broadcasted_iota(jnp.int32, (plan.levels, LANES), 1)
    ratio_c = add(jnp.where(diagonal, ratio, 0.0))
    shift_c = add(jnp.where(diagonal, shift, 0.0))
    b, u, t = f_ref[...], u_ref[...], t_ref[...]
    q = shift_c * b + (ratio_c * b - u)
    b_of_q = shift_c * u + t
    direction = step_0 * q + turn * b
    inc_ref[...] = step_0 * b + step_1 * direction
    res_ref[...] = step_0 * q - step_1 * (step_0 * (q + b_of_q) + turn * (b + u))


def vmem():
    return pl.BlockSpec(memory_space=pltpu.VMEM)


def smem():
    return pl.BlockSpec(memory_space=pltpu.SMEM)


def by_levels(plan, anomalies, forcing, pair_code, kernel, tile_taper):
    axes = ("band", "tile")
    bf16, f32 = jnp.bfloat16, jnp.float32
    n, rows, columns = plan.count, plan.rows, plan.columns
    side = (kernel.shape[0] + 1) // 4
    wide = 4 * side * side
    a, f = anomalies[0, 0], forcing[0, 0]
    sent = pl.pallas_call(
        functools.partial(pack_kernel, plan, tile_taper.shape[0]),
        out_shape=jax.ShapeDtypeStruct((n, plan.height, LANES), bf16),
        in_specs=[smem(), smem(), vmem(), vmem()],
        out_specs=vmem(),
        scratch_shapes=[pltpu.VMEM((n, 16, LANES), f32)],
        name="pack",
    )(pair_code, tile_taper, a, f)
    got = lax.all_to_all(sent, axes, 0, 0)
    me = lax.axis_index(axes)
    info = lax.dynamic_slice(jnp.asarray(plan.table()), (me, 0), (1, 8))[0]
    work = [
        pltpu.VMEM((2, n, columns), f32),
        pltpu.VMEM((len(DIRECTIONS), n, columns), f32),
        pltpu.VMEM((plan.bands * (plan.lons + 2) * rows, columns), bf16),
        pltpu.VMEM((n, rows, columns), f32),
    ]
    part, maps = pl.pallas_call(
        functools.partial(first_kernel, plan, side),
        out_shape=(jax.ShapeDtypeStruct((2, plan.bands, plan.lons, columns), f32),
                   jax.ShapeDtypeStruct((len(ALL_STEPS), columns, columns), bf16)),
        in_specs=[smem(), vmem(), vmem()],
        out_specs=(vmem(), vmem()),
        scratch_shapes=[pltpu.VMEM((4 * side - 1, wide), f32),
                        pltpu.VMEM((LANES // side, 3 * side, wide), bf16)] + work,
        name="first",
    )(info, got, kernel)
    part = part.reshape(2, n, columns)
    swap = [(i, i ^ 1) for i in range(plan.lons)]
    both = part + lax.ppermute(part, "tile", swap)
    onward = plan.onward()
    before = lax.ppermute(both[1], axes, onward)
    after = lax.ppermute(both[0], axes, [(t, s) for s, t in onward])
    back = pl.pallas_call(
        functools.partial(second_kernel, plan),
        out_shape=jax.ShapeDtypeStruct((n, 8, LANES), f32),
        in_specs=[smem()] + [vmem()] * 5,
        out_specs=vmem(),
        scratch_shapes=work + [pltpu.VMEM((2, plan.bands, plan.lons, columns), f32)],
        name="second",
    )(info, got, maps, both, before, after)
    home = lax.all_to_all(back, axes, 0, 0)
    increment, residual = pl.pallas_call(
        functools.partial(last_kernel, plan),
        out_shape=(jax.ShapeDtypeStruct(f.shape, f32),) * 2,
        in_specs=[vmem(), vmem()],
        out_specs=(vmem(), vmem()),
        scratch_shapes=[pltpu.VMEM(f.shape, f32)] * 2,
        name="last",
    )(f, home)
    return increment[None, None], residual[None, None]


def padded(block, sides, width):
    for axis, dim in sides:
        count = lax.axis_size(axis)
        forward = [(i, i + 1) for i in range(count - 1)]
        forward.append((count - 1, 0))
        backward = [(target, source) for source, target in forward]
        low = lax.ppermute(
            lax.slice_in_dim(block, block.shape[dim] - width, None, axis=dim), axis, forward
        )
        high = lax.ppermute(lax.slice_in_dim(block, 0, width, axis=dim), axis, backward)
        block = jnp.concatenate([low, block, high], axis=dim)
    return block


def selector(tile_side, offset):
    first_index = np.arange(tile_side)[:, None]
    second_index = np.arange(tile_side)[None, :]
    target = 2 * tile_side - 1 + offset * tile_side + second_index - first_index
    return (np.arange(4 * tile_side - 1)[None, None, :] == target[:, :, None]).astype(np.float32)


def local_map(kernel, row_step, col_step):
    by_lat = jnp.einsum(
        "abp,pq->abq", selector(SIDE, row_step), kernel, precision=lax.Precision.HIGHEST
    )
    full_map = jnp.einsum(
        "abq,cdq->acbd", by_lat, selector(SIDE, col_step), precision=lax.Precision.HIGHEST
    )
    return full_map.reshape(SIDE * SIDE, SIDE * SIDE).astype(jnp.bfloat16)


def all_maps(kernel):
    return [local_map(kernel, 0, 0)] + [
        local_map(kernel, row_step, col_step) for row_step, col_step in DIRECTIONS
    ]


def taper_lookup(tile_taper, code):
    entries = jnp.arange(1, tile_taper.shape[0] + 1, dtype=jnp.int32)
    return jnp.sum(jnp.where(entries == code, tile_taper, jnp.zeros_like(tile_taper)))


def weighted_block(block, field):
    return (block.astype(jnp.float32) * field[:, None, :]).astype(jnp.bfloat16)


def pair_term(own_block, weighted, matrix, weight):
    levels, members, columns = weighted.shape
    spread = lax.dot_general(
        weighted.reshape(levels * members, columns),
        matrix,
        (((1,), (1,)), ((), ())),
        preferred_element_type=jnp.float32,
    )
    summed = jnp.sum(
        own_block.astype(jnp.float32) * spread.reshape(levels, members, columns), axis=1
    )
    return summed * (weight / (members - 1))


def masked_term(code, weight, own_block, weighted, matrix):

    def active():
        return pair_term(own_block, weighted, matrix, weight)

    def inactive():
        return jnp.zeros((weighted.shape[0], weighted.shape[2]), jnp.float32)

    return lax.cond(code > 0, active, inactive)


def covariance_all(blocks, neighbours, pair_codes, tile_taper, local_maps):
    own_block = blocks[1, 1]
    summed_terms = pair_term(
        own_block, weighted_block(own_block, neighbours[1, 1]), local_maps[0], 1.0
    )
    for position, (row_step, col_step) in enumerate(DIRECTIONS):
        code = pair_codes[position]
        weight = taper_lookup(tile_taper, code)
        other_weighted = weighted_block(
            blocks[1 + row_step, 1 + col_step], neighbours[1 + row_step, 1 + col_step]
        )
        summed_terms = summed_terms + masked_term(
            code, weight, own_block, other_weighted, local_maps[position + 1]
        )
    return summed_terms


def global_total(factor_one, factor_two):
    return lax.psum(jnp.sum(factor_one * factor_two), ("band", "tile"))


def on_device(anomalies, forcing, pair_code, kernel, tile_taper):
    pair_codes = pair_code[0, 0]
    kept_maps = all_maps(kernel)
    residual = forcing[0, 0]
    increment = jnp.zeros_like(residual)
    direction = residual
    norm_now = global_total(residual, residual)
    for iteration in range(ITERS):
        blocks = padded(anomalies, (("band", 0), ("tile", 1)), 1)
        neighbours = padded(direction[None, None], (("band", 0), ("tile", 1)), 1)
        mapped = direction + covariance_all(blocks, neighbours, pair_codes, tile_taper, kept_maps)
        step_length = norm_now / global_total(direction, mapped)
        increment = increment + step_length * direction
        residual = residual - step_length * mapped
        norm_next = global_total(residual, residual)
        direction = residual + norm_next / norm_now * direction
        norm_now = norm_next
    return (increment[None, None], residual[None, None])


def solution(mesh):
    specs = (
        P("band", "tile", None, None, None),
        P("band", "tile", None, None),
        P("band", "tile", None),
        P(),
        P(),
    )

    def run(anomalies, forcing, pair_code, kernel, tile_taper):
        plan = Plan(mesh.shape["band"], mesh.shape["tile"], *anomalies.shape[2:])
        step = functools.partial(by_levels, plan) if plan.fits else on_device
        return step(anomalies, forcing, pair_code, kernel, tile_taper)

    return jax.shard_map(
        run,
        mesh=mesh,
        in_specs=specs,
        out_specs=(P("band", "tile", None, None), P("band", "tile", None, None)),
        check_vma=False,
    )
```

```python
import functools

import jax
import jax.numpy as jnp
import numpy as np
from jax import lax
from jax.experimental import pallas as pl
from jax.experimental.pallas import tpu as pltpu
from jax.sharding import PartitionSpec as P

SIDE = 16
ITERS = 2
GRAIN = 8
LANES = 128
SLOT = 32

DIRECTIONS = ((-1, -1), (-1, 0), (-1, 1), (0, -1), (0, 1), (1, -1), (1, 0), (1, 1))
ALL_STEPS = ((0, 0),) + DIRECTIONS


class Plan:
    def __init__(self, bands, lons, levels, members, columns):
        self.bands, self.lons = bands, lons
        self.levels, self.members, self.columns = levels, members, columns
        self.count = bands * lons
        self.depth = members // (2 * GRAIN)
        self.rows = GRAIN * (self.depth + 1)
        self.fits = (
            members % (2 * GRAIN) == 0
            and levels % (self.depth + 1) == 0
            and levels <= SLOT
            and lons % GRAIN == 0
            and columns == 2 * LANES
            and self.rows % 16 == 0
        )
        if not self.fits:
            return
        self.groups = levels // (self.depth + 1)
        chips = self.count // 2
        used = self.groups * self.depth
        self.fits = used <= chips < 2 * used
        if not self.fits:
            return
        across = lons // 2
        inner = [i ^ (i >> 1) for i in range(across)]
        if sorted(inner) != list(range(across)):
            inner = list(range(across))
        path = []
        for band in range(bands):
            path += [band * across + c for c in (inner if band % 2 == 0 else inner[::-1])]
        self.path = path
        self.extra = 2 * self.rows
        self.height = self.extra + 16

    def device(self, group, k, core):
        return 2 * self.path[group * self.depth + k] + core

    def owners(self):
        for group in range(self.groups):
            for k in range(self.depth):
                for core in range(2):
                    low = group * (self.depth + 1) + k
                    yield self.device(group, k, core), k, core, low

    def table(self):
        out = np.zeros((self.count, 8), np.int32)
        for device, k, core, low in self.owners():
            last = k == self.depth - 1
            out[device, :5] = (self.depth - k, core, int(core == 0), int(core == 1 and last), low)
        return out

    def onward(self):
        pairs = []
        for group in range(self.groups):
            for k in range(self.depth - 1):
                for core in range(2):
                    pairs.append((self.device(group, k, core), self.device(group, k + 1, core)))
        return pairs


def in_three(x):
    high = x.astype(jnp.bfloat16).astype(jnp.float32)
    rest = x - high
    middle = rest.astype(jnp.bfloat16).astype(jnp.float32)
    return high, middle, rest - middle


def pack_kernel(plan, tapers, code_ref, taper_ref, a_ref, f_ref, out_ref, ext_ref):
    parts = in_three(f_ref[:, 0, :])
    lane = lax.broadcasted_iota(jnp.int32, (1, LANES), 1)
    weights = jnp.zeros((1, LANES), jnp.float32)
    for k in range(len(DIRECTIONS)):
        code = code_ref[0, 0, k]
        weight = jnp.float32(0)
        for c in range(tapers):
            weight = jnp.where(code == c + 1, taper_ref[c], weight)
        weights = jnp.where(lane == k, weight, weights)
    weights = in_three(weights / jnp.float32(plan.members - 1))
    blank = jnp.zeros((1, LANES), jnp.float32)
    rows, depth = plan.rows, plan.depth
    taken = set()
    for device, k, core, low in plan.owners():
        taken.add(device)
        count = GRAIN * (depth - k)
        start = 2 * k * GRAIN + core * count
        other = GRAIN * (k + 1)
        for half in range(2):
            lanes = slice(half * LANES, (half + 1) * LANES)
            base = half * rows
            out_ref[device, base : base + count, :] = a_ref[low, start : start + count, lanes]
            out_ref[device, base + count : base + rows, :] = a_ref[
                low + 1, core * other : (core + 1) * other, lanes
            ]
            for level in range(2):
                for n, part in enumerate(parts):
                    row = 6 * half + 3 * level + n
                    ext_ref[device, row : row + 1, :] = part[low + level : low + level + 1, lanes]
        for n, part in enumerate(weights):
            ext_ref[device, 12 + n : 13 + n, :] = part
        ext_ref[device, 15:16, :] = blank
    for device in range(plan.count):
        if device in taken:
            out_ref[device, plan.extra : plan.extra + 16, :] = ext_ref[device].astype(jnp.bfloat16)
        else:
            out_ref[device] = jnp.zeros((plan.height, LANES), jnp.bfloat16)


def build_maps(side, kernel_ref, lt_ref, by_lat_ref, turned_ref):
    span = 4 * side - 1
    wide = (span + 1) * side
    square = (lax.broadcasted_iota(jnp.int32, (span, span), 0)
              == lax.broadcasted_iota(jnp.int32, (span, span), 1))
    table = kernel_ref[...].astype(jnp.bfloat16)
    flipped = lax.dot_general(
        square.astype(jnp.float32).astype(jnp.bfloat16), table, (((1,), (1,)), ((), ())),
        preferred_element_type=jnp.float32,
    ).astype(jnp.bfloat16)
    block = lax.broadcasted_iota(jnp.int32, (span, wide), 1) // side
    pick = (lax.broadcasted_iota(jnp.int32, (span, wide), 0) == span - 1 - block)
    by_lat_ref[...] = jnp.dot(
        flipped, pick.astype(jnp.float32).astype(jnp.bfloat16), preferred_element_type=jnp.float32
    )
    lane = lax.broadcasted_iota(jnp.int32, (3 * side, wide), 1) % side
    base = jnp.zeros((3 * side, wide), jnp.float32)
    for x in range(side):
        base = jnp.where(lane == x, by_lat_ref[side - 1 - x : 4 * side - 1 - x, :], base)
    turns = LANES // side
    for turn in range(turns):
        moved = base if turn == 0 else pltpu.roll(base, wide - turn * side, 1)
        turned_ref[turn] = moved.astype(jnp.bfloat16)
    for k, (p, q) in enumerate(ALL_STEPS):
        for y in range(side):
            start = (2 * side - 1 - p * side - y) * side
            turn, first = (start % LANES) // side, start // LANES * LANES
            lt_ref[k, y * side : (y + 1) * side, :] = turned_ref[
                turn, (q + 1) * side : (q + 2) * side, first : first + side * side
            ]


def read_weights(plan, got_ref, wide_ref):
    extra = got_ref[:, plan.extra : plan.extra + 16, :].astype(jnp.float32)
    weights = extra[:, 12, :] + extra[:, 13, :] + extra[:, 14, :]
    for k in range(len(DIRECTIONS)):
        wide_ref[k] = jnp.broadcast_to(weights[:, k : k + 1], (plan.count, plan.columns))
    return extra


def forcing_of(extra, level):
    halves = []
    for half in range(2):
        row = 6 * half + 3 * level
        halves.append(extra[:, row, :] + extra[:, row + 1, :] + extra[:, row + 2, :])
    return jnp.concatenate(halves, axis=1)


def apply_rows(plan, low, got_ref, v_ref, lt_ref, wide_ref, w_ref, s_ref, p_ref):
    bands, lons, rows = plan.bands, plan.lons, plan.rows
    grains = rows // GRAIN
    sides = [slice(half * LANES, (half + 1) * LANES) for half in range(2)]

    def block(tile, half):
        return got_ref[tile, half * rows : (half + 1) * rows, :].astype(jnp.float32)

    for tile in range(plan.count):
        v_low, v_high = v_ref[0, tile : tile + 1, :], v_ref[1, tile : tile + 1, :]
        for half, lanes in enumerate(sides):
            values = block(tile, half)
            pieces = []
            for g in range(grains):
                v = jnp.where(g < low, v_low[:, lanes], v_high[:, lanes])
                pieces.append(values[g * GRAIN : (g + 1) * GRAIN] * v)
            w_ref[tile * rows : (tile + 1) * rows, lanes] = jnp.concatenate(pieces, axis=0).astype(jnp.bfloat16)

    for k, (p, q) in enumerate(ALL_STEPS):
        first, last = max(0, p), min(bands, bands + p)
        y = jnp.dot(
            w_ref[first * lons * rows : last * lons * rows, :], lt_ref[k], preferred_element_type=jnp.float32
        )
        for band in range(first, last):
            for l in range(lons):
                tile = (band - p) * lons + (l - q) % lons
                at = ((band - first) * lons + l) * rows
                piece = y[at : at + rows]
                if k == 0:
                    s_ref[tile] = piece * jnp.float32(1.0 / (plan.members - 1))
                else:
                    s_ref[tile] += piece * wide_ref[k - 1, tile : tile + 1, :]

    shares = [jnp.where(g < low, jnp.float32(1), jnp.float32(0)) for g in range(grains)]
    for band in range(bands):
        for half, lanes in enumerate(sides):
            sums = [[], []]
            for l in range(lons):
                tile = band * lons + l
                product = block(tile, half) * s_ref[tile, :, lanes]
                lo = jnp.zeros((GRAIN, LANES), jnp.float32)
                hi = jnp.zeros((GRAIN, LANES), jnp.float32)
                for g in range(grains):
                    piece = product[g * GRAIN : (g + 1) * GRAIN]
                    lo = lo + piece * shares[g]
                    hi = hi + piece * (1 - shares[g])
                sums[0].append(jnp.sum(lo, axis=0, keepdims=True))
                sums[1].append(jnp.sum(hi, axis=0, keepdims=True))
            for level in range(2):
                p_ref[level, band, :, lanes] = jnp.concatenate(sums[level], axis=0)


def first_kernel(plan, info_ref, got_ref, lt_ref, p_ref, v_ref, wide_ref, w_ref, s_ref):
    extra = read_weights(plan, got_ref, wide_ref)
    v_ref[0] = forcing_of(extra, 0)
    v_ref[1] = forcing_of(extra, 1)
    apply_rows(plan, info_ref[0], got_ref, v_ref, lt_ref, wide_ref, w_ref, s_ref, p_ref)


def total(x):
    return jnp.sum(jnp.sum(x, axis=1, keepdims=True), axis=0, keepdims=True)


def second_kernel(plan, info_ref, got_ref, lt_ref, sum_ref, before_ref, after_ref, out_ref,
                  v_ref, wide_ref, w_ref, s_ref, p_ref):
    extra = read_weights(plan, got_ref, wide_ref)
    images = (sum_ref[0] + before_ref[...], sum_ref[1] + after_ref[...])
    lane = lax.broadcasted_iota(jnp.int32, (1, LANES), 1)
    first = jnp.zeros((1, LANES), jnp.float32)
    for level in range(2):
        b = forcing_of(extra, level)
        u = images[level]
        bb, bu = total(b * b), total(b * u)
        ratio = jnp.where(bb > 0, bu / jnp.where(bb > 0, bb, 1.0), 0.0)
        rest = ratio * b - u
        v_ref[level] = rest
        values = (bb, total(b * rest), total(rest * rest), ratio)
        speaks = jnp.where(info_ref[2 + level] > 0, jnp.float32(1), jnp.float32(0))
        for n, value in enumerate(values):
            at = lane == info_ref[4] + level + SLOT * n
            first = first + jnp.where(at, value, 0.0) * speaks
    apply_rows(plan, info_ref[0], got_ref, v_ref, lt_ref, wide_ref, w_ref, s_ref, p_ref)
    second = jnp.zeros((1, LANES), jnp.float32)
    for level in range(2):
        b = forcing_of(extra, level)
        t = p_ref[level].reshape(plan.count, plan.columns)
        for n, value in enumerate((total(v_ref[level] * t), total(b * t))):
            at = lane == info_ref[4] + level + SLOT * n
            second = second + jnp.where(at, value, 0.0)
    mine = jnp.where(info_ref[1] == 0, images[0], images[1])
    for half in range(2):
        lanes = slice(half * LANES, (half + 1) * LANES)
        out_ref[:, half, :] = mine[:, lanes]
        for level in range(2):
            share = p_ref[level, :, :, lanes].reshape(plan.count, LANES)
            out_ref[:, 2 + 2 * level + half, :] = share
    out_ref[:, 6, :] = jnp.broadcast_to(first, (plan.count, LANES))
    out_ref[:, 7, :] = jnp.broadcast_to(second, (plan.count, LANES))


def last_kernel(plan, f_ref, got_ref, inc_ref, res_ref, u_ref, t_ref):
    depth = plan.depth
    for level in range(plan.levels):
        group, j = divmod(level, depth + 1)
        speaker = plan.device(group, j, 0) if j < depth else plan.device(group, depth - 1, 1)
        for half in range(2):
            lanes = slice(half * LANES, (half + 1) * LANES)
            u_ref[level : level + 1, lanes] = got_ref[speaker, half : half + 1, :]
            t = None
            for core in range(2):
                for part in (0, 1):
                    k = j - part
                    if 0 <= k < depth:
                        row = 2 + 2 * part + half
                        term = got_ref[plan.device(group, k, core), row : row + 1, :]
                        t = term if t is None else t + term
            t_ref[level : level + 1, lanes] = t
    firsts = jnp.zeros((1, LANES), jnp.float32)
    seconds = jnp.zeros((1, LANES), jnp.float32)
    for device, _, _, _ in plan.owners():
        firsts = firsts + got_ref[device, 6:7, :]
        seconds = seconds + got_ref[device, 7:8, :]
    lane = lax.broadcasted_iota(jnp.int32, (1, LANES), 1)
    kept = lane < plan.levels

    def slot(row, n):
        moved = row if n == 0 else pltpu.roll(row, LANES - SLOT * n, 1)
        return jnp.where(kept, moved, 0.0)

    bb, bq, qq, ratio = (slot(firsts, n) for n in range(4))
    qt, bt = (slot(seconds, n) for n in range(2))

    def add(x):
        return jnp.sum(x, axis=1, keepdims=True)

    all_bb = add(bb)
    all_bu = add(ratio * bb - bq)
    whole = all_bu / all_bb
    shift = jnp.where(kept, whole - ratio, 0.0)
    q_q = add(shift * shift * bb + 2 * shift * bq + qq)
    q_bq = add(shift * shift * ratio * bb - shift * shift * bq + shift * bt
               + shift * ratio * bq - shift * qq + qt)
    b_bq = add(shift * ratio * bb - shift * bq + bt)
    q_u = add(shift * ratio * bb - shift * bq + ratio * bq - qq)
    energy = all_bb + all_bu
    step_0 = all_bb / energy
    norm_1 = step_0 * step_0 * q_q
    turn = norm_1 / all_bb
    curve = (step_0 * step_0 * (q_q + q_bq) + turn * step_0 * (q_u + b_bq) + turn * turn * energy)
    step_1 = norm_1 / curve

    rows = lax.broadcasted_iota(jnp.int32, (plan.levels, LANES), 0)
    diagonal = rows == lax.broadcasted_iota(jnp.int32, (plan.levels, LANES), 1)
    ratio_c = add(jnp.where(diagonal, ratio, 0.0))
    shift_c = add(jnp.where(diagonal, shift, 0.0))
    b, u, t = f_ref[:, 0, :], u_ref[...], t_ref[...]
    q = shift_c * b + (ratio_c * b - u)
    b_of_q = shift_c * u + t
    direction = step_0 * q + turn * b
    inc_ref[:, 0, :] = step_0 * b + step_1 * direction
    res_ref[:, 0, :] = step_0 * q - step_1 * (step_0 * (q + b_of_q) + turn * (b + u))


def room(mib):
    return pltpu.CompilerParams(vmem_limit_bytes=mib << 20)


def vmem():
    return pl.BlockSpec(memory_space=pltpu.VMEM)


def smem():
    return pl.BlockSpec(memory_space=pltpu.SMEM)


def by_levels(plan, anomalies, forcing, pair_code, kernel, tile_taper):
    axes = ("band", "tile")
    bf16, f32 = jnp.bfloat16, jnp.float32
    n, rows, columns = plan.count, plan.rows, plan.columns
    side = (kernel.shape[0] + 1) // 4
    wide = 4 * side * side
    a, f = anomalies[0, 0], jnp.swapaxes(forcing[0], 0, 1)
    sent = pl.pallas_call(
        functools.partial(pack_kernel, plan, tile_taper.shape[0]),
        out_shape=jax.ShapeDtypeStruct((n, plan.height, LANES), bf16),
        in_specs=[smem(), smem(), vmem(), vmem()],
        out_specs=vmem(),
        scratch_shapes=[pltpu.VMEM((n, 16, LANES), f32)],
        name="pack",
    )(pair_code, tile_taper, a, f)
    got = lax.all_to_all(sent, axes, 0, 0)
    me = lax.axis_index(axes)
    info = lax.dynamic_slice(jnp.asarray(plan.table()), (me, 0), (1, 8))[0]
    work = [
        pltpu.VMEM((2, n, columns), f32),
        pltpu.VMEM((len(DIRECTIONS), n, columns), f32),
        pltpu.VMEM((n * rows, columns), bf16),
        pltpu.VMEM((n, rows, columns), f32),
    ]
    maps = pl.pallas_call(
        functools.partial(build_maps, side),
        out_shape=jax.ShapeDtypeStruct((len(ALL_STEPS), columns, columns), bf16),
        in_specs=[vmem()],
        out_specs=vmem(),
        scratch_shapes=[pltpu.VMEM((4 * side - 1, wide), f32),
                        pltpu.VMEM((LANES // side, 3 * side, wide), bf16)],
        cost_estimate=pl.CostEstimate(flops=200_000_000, bytes_accessed=2_000_000, transcendentals=0),
        compiler_params=room(12),
        name="maps",
    )(kernel)
    part = pl.pallas_call(
        functools.partial(first_kernel, plan),
        out_shape=jax.ShapeDtypeStruct((2, plan.bands, plan.lons, columns), f32),
        in_specs=[smem(), vmem(), vmem()],
        out_specs=vmem(),
        scratch_shapes=work,
        compiler_params=room(20),
        name="first",
    )(info, got, maps)
    part = part.reshape(2, n, columns)
    swap = [(i, i ^ 1) for i in range(plan.lons)]
    both = part + lax.ppermute(part, "tile", swap)
    onward = plan.onward()
    before = lax.ppermute(both[1], axes, onward)
    after = lax.ppermute(both[0], axes, [(t, s) for s, t in onward])
    back = pl.pallas_call(
        functools.partial(second_kernel, plan),
        out_shape=jax.ShapeDtypeStruct((n, 8, LANES), f32),
        in_specs=[smem()] + [vmem()] * 5,
        out_specs=vmem(),
        scratch_shapes=work + [pltpu.VMEM((2, plan.bands, plan.lons, columns), f32)],
        compiler_params=room(20),
        name="second",
    )(info, got, maps, both, before, after)
    home = lax.all_to_all(back, axes, 0, 0)
    increment, residual = pl.pallas_call(
        functools.partial(last_kernel, plan),
        out_shape=(jax.ShapeDtypeStruct(f.shape, f32),) * 2,
        in_specs=[vmem(), vmem()],
        out_specs=(vmem(), vmem()),
        scratch_shapes=[pltpu.VMEM((plan.levels, columns), f32)] * 2,
        compiler_params=room(8),
        name="last",
    )(f, home)
    return jnp.swapaxes(increment, 0, 1)[None], jnp.swapaxes(residual, 0, 1)[None]


def padded(block, sides, width):
    for axis, dim in sides:
        count = lax.axis_size(axis)
        forward = [(i, i + 1) for i in range(count - 1)]
        forward.append((count - 1, 0))
        backward = [(target, source) for source, target in forward]
        low = lax.ppermute(
            lax.slice_in_dim(block, block.shape[dim] - width, None, axis=dim), axis, forward
        )
        high = lax.ppermute(lax.slice_in_dim(block, 0, width, axis=dim), axis, backward)
        block = jnp.concatenate([low, block, high], axis=dim)
    return block


def selector(tile_side, offset):
    first_index = np.arange(tile_side)[:, None]
    second_index = np.arange(tile_side)[None, :]
    target = 2 * tile_side - 1 + offset * tile_side + second_index - first_index
    return (np.arange(4 * tile_side - 1)[None, None, :] == target[:, :, None]).astype(np.float32)


def local_map(kernel, row_step, col_step):
    by_lat = jnp.einsum(
        "abp,pq->abq", selector(SIDE, row_step), kernel, precision=lax.Precision.HIGHEST
    )
    full_map = jnp.einsum(
        "abq,cdq->acbd", by_lat, selector(SIDE, col_step), precision=lax.Precision.HIGHEST
    )
    return full_map.reshape(SIDE * SIDE, SIDE * SIDE).astype(jnp.bfloat16)


def all_maps(kernel):
    return [local_map(kernel, 0, 0)] + [
        local_map(kernel, row_step, col_step) for row_step, col_step in DIRECTIONS
    ]


def taper_lookup(tile_taper, code):
    entries = jnp.arange(1, tile_taper.shape[0] + 1, dtype=jnp.int32)
    return jnp.sum(jnp.where(entries == code, tile_taper, jnp.zeros_like(tile_taper)))


def weighted_block(block, field):
    return (block.astype(jnp.float32) * field[:, None, :]).astype(jnp.bfloat16)


def pair_term(own_block, weighted, matrix, weight):
    levels, members, columns = weighted.shape
    spread = lax.dot_general(
        weighted.reshape(levels * members, columns),
        matrix,
        (((1,), (1,)), ((), ())),
        preferred_element_type=jnp.float32,
    )
    summed = jnp.sum(
        own_block.astype(jnp.float32) * spread.reshape(levels, members, columns), axis=1
    )
    return summed * (weight / (members - 1))


def masked_term(code, weight, own_block, weighted, matrix):

    def active():
        return pair_term(own_block, weighted, matrix, weight)

    def inactive():
        return jnp.zeros((weighted.shape[0], weighted.shape[2]), jnp.float32)

    return lax.cond(code > 0, active, inactive)


def covariance_all(blocks, neighbours, pair_codes, tile_taper, local_maps):
    own_block = blocks[1, 1]
    summed_terms = pair_term(
        own_block, weighted_block(own_block, neighbours[1, 1]), local_maps[0], 1.0
    )
    for position, (row_step, col_step) in enumerate(DIRECTIONS):
        code = pair_codes[position]
        weight = taper_lookup(tile_taper, code)
        other_weighted = weighted_block(
            blocks[1 + row_step, 1 + col_step], neighbours[1 + row_step, 1 + col_step]
        )
        summed_terms = summed_terms + masked_term(
            code, weight, own_block, other_weighted, local_maps[position + 1]
        )
    return summed_terms


def global_total(factor_one, factor_two):
    return lax.psum(jnp.sum(factor_one * factor_two), ("band", "tile"))


def on_device(anomalies, forcing, pair_code, kernel, tile_taper):
    pair_codes = pair_code[0, 0]
    kept_maps = all_maps(kernel)
    residual = forcing[0, 0]
    increment = jnp.zeros_like(residual)
    direction = residual
    norm_now = global_total(residual, residual)
    for iteration in range(ITERS):
        blocks = padded(anomalies, (("band", 0), ("tile", 1)), 1)
        neighbours = padded(direction[None, None], (("band", 0), ("tile", 1)), 1)
        mapped = direction + covariance_all(blocks, neighbours, pair_codes, tile_taper, kept_maps)
        step_length = norm_now / global_total(direction, mapped)
        increment = increment + step_length * direction
        residual = residual - step_length * mapped
        norm_next = global_total(residual, residual)
        direction = residual + norm_next / norm_now * direction
        norm_now = norm_next
    return (increment[None, None], residual[None, None])


def solution(mesh):
    specs = (
        P("band", "tile", None, None, None),
        P("band", "tile", None, None),
        P("band", "tile", None),
        P(),
        P(),
    )

    def run(anomalies, forcing, pair_code, kernel, tile_taper):
        plan = Plan(mesh.shape["band"], mesh.shape["tile"], *anomalies.shape[2:])
        step = functools.partial(by_levels, plan) if plan.fits else on_device
        return step(anomalies, forcing, pair_code, kernel, tile_taper)

    return jax.shard_map(
        run,
        mesh=mesh,
        in_specs=specs,
        out_specs=(P("band", "tile", None, None), P("band", "tile", None, None)),
        check_vma=False,
    )
```

```python
import functools

import jax
import jax.numpy as jnp
import numpy as np
from jax import lax
from jax.experimental import pallas as pl
from jax.experimental.pallas import tpu as pltpu
from jax.sharding import PartitionSpec as P

SIDE = 16
ITERS = 2
GRAIN = 8
LANES = 128
SLOT = 32

DIRECTIONS = ((-1, -1), (-1, 0), (-1, 1), (0, -1), (0, 1), (1, -1), (1, 0), (1, 1))
ALL_STEPS = ((0, 0),) + DIRECTIONS


class Plan:
    def __init__(self, bands, lons, levels, members, columns):
        self.bands, self.lons = bands, lons
        self.levels, self.members, self.columns = levels, members, columns
        self.count = bands * lons
        self.rows = levels * members // self.count
        self.step = 2 * self.rows - members
        self.fits = (
            levels * members % self.count == 0
            and members % 2 == 0
            and 0 < self.step < members
            and members % self.step == 0
            and levels <= SLOT
            and lons % GRAIN == 0
            and columns == 2 * LANES
        )
        if not self.fits:
            return
        self.depth = members // self.step
        self.fits = levels % (self.depth + 1) == 0
        if not self.fits:
            return
        self.groups = levels // (self.depth + 1)
        across = lons // 2
        inner = [i ^ (i >> 1) for i in range(across)]
        if sorted(inner) != list(range(across)):
            inner = list(range(across))
        path = []
        for band in range(bands):
            path += [band * across + c for c in (inner if band % 2 == 0 else inner[::-1])]
        self.path = path
        self.block = -(-(self.rows + 3) // 16) * 16
        self.height = 2 * self.block + GRAIN

    def low_rows(self, k):
        return (self.members - k * self.step) // 2

    def device(self, group, k, core):
        return 2 * self.path[group * self.depth + k] + core

    def owners(self):
        for group in range(self.groups):
            for k in range(self.depth):
                for core in range(2):
                    low = group * (self.depth + 1) + k
                    yield self.device(group, k, core), k, core, low

    def table(self):
        out = np.zeros((self.count, 8), np.int32)
        for device, k, core, low in self.owners():
            last = k == self.depth - 1
            out[device, :5] = (self.low_rows(k), core, int(core == 0), int(core == 1 and last), low)
        return out

    def onward(self):
        pairs = []
        for group in range(self.groups):
            for k in range(self.depth - 1):
                for core in range(2):
                    pairs.append((self.device(group, k, core), self.device(group, k + 1, core)))
        return pairs


def in_three(x):
    high = x.astype(jnp.bfloat16).astype(jnp.float32)
    rest = x - high
    middle = rest.astype(jnp.bfloat16).astype(jnp.float32)
    return [high, middle, rest - middle]


def pack_kernel(plan, tapers, code_ref, taper_ref, a_ref, f_ref, out_ref, wide_ref):
    for level in range(plan.levels):
        wide_ref[level * plan.members : (level + 1) * plan.members, :] = a_ref[level].astype(jnp.float32)
    forcing = in_three(f_ref[:, 0, :])
    lane = lax.broadcasted_iota(jnp.int32, (1, LANES), 1)
    weights = jnp.zeros((1, LANES), jnp.float32)
    for k in range(len(DIRECTIONS)):
        code = code_ref[0, 0, k]
        weight = jnp.float32(0)
        for c in range(tapers):
            weight = jnp.where(code == c + 1, taper_ref[c], weight)
        weights = jnp.where(lane == k, weight, weights)
    weights = weights / jnp.float32(plan.members - 1)
    high, middle, _ = in_three(weights)
    for device, k, core, low in plan.owners():
        count, other = plan.low_rows(k), plan.rows - plan.low_rows(k)
        start = low * plan.members + k * plan.step + core * count
        after = (low + 1) * plan.members + core * other
        for half in range(2):
            lanes = slice(half * LANES, (half + 1) * LANES)
            pieces = [wide_ref[start : start + count, lanes], wide_ref[after : after + other, lanes]]
            pieces += [part[low : low + 1, lanes] for part in forcing]
            spare = plan.block - plan.rows - 3
            if spare:
                pieces.append(jnp.zeros((spare, LANES), jnp.float32))
            out_ref[device, half * plan.block : (half + 1) * plan.block, :] = jnp.concatenate(
                pieces, axis=0
            ).astype(jnp.bfloat16)
        pieces = [part[low + 1 : low + 2, :LANES] for part in forcing]
        pieces += [part[low + 1 : low + 2, LANES:] for part in forcing]
        out_ref[device, 2 * plan.block :, :] = jnp.concatenate(pieces + [high, middle], axis=0).astype(jnp.bfloat16)


def build_maps(side, kernel_ref, lt_ref, by_lat_ref, turned_ref):
    span = 4 * side - 1
    wide = (span + 1) * side
    square = (lax.broadcasted_iota(jnp.int32, (span, span), 0)
              == lax.broadcasted_iota(jnp.int32, (span, span), 1))
    table = kernel_ref[...].astype(jnp.bfloat16)
    flipped = lax.dot_general(
        square.astype(jnp.float32).astype(jnp.bfloat16), table, (((1,), (1,)), ((), ())),
        preferred_element_type=jnp.float32,
    ).astype(jnp.bfloat16)
    block = lax.broadcasted_iota(jnp.int32, (span, wide), 1) // side
    pick = (lax.broadcasted_iota(jnp.int32, (span, wide), 0) == span - 1 - block)
    by_lat_ref[...] = jnp.dot(
        flipped, pick.astype(jnp.float32).astype(jnp.bfloat16), preferred_element_type=jnp.float32
    )
    lane = lax.broadcasted_iota(jnp.int32, (3 * side, wide), 1) % side
    base = jnp.zeros((3 * side, wide), jnp.float32)
    for x in range(side):
        base = jnp.where(lane == x, by_lat_ref[side - 1 - x : 4 * side - 1 - x, :], base)
    turns = LANES // side
    for turn in range(turns):
        moved = base if turn == 0 else pltpu.roll(base, wide - turn * side, 1)
        turned_ref[turn] = moved.astype(jnp.bfloat16)
    for k, (p, q) in enumerate(ALL_STEPS):
        for y in range(side):
            start = (2 * side - 1 - p * side - y) * side
            turn, first = (start % LANES) // side, start // LANES * LANES
            lt_ref[k, y * side : (y + 1) * side, :] = turned_ref[
                turn, (q + 1) * side : (q + 2) * side, first : first + side * side
            ]


def read_extra(plan, got_ref, wide_ref):
    first = plan.rows // 16 * 16
    at = plan.rows - first
    tail = got_ref[:, 2 * plan.block :, :].astype(jnp.float32)
    weights = tail[:, 6, :] + tail[:, 7, :]
    for k in range(len(DIRECTIONS)):
        wide_ref[k] = jnp.broadcast_to(weights[:, k : k + 1], (plan.count, plan.columns))
    low, high = [], []
    for half in range(2):
        slab = got_ref[:, half * plan.block + first : (half + 1) * plan.block, :].astype(jnp.float32)
        low.append(slab[:, at, :] + slab[:, at + 1, :] + slab[:, at + 2, :])
        high.append(tail[:, 3 * half, :] + tail[:, 3 * half + 1, :] + tail[:, 3 * half + 2, :])
    return [jnp.concatenate(low, axis=1), jnp.concatenate(high, axis=1)]


def apply_rows(plan, low, got_ref, v_ref, lt_ref, wide_ref, w_ref, s_ref, p_ref):
    bands, lons, rows = plan.bands, plan.lons, plan.block
    place = lax.broadcasted_iota(jnp.int32, (rows, LANES), 0)
    is_low = place < low
    sides = [slice(half * LANES, (half + 1) * LANES) for half in range(2)]

    def block(tile, half):
        return got_ref[tile, half * rows : (half + 1) * rows, :].astype(jnp.float32)

    for tile in range(plan.count):
        v_low, v_high = v_ref[0, tile : tile + 1, :], v_ref[1, tile : tile + 1, :]
        for half, lanes in enumerate(sides):
            v = jnp.where(is_low, v_low[:, lanes], v_high[:, lanes])
            w_ref[tile * rows : (tile + 1) * rows, lanes] = (block(tile, half) * v).astype(jnp.bfloat16)

    for k, (p, q) in enumerate(ALL_STEPS):
        first, last = max(0, p), min(bands, bands + p)
        y = jnp.dot(
            w_ref[first * lons * rows : last * lons * rows, :], lt_ref[k], preferred_element_type=jnp.float32
        )
        for band in range(first, last):
            for l in range(lons):
                tile = (band - p) * lons + (l - q) % lons
                at = ((band - first) * lons + l) * rows
                piece = y[at : at + rows]
                if k == 0:
                    s_ref[tile] = piece * jnp.float32(1.0 / (plan.members - 1))
                else:
                    s_ref[tile] += piece * wide_ref[k - 1, tile : tile + 1, :]

    low_share = jnp.where(is_low, jnp.float32(1), jnp.float32(0))
    high_share = jnp.where(is_low | (place >= plan.rows), jnp.float32(0), jnp.float32(1))
    for band in range(bands):
        for half, lanes in enumerate(sides):
            sums = [[], []]
            for l in range(lons):
                tile = band * lons + l
                product = block(tile, half) * s_ref[tile, :, lanes]
                sums[0].append(jnp.sum(product * low_share, axis=0, keepdims=True))
                sums[1].append(jnp.sum(product * high_share, axis=0, keepdims=True))
            for level in range(2):
                p_ref[level, band, :, lanes] = jnp.concatenate(sums[level], axis=0)


def first_kernel(plan, info_ref, got_ref, lt_ref, p_ref, v_ref, wide_ref, w_ref, s_ref):
    v_ref[0], v_ref[1] = read_extra(plan, got_ref, wide_ref)
    apply_rows(plan, info_ref[0], got_ref, v_ref, lt_ref, wide_ref, w_ref, s_ref, p_ref)


def total(x):
    return jnp.sum(jnp.sum(x, axis=1, keepdims=True), axis=0, keepdims=True)


def second_kernel(plan, info_ref, got_ref, lt_ref, sum_ref, before_ref, after_ref, out_ref,
                  v_ref, wide_ref, w_ref, s_ref, p_ref):
    forcing = read_extra(plan, got_ref, wide_ref)
    images = (sum_ref[0] + before_ref[...], sum_ref[1] + after_ref[...])
    lane = lax.broadcasted_iota(jnp.int32, (1, LANES), 1)
    first = jnp.zeros((1, LANES), jnp.float32)
    for level in range(2):
        b = forcing[level]
        u = images[level]
        bb, bu = total(b * b), total(b * u)
        ratio = jnp.where(bb > 0, bu / jnp.where(bb > 0, bb, 1.0), 0.0)
        rest = ratio * b - u
        v_ref[level] = rest
        values = (bb, total(b * rest), total(rest * rest), ratio)
        speaks = jnp.where(info_ref[2 + level] > 0, jnp.float32(1), jnp.float32(0))
        for n, value in enumerate(values):
            at = lane == info_ref[4] + level + SLOT * n
            first = first + jnp.where(at, value, 0.0) * speaks
    apply_rows(plan, info_ref[0], got_ref, v_ref, lt_ref, wide_ref, w_ref, s_ref, p_ref)
    second = jnp.zeros((1, LANES), jnp.float32)
    for level in range(2):
        b = forcing[level]
        t = p_ref[level].reshape(plan.count, plan.columns)
        for n, value in enumerate((total(v_ref[level] * t), total(b * t))):
            at = lane == info_ref[4] + level + SLOT * n
            second = second + jnp.where(at, value, 0.0)
    mine = jnp.where(info_ref[1] == 0, images[0], images[1])
    for half in range(2):
        lanes = slice(half * LANES, (half + 1) * LANES)
        out_ref[:, half, :] = mine[:, lanes]
        for level in range(2):
            share = p_ref[level, :, :, lanes].reshape(plan.count, LANES)
            out_ref[:, 2 + 2 * level + half, :] = share
    out_ref[:, 6, :] = jnp.broadcast_to(first, (plan.count, LANES))
    out_ref[:, 7, :] = jnp.broadcast_to(second, (plan.count, LANES))


def last_kernel(plan, f_ref, got_ref, inc_ref, res_ref, u_ref, t_ref):
    depth = plan.depth
    for level in range(plan.levels):
        group, j = divmod(level, depth + 1)
        speaker = plan.device(group, j, 0) if j < depth else plan.device(group, depth - 1, 1)
        for half in range(2):
            lanes = slice(half * LANES, (half + 1) * LANES)
            u_ref[level : level + 1, lanes] = got_ref[speaker, half : half + 1, :]
            t = None
            for core in range(2):
                for part in (0, 1):
                    k = j - part
                    if 0 <= k < depth:
                        row = 2 + 2 * part + half
                        term = got_ref[plan.device(group, k, core), row : row + 1, :]
                        t = term if t is None else t + term
            t_ref[level : level + 1, lanes] = t
    firsts = jnp.zeros((1, LANES), jnp.float32)
    seconds = jnp.zeros((1, LANES), jnp.float32)
    for device, _, _, _ in plan.owners():
        firsts = firsts + got_ref[device, 6:7, :]
        seconds = seconds + got_ref[device, 7:8, :]
    lane = lax.broadcasted_iota(jnp.int32, (1, LANES), 1)
    kept = lane < plan.levels

    def slot(row, n):
        moved = row if n == 0 else pltpu.roll(row, LANES - SLOT * n, 1)
        return jnp.where(kept, moved, 0.0)

    bb, bq, qq, ratio = (slot(firsts, n) for n in range(4))
    qt, bt = (slot(seconds, n) for n in range(2))

    def add(x):
        return jnp.sum(x, axis=1, keepdims=True)

    all_bb = add(bb)
    all_bu = add(ratio * bb - bq)
    whole = all_bu / all_bb
    shift = jnp.where(kept, whole - ratio, 0.0)
    q_q = add(shift * shift * bb + 2 * shift * bq + qq)
    q_bq = add(shift * shift * ratio * bb - shift * shift * bq + shift * bt
               + shift * ratio * bq - shift * qq + qt)
    b_bq = add(shift * ratio * bb - shift * bq + bt)
    q_u = add(shift * ratio * bb - shift * bq + ratio * bq - qq)
    energy = all_bb + all_bu
    step_0 = all_bb / energy
    norm_1 = step_0 * step_0 * q_q
    turn = norm_1 / all_bb
    curve = (step_0 * step_0 * (q_q + q_bq) + turn * step_0 * (q_u + b_bq) + turn * turn * energy)
    step_1 = norm_1 / curve

    rows = lax.broadcasted_iota(jnp.int32, (plan.levels, LANES), 0)
    diagonal = rows == lax.broadcasted_iota(jnp.int32, (plan.levels, LANES), 1)
    ratio_c = add(jnp.where(diagonal, ratio, 0.0))
    shift_c = add(jnp.where(diagonal, shift, 0.0))
    b, u, t = f_ref[:, 0, :], u_ref[...], t_ref[...]
    q = shift_c * b + (ratio_c * b - u)
    b_of_q = shift_c * u + t
    direction = step_0 * q + turn * b
    inc_ref[:, 0, :] = step_0 * b + step_1 * direction
    res_ref[:, 0, :] = step_0 * q - step_1 * (step_0 * (q + b_of_q) + turn * (b + u))


def room(mib):
    return pltpu.CompilerParams(vmem_limit_bytes=mib << 20)


def vmem():
    return pl.BlockSpec(memory_space=pltpu.VMEM)


def smem():
    return pl.BlockSpec(memory_space=pltpu.SMEM)


def by_levels(plan, anomalies, forcing, pair_code, kernel, tile_taper):
    axes = ("band", "tile")
    bf16, f32 = jnp.bfloat16, jnp.float32
    n, rows, columns = plan.count, plan.block, plan.columns
    side = (kernel.shape[0] + 1) // 4
    wide = 4 * side * side
    a, f = anomalies[0, 0], jnp.swapaxes(forcing[0], 0, 1)
    sent = pl.pallas_call(
        functools.partial(pack_kernel, plan, tile_taper.shape[0]),
        out_shape=jax.ShapeDtypeStruct((n, plan.height, LANES), bf16),
        in_specs=[smem(), smem(), vmem(), vmem()],
        out_specs=vmem(),
        scratch_shapes=[pltpu.VMEM((plan.levels * plan.members, columns), f32)],
        name="pack",
    )(pair_code, tile_taper, a, f)
    got = lax.all_to_all(sent, axes, 0, 0)
    me = lax.axis_index(axes)
    info = lax.dynamic_slice(jnp.asarray(plan.table()), (me, 0), (1, 8))[0]
    work = [
        pltpu.VMEM((2, n, columns), f32),
        pltpu.VMEM((len(DIRECTIONS), n, columns), f32),
        pltpu.VMEM((n * rows, columns), bf16),
        pltpu.VMEM((n, rows, columns), f32),
    ]
    maps = pl.pallas_call(
        functools.partial(build_maps, side),
        out_shape=jax.ShapeDtypeStruct((len(ALL_STEPS), columns, columns), bf16),
        in_specs=[vmem()],
        out_specs=vmem(),
        scratch_shapes=[pltpu.VMEM((4 * side - 1, wide), f32),
                        pltpu.VMEM((LANES // side, 3 * side, wide), bf16)],
        cost_estimate=pl.CostEstimate(flops=200_000_000, bytes_accessed=2_000_000, transcendentals=0),
        compiler_params=room(12),
        name="maps",
    )(kernel)
    part = pl.pallas_call(
        functools.partial(first_kernel, plan),
        out_shape=jax.ShapeDtypeStruct((2, plan.bands, plan.lons, columns), f32),
        in_specs=[smem(), vmem(), vmem()],
        out_specs=vmem(),
        scratch_shapes=work,
        compiler_params=room(20),
        name="first",
    )(info, got, maps)
    part = part.reshape(2, n, columns)
    swap = [(i, i ^ 1) for i in range(plan.lons)]
    both = part + lax.ppermute(part, "tile", swap)
    onward = plan.onward()
    before = lax.ppermute(both[1], axes, onward)
    after = lax.ppermute(both[0], axes, [(t, s) for s, t in onward])
    back = pl.pallas_call(
        functools.partial(second_kernel, plan),
        out_shape=jax.ShapeDtypeStruct((n, 8, LANES), f32),
        in_specs=[smem()] + [vmem()] * 5,
        out_specs=vmem(),
        scratch_shapes=work + [pltpu.VMEM((2, plan.bands, plan.lons, columns), f32)],
        compiler_params=room(20),
        name="second",
    )(info, got, maps, both, before, after)
    home = lax.all_to_all(back, axes, 0, 0)
    increment, residual = pl.pallas_call(
        functools.partial(last_kernel, plan),
        out_shape=(jax.ShapeDtypeStruct(f.shape, f32),) * 2,
        in_specs=[vmem(), vmem()],
        out_specs=(vmem(), vmem()),
        scratch_shapes=[pltpu.VMEM((plan.levels, columns), f32)] * 2,
        compiler_params=room(8),
        name="last",
    )(f, home)
    return jnp.swapaxes(increment, 0, 1)[None], jnp.swapaxes(residual, 0, 1)[None]


def padded(block, sides, width):
    for axis, dim in sides:
        count = lax.axis_size(axis)
        forward = [(i, i + 1) for i in range(count - 1)]
        forward.append((count - 1, 0))
        backward = [(target, source) for source, target in forward]
        low = lax.ppermute(
            lax.slice_in_dim(block, block.shape[dim] - width, None, axis=dim), axis, forward
        )
        high = lax.ppermute(lax.slice_in_dim(block, 0, width, axis=dim), axis, backward)
        block = jnp.concatenate([low, block, high], axis=dim)
    return block


def selector(tile_side, offset):
    first_index = np.arange(tile_side)[:, None]
    second_index = np.arange(tile_side)[None, :]
    target = 2 * tile_side - 1 + offset * tile_side + second_index - first_index
    return (np.arange(4 * tile_side - 1)[None, None, :] == target[:, :, None]).astype(np.float32)


def local_map(kernel, row_step, col_step):
    by_lat = jnp.einsum(
        "abp,pq->abq", selector(SIDE, row_step), kernel, precision=lax.Precision.HIGHEST
    )
    full_map = jnp.einsum(
        "abq,cdq->acbd", by_lat, selector(SIDE, col_step), precision=lax.Precision.HIGHEST
    )
    return full_map.reshape(SIDE * SIDE, SIDE * SIDE).astype(jnp.bfloat16)


def all_maps(kernel):
    return [local_map(kernel, 0, 0)] + [
        local_map(kernel, row_step, col_step) for row_step, col_step in DIRECTIONS
    ]


def taper_lookup(tile_taper, code):
    entries = jnp.arange(1, tile_taper.shape[0] + 1, dtype=jnp.int32)
    return jnp.sum(jnp.where(entries == code, tile_taper, jnp.zeros_like(tile_taper)))


def weighted_block(block, field):
    return (block.astype(jnp.float32) * field[:, None, :]).astype(jnp.bfloat16)


def pair_term(own_block, weighted, matrix, weight):
    levels, members, columns = weighted.shape
    spread = lax.dot_general(
        weighted.reshape(levels * members, columns),
        matrix,
        (((1,), (1,)), ((), ())),
        preferred_element_type=jnp.float32,
    )
    summed = jnp.sum(
        own_block.astype(jnp.float32) * spread.reshape(levels, members, columns), axis=1
    )
    return summed * (weight / (members - 1))


def masked_term(code, weight, own_block, weighted, matrix):

    def active():
        return pair_term(own_block, weighted, matrix, weight)

    def inactive():
        return jnp.zeros((weighted.shape[0], weighted.shape[2]), jnp.float32)

    return lax.cond(code > 0, active, inactive)


def covariance_all(blocks, neighbours, pair_codes, tile_taper, local_maps):
    own_block = blocks[1, 1]
    summed_terms = pair_term(
        own_block, weighted_block(own_block, neighbours[1, 1]), local_maps[0], 1.0
    )
    for position, (row_step, col_step) in enumerate(DIRECTIONS):
        code = pair_codes[position]
        weight = taper_lookup(tile_taper, code)
        other_weighted = weighted_block(
            blocks[1 + row_step, 1 + col_step], neighbours[1 + row_step, 1 + col_step]
        )
        summed_terms = summed_terms + masked_term(
            code, weight, own_block, other_weighted, local_maps[position + 1]
        )
    return summed_terms


def global_total(factor_one, factor_two):
    return lax.psum(jnp.sum(factor_one * factor_two), ("band", "tile"))


def on_device(anomalies, forcing, pair_code, kernel, tile_taper):
    pair_codes = pair_code[0, 0]
    kept_maps = all_maps(kernel)
    residual = forcing[0, 0]
    increment = jnp.zeros_like(residual)
    direction = residual
    norm_now = global_total(residual, residual)
    for iteration in range(ITERS):
        blocks = padded(anomalies, (("band", 0), ("tile", 1)), 1)
        neighbours = padded(direction[None, None], (("band", 0), ("tile", 1)), 1)
        mapped = direction + covariance_all(blocks, neighbours, pair_codes, tile_taper, kept_maps)
        step_length = norm_now / global_total(direction, mapped)
        increment = increment + step_length * direction
        residual = residual - step_length * mapped
        norm_next = global_total(residual, residual)
        direction = residual + norm_next / norm_now * direction
        norm_now = norm_next
    return (increment[None, None], residual[None, None])


def solution(mesh):
    specs = (
        P("band", "tile", None, None, None),
        P("band", "tile", None, None),
        P("band", "tile", None),
        P(),
        P(),
    )

    def run(anomalies, forcing, pair_code, kernel, tile_taper):
        plan = Plan(mesh.shape["band"], mesh.shape["tile"], *anomalies.shape[2:])
        step = functools.partial(by_levels, plan) if plan.fits else on_device
        return step(anomalies, forcing, pair_code, kernel, tile_taper)

    return jax.shard_map(
        run,
        mesh=mesh,
        in_specs=specs,
        out_specs=(P("band", "tile", None, None), P("band", "tile", None, None)),
        check_vma=False,
    )
```

```python
import functools

import jax
import jax.numpy as jnp
import numpy as np
from jax import lax
from jax.experimental import pallas as pl
from jax.experimental.pallas import tpu as pltpu
from jax.sharding import PartitionSpec as P

SIDE = 16
ITERS = 2
GRAIN = 8
LANES = 128
SLOT = 32

DIRECTIONS = ((-1, -1), (-1, 0), (-1, 1), (0, -1), (0, 1), (1, -1), (1, 0), (1, 1))
ALL_STEPS = ((0, 0),) + DIRECTIONS


class Plan:
    def __init__(self, bands, lons, levels, members, columns):
        self.bands, self.lons = bands, lons
        self.levels, self.members, self.columns = levels, members, columns
        self.count = bands * lons
        self.rows = levels * members // self.count
        self.step = 2 * self.rows - members
        self.fits = (
            levels * members % self.count == 0
            and members % 2 == 0
            and 0 < self.step < members
            and members % self.step == 0
            and levels <= SLOT
            and lons % GRAIN == 0
            and columns == 2 * LANES
        )
        if not self.fits:
            return
        self.depth = members // self.step
        self.fits = levels % (self.depth + 1) == 0
        if not self.fits:
            return
        self.groups = levels // (self.depth + 1)
        across = lons // 2
        inner = [i ^ (i >> 1) for i in range(across)]
        if sorted(inner) != list(range(across)):
            inner = list(range(across))
        path = []
        for band in range(bands):
            path += [band * across + c for c in (inner if band % 2 == 0 else inner[::-1])]
        self.path = path
        self.block = -(-(self.rows + 3) // 16) * 16
        self.height = 2 * self.block + GRAIN

    def low_rows(self, k):
        return (self.members - k * self.step) // 2

    def device(self, group, k, core):
        return 2 * self.path[group * self.depth + k] + core

    def owners(self):
        for group in range(self.groups):
            for k in range(self.depth):
                for core in range(2):
                    low = group * (self.depth + 1) + k
                    yield self.device(group, k, core), k, core, low

    def table(self):
        out = np.zeros((self.count, 8), np.int32)
        for device, k, core, low in self.owners():
            last = k == self.depth - 1
            out[device, :5] = (self.low_rows(k), core, int(core == 0), int(core == 1 and last), low)
        return out

    def outward(self):
        pairs = []
        for group in range(self.groups):
            for k in range(1, self.depth):
                pairs.append((self.device(group, k, 0), self.device(group, k - 1, 0)))
                pairs.append((self.device(group, k - 1, 1), self.device(group, k, 1)))
        return pairs


def in_three(x):
    high = x.astype(jnp.bfloat16).astype(jnp.float32)
    rest = x - high
    middle = rest.astype(jnp.bfloat16).astype(jnp.float32)
    return [high, middle, rest - middle]


def pack_kernel(plan, tapers, code_ref, taper_ref, a_ref, f_ref, out_ref, wide_ref):
    for level in range(plan.levels):
        wide_ref[level * plan.members : (level + 1) * plan.members, :] = a_ref[level].astype(jnp.float32)
    forcing = in_three(f_ref[:, 0, :])
    lane = lax.broadcasted_iota(jnp.int32, (1, LANES), 1)
    weights = jnp.zeros((1, LANES), jnp.float32)
    for k in range(len(DIRECTIONS)):
        code = code_ref[0, 0, k]
        weight = jnp.float32(0)
        for c in range(tapers):
            weight = jnp.where(code == c + 1, taper_ref[c], weight)
        weights = jnp.where(lane == k, weight, weights)
    weights = weights / jnp.float32(plan.members - 1)
    high, middle, _ = in_three(weights)
    for device, k, core, low in plan.owners():
        count, other = plan.low_rows(k), plan.rows - plan.low_rows(k)
        start = low * plan.members + k * plan.step + core * count
        after = (low + 1) * plan.members + core * other
        for half in range(2):
            lanes = slice(half * LANES, (half + 1) * LANES)
            pieces = [wide_ref[start : start + count, lanes], wide_ref[after : after + other, lanes]]
            pieces += [part[low : low + 1, lanes] for part in forcing]
            spare = plan.block - plan.rows - 3
            if spare:
                pieces.append(jnp.zeros((spare, LANES), jnp.float32))
            out_ref[device, half * plan.block : (half + 1) * plan.block, :] = jnp.concatenate(
                pieces, axis=0
            ).astype(jnp.bfloat16)
        pieces = [part[low + 1 : low + 2, :LANES] for part in forcing]
        pieces += [part[low + 1 : low + 2, LANES:] for part in forcing]
        out_ref[device, 2 * plan.block :, :] = jnp.concatenate(pieces + [high, middle], axis=0).astype(jnp.bfloat16)


def build_maps(side, kernel_ref, lt_ref, by_lat_ref, turned_ref):
    span = 4 * side - 1
    wide = (span + 1) * side
    square = (lax.broadcasted_iota(jnp.int32, (span, span), 0)
              == lax.broadcasted_iota(jnp.int32, (span, span), 1))
    table = kernel_ref[...].astype(jnp.bfloat16)
    flipped = lax.dot_general(
        square.astype(jnp.float32).astype(jnp.bfloat16), table, (((1,), (1,)), ((), ())),
        preferred_element_type=jnp.float32,
    ).astype(jnp.bfloat16)
    block = lax.broadcasted_iota(jnp.int32, (span, wide), 1) // side
    pick = (lax.broadcasted_iota(jnp.int32, (span, wide), 0) == span - 1 - block)
    by_lat_ref[...] = jnp.dot(
        flipped, pick.astype(jnp.float32).astype(jnp.bfloat16), preferred_element_type=jnp.float32
    )
    lane = lax.broadcasted_iota(jnp.int32, (3 * side, wide), 1) % side
    base = jnp.zeros((3 * side, wide), jnp.float32)
    for x in range(side):
        base = jnp.where(lane == x, by_lat_ref[side - 1 - x : 4 * side - 1 - x, :], base)
    turns = LANES // side
    for turn in range(turns):
        moved = base if turn == 0 else pltpu.roll(base, wide - turn * side, 1)
        turned_ref[turn] = moved.astype(jnp.bfloat16)
    for k, (p, q) in enumerate(ALL_STEPS):
        for y in range(side):
            start = (2 * side - 1 - p * side - y) * side
            turn, first = (start % LANES) // side, start // LANES * LANES
            lt_ref[k, y * side : (y + 1) * side, :] = turned_ref[
                turn, (q + 1) * side : (q + 2) * side, first : first + side * side
            ]


def read_extra(plan, got_ref, wide_ref):
    first = plan.rows // 16 * 16
    at = plan.rows - first
    tail = got_ref[:, 2 * plan.block :, :].astype(jnp.float32)
    weights = tail[:, 6, :] + tail[:, 7, :]
    for k in range(len(DIRECTIONS)):
        wide_ref[k] = jnp.broadcast_to(weights[:, k : k + 1], (plan.count, plan.columns))
    low, high = [], []
    for half in range(2):
        slab = got_ref[:, half * plan.block + first : (half + 1) * plan.block, :].astype(jnp.float32)
        low.append(slab[:, at, :] + slab[:, at + 1, :] + slab[:, at + 2, :])
        high.append(tail[:, 3 * half, :] + tail[:, 3 * half + 1, :] + tail[:, 3 * half + 2, :])
    return [jnp.concatenate(low, axis=1), jnp.concatenate(high, axis=1)]


def apply_rows(plan, low, order, got_ref, v_ref, lt_ref, wide_ref, w_ref, s_ref, p_ref):
    bands, lons, rows = plan.bands, plan.lons, plan.block
    place = lax.broadcasted_iota(jnp.int32, (rows, LANES), 0)
    is_low = place < low
    sides = [slice(half * LANES, (half + 1) * LANES) for half in range(2)]

    def block(tile, half):
        return got_ref[tile, half * rows : (half + 1) * rows, :].astype(jnp.float32)

    for tile in range(plan.count):
        v_low, v_high = v_ref[0, tile : tile + 1, :], v_ref[1, tile : tile + 1, :]
        for half, lanes in enumerate(sides):
            v = jnp.where(is_low, v_low[:, lanes], v_high[:, lanes])
            w_ref[tile * rows : (tile + 1) * rows, lanes] = (block(tile, half) * v).astype(jnp.bfloat16)

    for k, (p, q) in enumerate(ALL_STEPS):
        first, last = max(0, p), min(bands, bands + p)
        y = jnp.dot(
            w_ref[first * lons * rows : last * lons * rows, :], lt_ref[k], preferred_element_type=jnp.float32
        )
        for band in range(first, last):
            for l in range(lons):
                tile = (band - p) * lons + (l - q) % lons
                at = ((band - first) * lons + l) * rows
                piece = y[at : at + rows]
                if k == 0:
                    s_ref[tile] = piece * jnp.float32(1.0 / (plan.members - 1))
                else:
                    s_ref[tile] += piece * wide_ref[k - 1, tile : tile + 1, :]

    low_share = jnp.where(is_low, jnp.float32(1), jnp.float32(0))
    high_share = jnp.where(is_low | (place >= plan.rows), jnp.float32(0), jnp.float32(1))
    for band in range(bands):
        for half, lanes in enumerate(sides):
            sums = [[], []]
            for l in range(lons):
                tile = band * lons + l
                product = block(tile, half) * s_ref[tile, :, lanes]
                sums[0].append(jnp.sum(product * low_share, axis=0, keepdims=True))
                sums[1].append(jnp.sum(product * high_share, axis=0, keepdims=True))
            for level in range(2):
                p_ref[order[level], band, :, lanes] = jnp.concatenate(sums[level], axis=0)


def first_kernel(plan, info_ref, got_ref, lt_ref, p_ref, v_ref, wide_ref, w_ref, s_ref):
    v_ref[0], v_ref[1] = read_extra(plan, got_ref, wide_ref)
    order = (info_ref[1], 1 - info_ref[1])
    apply_rows(plan, info_ref[0], order, got_ref, v_ref, lt_ref, wide_ref, w_ref, s_ref, p_ref)


def total(x):
    return jnp.sum(jnp.sum(x, axis=1, keepdims=True), axis=0, keepdims=True)


def second_kernel(plan, info_ref, got_ref, lt_ref, own_ref, other_ref, far_ref, far_other_ref, out_ref,
                  v_ref, wide_ref, w_ref, s_ref, p_ref):
    forcing = read_extra(plan, got_ref, wide_ref)
    mine = (own_ref[0] + other_ref[1]) + far_other_ref[...]
    rest = (own_ref[1] + other_ref[0]) + far_ref[...]
    first_core = info_ref[1] == 0
    images = (jnp.where(first_core, mine, rest), jnp.where(first_core, rest, mine))
    lane = lax.broadcasted_iota(jnp.int32, (1, LANES), 1)
    first = jnp.zeros((1, LANES), jnp.float32)
    for level in range(2):
        b = forcing[level]
        u = images[level]
        bb, bu = total(b * b), total(b * u)
        ratio = jnp.where(bb > 0, bu / jnp.where(bb > 0, bb, 1.0), 0.0)
        q = ratio * b - u
        v_ref[level] = q
        values = (bb, total(b * q), total(q * q), ratio)
        speaks = jnp.where(info_ref[2 + level] > 0, jnp.float32(1), jnp.float32(0))
        for n, value in enumerate(values):
            at = lane == info_ref[4] + level + SLOT * n
            first = first + jnp.where(at, value, 0.0) * speaks
    apply_rows(plan, info_ref[0], (0, 1), got_ref, v_ref, lt_ref, wide_ref, w_ref, s_ref, p_ref)
    second = jnp.zeros((1, LANES), jnp.float32)
    for level in range(2):
        b = forcing[level]
        t = p_ref[level].reshape(plan.count, plan.columns)
        for n, value in enumerate((total(v_ref[level] * t), total(b * t))):
            at = lane == info_ref[4] + level + SLOT * n
            second = second + jnp.where(at, value, 0.0)
    for half in range(2):
        lanes = slice(half * LANES, (half + 1) * LANES)
        out_ref[:, half, :] = mine[:, lanes]
        for level in range(2):
            share = p_ref[level, :, :, lanes].reshape(plan.count, LANES)
            out_ref[:, 2 + 2 * level + half, :] = share
    out_ref[:, 6, :] = jnp.broadcast_to(first, (plan.count, LANES))
    out_ref[:, 7, :] = jnp.broadcast_to(second, (plan.count, LANES))


def last_kernel(plan, f_ref, got_ref, inc_ref, res_ref, u_ref, t_ref):
    depth = plan.depth
    for level in range(plan.levels):
        group, j = divmod(level, depth + 1)
        speaker = plan.device(group, j, 0) if j < depth else plan.device(group, depth - 1, 1)
        for half in range(2):
            lanes = slice(half * LANES, (half + 1) * LANES)
            u_ref[level : level + 1, lanes] = got_ref[speaker, half : half + 1, :]
            t = None
            for core in range(2):
                for part in (0, 1):
                    k = j - part
                    if 0 <= k < depth:
                        row = 2 + 2 * part + half
                        term = got_ref[plan.device(group, k, core), row : row + 1, :]
                        t = term if t is None else t + term
            t_ref[level : level + 1, lanes] = t
    firsts = jnp.zeros((1, LANES), jnp.float32)
    seconds = jnp.zeros((1, LANES), jnp.float32)
    for device, _, _, _ in plan.owners():
        firsts = firsts + got_ref[device, 6:7, :]
        seconds = seconds + got_ref[device, 7:8, :]
    lane = lax.broadcasted_iota(jnp.int32, (1, LANES), 1)
    kept = lane < plan.levels

    def slot(row, n):
        moved = row if n == 0 else pltpu.roll(row, LANES - SLOT * n, 1)
        return jnp.where(kept, moved, 0.0)

    bb, bq, qq, ratio = (slot(firsts, n) for n in range(4))
    qt, bt = (slot(seconds, n) for n in range(2))

    def add(x):
        return jnp.sum(x, axis=1, keepdims=True)

    all_bb = add(bb)
    all_bu = add(ratio * bb - bq)
    whole = all_bu / all_bb
    shift = jnp.where(kept, whole - ratio, 0.0)
    q_q = add(shift * shift * bb + 2 * shift * bq + qq)
    q_bq = add(shift * shift * ratio * bb - shift * shift * bq + shift * bt
               + shift * ratio * bq - shift * qq + qt)
    b_bq = add(shift * ratio * bb - shift * bq + bt)
    q_u = add(shift * ratio * bb - shift * bq + ratio * bq - qq)
    energy = all_bb + all_bu
    step_0 = all_bb / energy
    norm_1 = step_0 * step_0 * q_q
    turn = norm_1 / all_bb
    curve = (step_0 * step_0 * (q_q + q_bq) + turn * step_0 * (q_u + b_bq) + turn * turn * energy)
    step_1 = norm_1 / curve

    rows = lax.broadcasted_iota(jnp.int32, (plan.levels, LANES), 0)
    diagonal = rows == lax.broadcasted_iota(jnp.int32, (plan.levels, LANES), 1)
    ratio_c = add(jnp.where(diagonal, ratio, 0.0))
    shift_c = add(jnp.where(diagonal, shift, 0.0))
    b, u, t = f_ref[:, 0, :], u_ref[...], t_ref[...]
    q = shift_c * b + (ratio_c * b - u)
    b_of_q = shift_c * u + t
    direction = step_0 * q + turn * b
    inc_ref[:, 0, :] = step_0 * b + step_1 * direction
    res_ref[:, 0, :] = step_0 * q - step_1 * (step_0 * (q + b_of_q) + turn * (b + u))


def room(mib):
    return pltpu.CompilerParams(vmem_limit_bytes=mib << 20)


def vmem():
    return pl.BlockSpec(memory_space=pltpu.VMEM)


def smem():
    return pl.BlockSpec(memory_space=pltpu.SMEM)


def by_levels(plan, anomalies, forcing, pair_code, kernel, tile_taper):
    axes = ("band", "tile")
    bf16, f32 = jnp.bfloat16, jnp.float32
    n, rows, columns = plan.count, plan.block, plan.columns
    side = (kernel.shape[0] + 1) // 4
    wide = 4 * side * side
    a, f = anomalies[0, 0], jnp.swapaxes(forcing[0], 0, 1)
    sent = pl.pallas_call(
        functools.partial(pack_kernel, plan, tile_taper.shape[0]),
        out_shape=jax.ShapeDtypeStruct((n, plan.height, LANES), bf16),
        in_specs=[smem(), smem(), vmem(), vmem()],
        out_specs=vmem(),
        scratch_shapes=[pltpu.VMEM((plan.levels * plan.members, columns), f32)],
        name="pack",
    )(pair_code, tile_taper, a, f)
    got = lax.all_to_all(sent, axes, 0, 0)
    me = lax.axis_index(axes)
    info = lax.dynamic_slice(jnp.asarray(plan.table()), (me, 0), (1, 8))[0]
    work = [
        pltpu.VMEM((2, n, columns), f32),
        pltpu.VMEM((len(DIRECTIONS), n, columns), f32),
        pltpu.VMEM((n * rows, columns), bf16),
        pltpu.VMEM((n, rows, columns), f32),
    ]
    maps = pl.pallas_call(
        functools.partial(build_maps, side),
        out_shape=jax.ShapeDtypeStruct((len(ALL_STEPS), columns, columns), bf16),
        in_specs=[vmem()],
        out_specs=vmem(),
        scratch_shapes=[pltpu.VMEM((4 * side - 1, wide), f32),
                        pltpu.VMEM((LANES // side, 3 * side, wide), bf16)],
        cost_estimate=pl.CostEstimate(flops=200_000_000, bytes_accessed=2_000_000, transcendentals=0),
        compiler_params=room(12),
        name="maps",
    )(kernel)
    part = pl.pallas_call(
        functools.partial(first_kernel, plan),
        out_shape=jax.ShapeDtypeStruct((2, plan.bands, plan.lons, columns), f32),
        in_specs=[smem(), vmem(), vmem()],
        out_specs=vmem(),
        scratch_shapes=work,
        compiler_params=room(20),
        name="first",
    )(info, got, maps)
    part = part.reshape(2, n, columns)
    swap = [(i, i ^ 1) for i in range(plan.lons)]
    other = lax.ppermute(part, "tile", swap)
    far = lax.ppermute(part[0] + other[1], axes, plan.outward())
    far_other = lax.ppermute(far, "tile", swap)
    back = pl.pallas_call(
        functools.partial(second_kernel, plan),
        out_shape=jax.ShapeDtypeStruct((n, 8, LANES), f32),
        in_specs=[smem()] + [vmem()] * 6,
        out_specs=vmem(),
        scratch_shapes=work + [pltpu.VMEM((2, plan.bands, plan.lons, columns), f32)],
        compiler_params=room(20),
        name="second",
    )(info, got, maps, part, other, far, far_other)
    home = lax.all_to_all(back, axes, 0, 0)
    increment, residual = pl.pallas_call(
        functools.partial(last_kernel, plan),
        out_shape=(jax.ShapeDtypeStruct(f.shape, f32),) * 2,
        in_specs=[vmem(), vmem()],
        out_specs=(vmem(), vmem()),
        scratch_shapes=[pltpu.VMEM((plan.levels, columns), f32)] * 2,
        compiler_params=room(8),
        name="last",
    )(f, home)
    return jnp.swapaxes(increment, 0, 1)[None], jnp.swapaxes(residual, 0, 1)[None]


def padded(block, sides, width):
    for axis, dim in sides:
        count = lax.axis_size(axis)
        forward = [(i, i + 1) for i in range(count - 1)]
        forward.append((count - 1, 0))
        backward = [(target, source) for source, target in forward]
        low = lax.ppermute(
            lax.slice_in_dim(block, block.shape[dim] - width, None, axis=dim), axis, forward
        )
        high = lax.ppermute(lax.slice_in_dim(block, 0, width, axis=dim), axis, backward)
        block = jnp.concatenate([low, block, high], axis=dim)
    return block


def selector(tile_side, offset):
    first_index = np.arange(tile_side)[:, None]
    second_index = np.arange(tile_side)[None, :]
    target = 2 * tile_side - 1 + offset * tile_side + second_index - first_index
    return (np.arange(4 * tile_side - 1)[None, None, :] == target[:, :, None]).astype(np.float32)


def local_map(kernel, row_step, col_step):
    by_lat = jnp.einsum(
        "abp,pq->abq", selector(SIDE, row_step), kernel, precision=lax.Precision.HIGHEST
    )
    full_map = jnp.einsum(
        "abq,cdq->acbd", by_lat, selector(SIDE, col_step), precision=lax.Precision.HIGHEST
    )
    return full_map.reshape(SIDE * SIDE, SIDE * SIDE).astype(jnp.bfloat16)


def all_maps(kernel):
    return [local_map(kernel, 0, 0)] + [
        local_map(kernel, row_step, col_step) for row_step, col_step in DIRECTIONS
    ]


def taper_lookup(tile_taper, code):
    entries = jnp.arange(1, tile_taper.shape[0] + 1, dtype=jnp.int32)
    return jnp.sum(jnp.where(entries == code, tile_taper, jnp.zeros_like(tile_taper)))


def weighted_block(block, field):
    return (block.astype(jnp.float32) * field[:, None, :]).astype(jnp.bfloat16)


def pair_term(own_block, weighted, matrix, weight):
    levels, members, columns = weighted.shape
    spread = lax.dot_general(
        weighted.reshape(levels * members, columns),
        matrix,
        (((1,), (1,)), ((), ())),
        preferred_element_type=jnp.float32,
    )
    summed = jnp.sum(
        own_block.astype(jnp.float32) * spread.reshape(levels, members, columns), axis=1
    )
    return summed * (weight / (members - 1))


def masked_term(code, weight, own_block, weighted, matrix):

    def active():
        return pair_term(own_block, weighted, matrix, weight)

    def inactive():
        return jnp.zeros((weighted.shape[0], weighted.shape[2]), jnp.float32)

    return lax.cond(code > 0, active, inactive)


def covariance_all(blocks, neighbours, pair_codes, tile_taper, local_maps):
    own_block = blocks[1, 1]
    summed_terms = pair_term(
        own_block, weighted_block(own_block, neighbours[1, 1]), local_maps[0], 1.0
    )
    for position, (row_step, col_step) in enumerate(DIRECTIONS):
        code = pair_codes[position]
        weight = taper_lookup(tile_taper, code)
        other_weighted = weighted_block(
            blocks[1 + row_step, 1 + col_step], neighbours[1 + row_step, 1 + col_step]
        )
        summed_terms = summed_terms + masked_term(
            code, weight, own_block, other_weighted, local_maps[position + 1]
        )
    return summed_terms


def global_total(factor_one, factor_two):
    return lax.psum(jnp.sum(factor_one * factor_two), ("band", "tile"))


def on_device(anomalies, forcing, pair_code, kernel, tile_taper):
    pair_codes = pair_code[0, 0]
    kept_maps = all_maps(kernel)
    residual = forcing[0, 0]
    increment = jnp.zeros_like(residual)
    direction = residual
    norm_now = global_total(residual, residual)
    for iteration in range(ITERS):
        blocks = padded(anomalies, (("band", 0), ("tile", 1)), 1)
        neighbours = padded(direction[None, None], (("band", 0), ("tile", 1)), 1)
        mapped = direction + covariance_all(blocks, neighbours, pair_codes, tile_taper, kept_maps)
        step_length = norm_now / global_total(direction, mapped)
        increment = increment + step_length * direction
        residual = residual - step_length * mapped
        norm_next = global_total(residual, residual)
        direction = residual + norm_next / norm_now * direction
        norm_now = norm_next
    return (increment[None, None], residual[None, None])


def solution(mesh):
    specs = (
        P("band", "tile", None, None, None),
        P("band", "tile", None, None),
        P("band", "tile", None),
        P(),
        P(),
    )

    def run(anomalies, forcing, pair_code, kernel, tile_taper):
        plan = Plan(mesh.shape["band"], mesh.shape["tile"], *anomalies.shape[2:])
        step = functools.partial(by_levels, plan) if plan.fits else on_device
        return step(anomalies, forcing, pair_code, kernel, tile_taper)

    return jax.shard_map(
        run,
        mesh=mesh,
        in_specs=specs,
        out_specs=(P("band", "tile", None, None), P("band", "tile", None, None)),
        check_vma=False,
    )
```

```python
import functools

import jax
import jax.numpy as jnp
import numpy as np
from jax import lax
from jax.experimental import pallas as pl
from jax.experimental.pallas import tpu as pltpu
from jax.sharding import PartitionSpec as P

SIDE = 16
ITERS = 2
GRAIN = 8
LANES = 128
SLOT = 32
CHUNK = 1

DIRECTIONS = ((-1, -1), (-1, 0), (-1, 1), (0, -1), (0, 1), (1, -1), (1, 0), (1, 1))
ALL_STEPS = ((0, 0),) + DIRECTIONS


class Plan:
    def __init__(self, bands, lons, levels, members, columns):
        self.bands, self.lons = bands, lons
        self.levels, self.members, self.columns = levels, members, columns
        self.count = bands * lons
        self.rows = levels * members // self.count
        self.step = 2 * self.rows - members
        self.fits = (
            levels * members % self.count == 0
            and members % 2 == 0
            and 0 < self.step < members
            and members % self.step == 0
            and levels <= SLOT
            and lons % GRAIN == 0
            and columns == 2 * LANES
        )
        if not self.fits:
            return
        self.depth = members // self.step
        self.fits = levels % (self.depth + 1) == 0
        if not self.fits:
            return
        self.groups = levels // (self.depth + 1)
        across = lons // 2
        inner = [i ^ (i >> 1) for i in range(across)]
        if sorted(inner) != list(range(across)):
            inner = list(range(across))
        path = []
        for band in range(bands):
            path += [band * across + c for c in (inner if band % 2 == 0 else inner[::-1])]
        self.path = path
        self.block = -(-(self.rows + 3) // 16) * 16
        self.height = 2 * self.block + GRAIN

    def low_rows(self, k):
        return (self.members - k * self.step) // 2

    def device(self, group, k, core):
        return 2 * self.path[group * self.depth + k] + core

    def owners(self):
        for group in range(self.groups):
            for k in range(self.depth):
                for core in range(2):
                    low = group * (self.depth + 1) + k
                    yield self.device(group, k, core), k, core, low

    def table(self):
        out = np.zeros((self.count, 8), np.int32)
        for device, k, core, low in self.owners():
            last = k == self.depth - 1
            out[device, :5] = (self.low_rows(k), core, int(core == 0), int(core == 1 and last), low)
        return out

    def outward(self):
        pairs = []
        for group in range(self.groups):
            for k in range(1, self.depth):
                pairs.append((self.device(group, k, 0), self.device(group, k - 1, 0)))
                pairs.append((self.device(group, k - 1, 1), self.device(group, k, 1)))
        return pairs


def in_three(x):
    high = x.astype(jnp.bfloat16).astype(jnp.float32)
    rest = x - high
    middle = rest.astype(jnp.bfloat16).astype(jnp.float32)
    return [high, middle, rest - middle]


def pack_kernel(plan, tapers, code_hbm, taper_hbm, a_ref, f_hbm, out_ref,
                code_ref, taper_ref, f_ref, near_ref, wide_ref, sent_ref, small_sem, in_sem, out_sem):
    share, size = plan.depth + 1, plan.count // plan.groups

    def fetch(group):
        run = pl.ds(group * share, share)
        return pltpu.make_async_copy(a_ref.at[run], near_ref.at[run], in_sem.at[group])

    small = [
        pltpu.make_async_copy(source, target, small_sem.at[n])
        for n, (source, target) in enumerate(((code_hbm, code_ref), (taper_hbm, taper_ref), (f_hbm, f_ref)))
    ]
    for copy in small:
        copy.start()
    for group in range(plan.groups):
        fetch(group).start()
    for copy in small:
        copy.wait()
    forcing = in_three(f_ref[:, 0, :])
    lane = lax.broadcasted_iota(jnp.int32, (1, LANES), 1)
    weights = jnp.zeros((1, LANES), jnp.float32)
    for k in range(len(DIRECTIONS)):
        code = code_ref[0, 0, k]
        weight = jnp.float32(0)
        for c in range(tapers):
            weight = jnp.where(code == c + 1, taper_ref[c], weight)
        weights = jnp.where(lane == k, weight, weights)
    weights = weights / jnp.float32(plan.members - 1)
    high, middle, _ = in_three(weights)
    here = 0
    copies = []
    for device, k, core, low in plan.owners():
        if low % share == 0 and core == 0:
            fetch(low // share).wait()
        while here < low + 2:
            wide_ref[here * plan.members : (here + 1) * plan.members, :] = near_ref[here].astype(jnp.float32)
            here += 1
        count, other = plan.low_rows(k), plan.rows - plan.low_rows(k)
        start = low * plan.members + k * plan.step + core * count
        after = (low + 1) * plan.members + core * other
        for half in range(2):
            lanes = slice(half * LANES, (half + 1) * LANES)
            pieces = [wide_ref[start : start + count, lanes], wide_ref[after : after + other, lanes]]
            pieces += [part[low : low + 1, lanes] for part in forcing]
            spare = plan.block - plan.rows - 3
            if spare:
                pieces.append(jnp.zeros((spare, LANES), jnp.float32))
            sent_ref[device, half * plan.block : (half + 1) * plan.block, :] = jnp.concatenate(
                pieces, axis=0
            ).astype(jnp.bfloat16)
        pieces = [part[low + 1 : low + 2, :LANES] for part in forcing]
        pieces += [part[low + 1 : low + 2, LANES:] for part in forcing]
        sent_ref[device, 2 * plan.block :, :] = jnp.concatenate(pieces + [high, middle], axis=0).astype(jnp.bfloat16)
        if k == plan.depth - 1 and core == 1:
            run = pl.ds(len(copies) * size, size)
            copies.append(pltpu.make_async_copy(sent_ref.at[run], out_ref.at[run], out_sem.at[len(copies)]))
            copies[-1].start()
    for copy in copies:
        copy.wait()


def build_maps(side, kernel_ref, lt_ref, by_lat_ref, turned_ref):
    span = 4 * side - 1
    wide = (span + 1) * side
    square = (lax.broadcasted_iota(jnp.int32, (span, span), 0)
              == lax.broadcasted_iota(jnp.int32, (span, span), 1))
    table = kernel_ref[...].astype(jnp.bfloat16)
    flipped = lax.dot_general(
        square.astype(jnp.float32).astype(jnp.bfloat16), table, (((1,), (1,)), ((), ())),
        preferred_element_type=jnp.float32,
    ).astype(jnp.bfloat16)
    block = lax.broadcasted_iota(jnp.int32, (span, wide), 1) // side
    pick = (lax.broadcasted_iota(jnp.int32, (span, wide), 0) == span - 1 - block)
    by_lat_ref[...] = jnp.dot(
        flipped, pick.astype(jnp.float32).astype(jnp.bfloat16), preferred_element_type=jnp.float32
    )
    lane = lax.broadcasted_iota(jnp.int32, (3 * side, wide), 1) % side
    base = jnp.zeros((3 * side, wide), jnp.float32)
    for x in range(side):
        base = jnp.where(lane == x, by_lat_ref[side - 1 - x : 4 * side - 1 - x, :], base)
    turns = LANES // side
    for turn in range(turns):
        moved = base if turn == 0 else pltpu.roll(base, wide - turn * side, 1)
        turned_ref[turn] = moved.astype(jnp.bfloat16)
    for k, (p, q) in enumerate(ALL_STEPS):
        for y in range(side):
            start = (2 * side - 1 - p * side - y) * side
            turn, first = (start % LANES) // side, start // LANES * LANES
            lt_ref[k, y * side : (y + 1) * side, :] = turned_ref[
                turn, (q + 1) * side : (q + 2) * side, first : first + side * side
            ]


def read_extra(plan, got_ref, wide_ref):
    first = plan.rows // 16 * 16
    at = plan.rows - first
    tail = got_ref[:, 2 * plan.block :, :].astype(jnp.float32)
    weights = tail[:, 6, :] + tail[:, 7, :]
    for k in range(len(DIRECTIONS)):
        wide_ref[k] = jnp.broadcast_to(weights[:, k : k + 1], (plan.count, plan.columns))
    low, high = [], []
    for half in range(2):
        slab = got_ref[:, half * plan.block + first : (half + 1) * plan.block, :].astype(jnp.float32)
        low.append(slab[:, at, :] + slab[:, at + 1, :] + slab[:, at + 2, :])
        high.append(tail[:, 3 * half, :] + tail[:, 3 * half + 1, :] + tail[:, 3 * half + 2, :])
    return [jnp.concatenate(low, axis=1), jnp.concatenate(high, axis=1)]


def apply_rows(plan, low, order, got_ref, v_ref, lt_ref, wide_ref, w_ref, s_ref, p_ref):
    bands, lons, rows = plan.bands, plan.lons, plan.block
    place = lax.broadcasted_iota(jnp.int32, (rows, LANES), 0)
    is_low = place < low
    sides = [slice(half * LANES, (half + 1) * LANES) for half in range(2)]

    def block(tile, half):
        return got_ref[tile, half * rows : (half + 1) * rows, :].astype(jnp.float32)

    for tile in range(plan.count):
        v_low, v_high = v_ref[0, tile : tile + 1, :], v_ref[1, tile : tile + 1, :]
        for half, lanes in enumerate(sides):
            v = jnp.where(is_low, v_low[:, lanes], v_high[:, lanes])
            w_ref[tile * rows : (tile + 1) * rows, lanes] = (block(tile, half) * v).astype(jnp.bfloat16)

    low_share = jnp.where(is_low, jnp.float32(1), jnp.float32(0))
    high_share = jnp.where(is_low | (place >= plan.rows), jnp.float32(0), jnp.float32(1))
    sums = {}

    def finish(tile, spread):
        for half, lanes in enumerate(sides):
            product = block(tile, half) * spread[:, lanes]
            for level, share in enumerate((low_share, high_share)):
                sums[tile, level, half] = jnp.sum(product * share, axis=0, keepdims=True)

    touched = set()
    steps = sorted(ALL_STEPS, key=lambda step: (step[0] == 0, step == (0, 0)))
    for start in range(0, bands, CHUNK):
        stop = min(start + CHUNK, bands)
        for p, q in steps:
            first, last = max(0, start + p), min(bands, stop + p)
            if first >= last:
                continue
            k = ALL_STEPS.index((p, q))
            y = jnp.dot(
                w_ref[first * lons * rows : last * lons * rows, :], lt_ref[k], preferred_element_type=jnp.float32
            )
            for band in range(first, last):
                for l in range(lons):
                    tile = (band - p) * lons + (l - q) % lons
                    at = ((band - first) * lons + l) * rows
                    term = y[at : at + rows]
                    if k == 0:
                        finish(tile, s_ref[tile] + term * jnp.float32(1.0 / (plan.members - 1)))
                        continue
                    term = term * wide_ref[k - 1, tile : tile + 1, :]
                    if tile in touched:
                        s_ref[tile] += term
                    else:
                        s_ref[tile] = term
                        touched.add(tile)
                if k == 0:
                    for level in range(2):
                        for half, lanes in enumerate(sides):
                            p_ref[order[level], band, :, lanes] = jnp.concatenate(
                                [sums[band * lons + l, level, half] for l in range(lons)], axis=0
                            )


def first_kernel(plan, info_ref, got_ref, lt_ref, p_ref, v_ref, wide_ref, w_ref, s_ref):
    v_ref[0], v_ref[1] = read_extra(plan, got_ref, wide_ref)
    order = (info_ref[1], 1 - info_ref[1])
    apply_rows(plan, info_ref[0], order, got_ref, v_ref, lt_ref, wide_ref, w_ref, s_ref, p_ref)


def total(x):
    return jnp.sum(jnp.sum(x, axis=1, keepdims=True), axis=0, keepdims=True)


def second_kernel(plan, info_ref, got_ref, lt_ref, b_ref, wide_ref, own_ref, other_ref, far_ref, far_other_ref,
                  out_ref, v_ref, w_ref, s_ref, p_ref):
    mine = (own_ref[0] + other_ref[1]) + far_other_ref[...]
    rest = (own_ref[1] + other_ref[0]) + far_ref[...]
    first_core = info_ref[1] == 0
    images = (jnp.where(first_core, mine, rest), jnp.where(first_core, rest, mine))
    lane = lax.broadcasted_iota(jnp.int32, (1, LANES), 1)
    first = jnp.zeros((1, LANES), jnp.float32)
    for level in range(2):
        b = b_ref[level]
        u = images[level]
        bb, bu = total(b * b), total(b * u)
        ratio = jnp.where(bb > 0, bu / jnp.where(bb > 0, bb, 1.0), 0.0)
        q = ratio * b - u
        v_ref[level] = q
        values = (bb, total(b * q), total(q * q), ratio)
        speaks = jnp.where(info_ref[2 + level] > 0, jnp.float32(1), jnp.float32(0))
        for n, value in enumerate(values):
            at = lane == info_ref[4] + level + SLOT * n
            first = first + jnp.where(at, value, 0.0) * speaks
    apply_rows(plan, info_ref[0], (0, 1), got_ref, v_ref, lt_ref, wide_ref, w_ref, s_ref, p_ref)
    second = jnp.zeros((1, LANES), jnp.float32)
    for level in range(2):
        b = b_ref[level]
        t = p_ref[level].reshape(plan.count, plan.columns)
        for n, value in enumerate((total(v_ref[level] * t), total(b * t))):
            at = lane == info_ref[4] + level + SLOT * n
            second = second + jnp.where(at, value, 0.0)
    for half in range(2):
        lanes = slice(half * LANES, (half + 1) * LANES)
        out_ref[:, half, :] = mine[:, lanes]
        for level in range(2):
            share = p_ref[level, :, :, lanes].reshape(plan.count, LANES)
            out_ref[:, 2 + 2 * level + half, :] = share
    out_ref[:, 6, :] = jnp.broadcast_to(first, (plan.count, LANES))
    out_ref[:, 7, :] = jnp.broadcast_to(second, (plan.count, LANES))


def last_kernel(plan, f_ref, got_ref, inc_ref, res_ref, u_ref, t_ref):
    depth = plan.depth
    for level in range(plan.levels):
        group, j = divmod(level, depth + 1)
        speaker = plan.device(group, j, 0) if j < depth else plan.device(group, depth - 1, 1)
        for half in range(2):
            lanes = slice(half * LANES, (half + 1) * LANES)
            u_ref[level : level + 1, lanes] = got_ref[speaker, half : half + 1, :]
            t = None
            for core in range(2):
                for part in (0, 1):
                    k = j - part
                    if 0 <= k < depth:
                        row = 2 + 2 * part + half
                        term = got_ref[plan.device(group, k, core), row : row + 1, :]
                        t = term if t is None else t + term
            t_ref[level : level + 1, lanes] = t
    firsts = jnp.zeros((1, LANES), jnp.float32)
    seconds = jnp.zeros((1, LANES), jnp.float32)
    for device, _, _, _ in plan.owners():
        firsts = firsts + got_ref[device, 6:7, :]
        seconds = seconds + got_ref[device, 7:8, :]
    lane = lax.broadcasted_iota(jnp.int32, (1, LANES), 1)
    kept = lane < plan.levels

    def slot(row, n):
        moved = row if n == 0 else pltpu.roll(row, LANES - SLOT * n, 1)
        return jnp.where(kept, moved, 0.0)

    bb, bq, qq, ratio = (slot(firsts, n) for n in range(4))
    qt, bt = (slot(seconds, n) for n in range(2))

    def add(x):
        return jnp.sum(x, axis=1, keepdims=True)

    all_bb = add(bb)
    all_bu = add(ratio * bb - bq)
    whole = all_bu / all_bb
    shift = jnp.where(kept, whole - ratio, 0.0)
    q_q = add(shift * shift * bb + 2 * shift * bq + qq)
    q_bq = add(shift * shift * ratio * bb - shift * shift * bq + shift * bt
               + shift * ratio * bq - shift * qq + qt)
    b_bq = add(shift * ratio * bb - shift * bq + bt)
    q_u = add(shift * ratio * bb - shift * bq + ratio * bq - qq)
    energy = all_bb + all_bu
    step_0 = all_bb / energy
    norm_1 = step_0 * step_0 * q_q
    turn = norm_1 / all_bb
    curve = (step_0 * step_0 * (q_q + q_bq) + turn * step_0 * (q_u + b_bq) + turn * turn * energy)
    step_1 = norm_1 / curve

    rows = lax.broadcasted_iota(jnp.int32, (plan.levels, LANES), 0)
    diagonal = rows == lax.broadcasted_iota(jnp.int32, (plan.levels, LANES), 1)
    ratio_c = add(jnp.where(diagonal, ratio, 0.0))
    shift_c = add(jnp.where(diagonal, shift, 0.0))
    b, u, t = f_ref[:, 0, :], u_ref[...], t_ref[...]
    q = shift_c * b + (ratio_c * b - u)
    b_of_q = shift_c * u + t
    direction = step_0 * q + turn * b
    inc_ref[:, 0, :] = step_0 * b + step_1 * direction
    res_ref[:, 0, :] = step_0 * q - step_1 * (step_0 * (q + b_of_q) + turn * (b + u))


def room(mib):
    return pltpu.CompilerParams(vmem_limit_bytes=mib << 20)


def vmem():
    return pl.BlockSpec(memory_space=pltpu.VMEM)


def smem():
    return pl.BlockSpec(memory_space=pltpu.SMEM)


def by_levels(plan, anomalies, forcing, pair_code, kernel, tile_taper):
    axes = ("band", "tile")
    bf16, f32 = jnp.bfloat16, jnp.float32
    n, rows, columns = plan.count, plan.block, plan.columns
    side = (kernel.shape[0] + 1) // 4
    wide = 4 * side * side
    a, f = anomalies[0, 0], jnp.swapaxes(forcing[0], 0, 1)
    sent = pl.pallas_call(
        functools.partial(pack_kernel, plan, tile_taper.shape[0]),
        out_shape=jax.ShapeDtypeStruct((n, plan.height, LANES), bf16),
        in_specs=[pl.BlockSpec(memory_space=pl.ANY)] * 4,
        out_specs=pl.BlockSpec(memory_space=pl.ANY),
        scratch_shapes=[pltpu.SMEM(pair_code.shape, jnp.int32),
                        pltpu.SMEM(tile_taper.shape, f32),
                        pltpu.VMEM(f.shape, f32),
                        pltpu.VMEM(a.shape, bf16),
                        pltpu.VMEM((plan.levels * plan.members, columns), f32),
                        pltpu.VMEM((n, plan.height, LANES), bf16),
                        pltpu.SemaphoreType.DMA((3,)),
                        pltpu.SemaphoreType.DMA((plan.groups,)),
                        pltpu.SemaphoreType.DMA((plan.groups,))],
        name="pack",
    )(pair_code, tile_taper, a, f)
    got = lax.all_to_all(sent, axes, 0, 0)
    me = lax.axis_index(axes)
    info = lax.dynamic_slice(jnp.asarray(plan.table()), (me, 0), (1, 8))[0]
    both = jax.ShapeDtypeStruct((2, n, columns), f32)
    shares = jax.ShapeDtypeStruct((2, plan.bands, plan.lons, columns), f32)
    weights = jax.ShapeDtypeStruct((len(DIRECTIONS), n, columns), f32)
    work = [pltpu.VMEM((n * rows, columns), bf16), pltpu.VMEM((n, rows, columns), f32)]
    maps = pl.pallas_call(
        functools.partial(build_maps, side),
        out_shape=jax.ShapeDtypeStruct((len(ALL_STEPS), columns, columns), bf16),
        in_specs=[vmem()],
        out_specs=vmem(),
        scratch_shapes=[pltpu.VMEM((4 * side - 1, wide), f32),
                        pltpu.VMEM((LANES // side, 3 * side, wide), bf16)],
        cost_estimate=pl.CostEstimate(flops=200_000_000, bytes_accessed=2_000_000, transcendentals=0),
        compiler_params=room(12),
        name="maps",
    )(kernel)
    part, b, wide_weights = pl.pallas_call(
        functools.partial(first_kernel, plan),
        out_shape=(shares, both, weights),
        in_specs=[smem(), vmem(), vmem()],
        out_specs=(vmem(),) * 3,
        scratch_shapes=work,
        compiler_params=room(20),
        name="first",
    )(info, got, maps)
    part = part.reshape(2, n, columns)
    swap = [(i, i ^ 1) for i in range(plan.lons)]
    other = lax.ppermute(part, "tile", swap)
    far = lax.ppermute(part[0] + other[1], axes, plan.outward())
    far_other = lax.ppermute(far, "tile", swap)
    back = pl.pallas_call(
        functools.partial(second_kernel, plan),
        out_shape=jax.ShapeDtypeStruct((n, 8, LANES), f32),
        in_specs=[smem()] + [vmem()] * 8,
        out_specs=vmem(),
        scratch_shapes=[pltpu.VMEM(both.shape, f32)] + work + [pltpu.VMEM(shares.shape, f32)],
        compiler_params=room(20),
        name="second",
    )(info, got, maps, b, wide_weights, part, other, far, far_other)
    home = lax.all_to_all(back, axes, 0, 0)
    increment, residual = pl.pallas_call(
        functools.partial(last_kernel, plan),
        out_shape=(jax.ShapeDtypeStruct(f.shape, f32),) * 2,
        in_specs=[vmem(), vmem()],
        out_specs=(vmem(), vmem()),
        scratch_shapes=[pltpu.VMEM((plan.levels, columns), f32)] * 2,
        compiler_params=room(8),
        name="last",
    )(f, home)
    return jnp.swapaxes(increment, 0, 1)[None], jnp.swapaxes(residual, 0, 1)[None]


def padded(block, sides, width):
    for axis, dim in sides:
        count = lax.axis_size(axis)
        forward = [(i, i + 1) for i in range(count - 1)]
        forward.append((count - 1, 0))
        backward = [(target, source) for source, target in forward]
        low = lax.ppermute(
            lax.slice_in_dim(block, block.shape[dim] - width, None, axis=dim), axis, forward
        )
        high = lax.ppermute(lax.slice_in_dim(block, 0, width, axis=dim), axis, backward)
        block = jnp.concatenate([low, block, high], axis=dim)
    return block


def selector(tile_side, offset):
    first_index = np.arange(tile_side)[:, None]
    second_index = np.arange(tile_side)[None, :]
    target = 2 * tile_side - 1 + offset * tile_side + second_index - first_index
    return (np.arange(4 * tile_side - 1)[None, None, :] == target[:, :, None]).astype(np.float32)


def local_map(kernel, row_step, col_step):
    by_lat = jnp.einsum(
        "abp,pq->abq", selector(SIDE, row_step), kernel, precision=lax.Precision.HIGHEST
    )
    full_map = jnp.einsum(
        "abq,cdq->acbd", by_lat, selector(SIDE, col_step), precision=lax.Precision.HIGHEST
    )
    return full_map.reshape(SIDE * SIDE, SIDE * SIDE).astype(jnp.bfloat16)


def all_maps(kernel):
    return [local_map(kernel, 0, 0)] + [
        local_map(kernel, row_step, col_step) for row_step, col_step in DIRECTIONS
    ]


def taper_lookup(tile_taper, code):
    entries = jnp.arange(1, tile_taper.shape[0] + 1, dtype=jnp.int32)
    return jnp.sum(jnp.where(entries == code, tile_taper, jnp.zeros_like(tile_taper)))


def weighted_block(block, field):
    return (block.astype(jnp.float32) * field[:, None, :]).astype(jnp.bfloat16)


def pair_term(own_block, weighted, matrix, weight):
    levels, members, columns = weighted.shape
    spread = lax.dot_general(
        weighted.reshape(levels * members, columns),
        matrix,
        (((1,), (1,)), ((), ())),
        preferred_element_type=jnp.float32,
    )
    summed = jnp.sum(
        own_block.astype(jnp.float32) * spread.reshape(levels, members, columns), axis=1
    )
    return summed * (weight / (members - 1))


def masked_term(code, weight, own_block, weighted, matrix):

    def active():
        return pair_term(own_block, weighted, matrix, weight)

    def inactive():
        return jnp.zeros((weighted.shape[0], weighted.shape[2]), jnp.float32)

    return lax.cond(code > 0, active, inactive)


def covariance_all(blocks, neighbours, pair_codes, tile_taper, local_maps):
    own_block = blocks[1, 1]
    summed_terms = pair_term(
        own_block, weighted_block(own_block, neighbours[1, 1]), local_maps[0], 1.0
    )
    for position, (row_step, col_step) in enumerate(DIRECTIONS):
        code = pair_codes[position]
        weight = taper_lookup(tile_taper, code)
        other_weighted = weighted_block(
            blocks[1 + row_step, 1 + col_step], neighbours[1 + row_step, 1 + col_step]
        )
        summed_terms = summed_terms + masked_term(
            code, weight, own_block, other_weighted, local_maps[position + 1]
        )
    return summed_terms


def global_total(factor_one, factor_two):
    return lax.psum(jnp.sum(factor_one * factor_two), ("band", "tile"))


def on_device(anomalies, forcing, pair_code, kernel, tile_taper):
    pair_codes = pair_code[0, 0]
    kept_maps = all_maps(kernel)
    residual = forcing[0, 0]
    increment = jnp.zeros_like(residual)
    direction = residual
    norm_now = global_total(residual, residual)
    for iteration in range(ITERS):
        blocks = padded(anomalies, (("band", 0), ("tile", 1)), 1)
        neighbours = padded(direction[None, None], (("band", 0), ("tile", 1)), 1)
        mapped = direction + covariance_all(blocks, neighbours, pair_codes, tile_taper, kept_maps)
        step_length = norm_now / global_total(direction, mapped)
        increment = increment + step_length * direction
        residual = residual - step_length * mapped
        norm_next = global_total(residual, residual)
        direction = residual + norm_next / norm_now * direction
        norm_now = norm_next
    return (increment[None, None], residual[None, None])


def solution(mesh):
    specs = (
        P("band", "tile", None, None, None),
        P("band", "tile", None, None),
        P("band", "tile", None),
        P(),
        P(),
    )

    def run(anomalies, forcing, pair_code, kernel, tile_taper):
        plan = Plan(mesh.shape["band"], mesh.shape["tile"], *anomalies.shape[2:])
        step = functools.partial(by_levels, plan) if plan.fits else on_device
        return step(anomalies, forcing, pair_code, kernel, tile_taper)

    return jax.shard_map(
        run,
        mesh=mesh,
        in_specs=specs,
        out_specs=(P("band", "tile", None, None), P("band", "tile", None, None)),
        check_vma=False,
    )
```

```python
import functools

import jax
import jax.numpy as jnp
import numpy as np
from jax import lax
from jax.experimental import pallas as pl
from jax.experimental.pallas import tpu as pltpu
from jax.sharding import PartitionSpec as P

SIDE = 16
ITERS = 2
GRAIN = 8
LANES = 128
SLOT = 32
CHUNK = 1

DIRECTIONS = ((-1, -1), (-1, 0), (-1, 1), (0, -1), (0, 1), (1, -1), (1, 0), (1, 1))
ALL_STEPS = ((0, 0),) + DIRECTIONS


class Plan:
    def __init__(self, bands, lons, levels, members, columns):
        self.bands, self.lons = bands, lons
        self.levels, self.members, self.columns = levels, members, columns
        self.count = bands * lons
        self.rows = levels * members // self.count
        self.step = 2 * self.rows - members
        self.fits = (
            levels * members % self.count == 0
            and members % 2 == 0
            and 0 < self.step < members
            and members % self.step == 0
            and levels <= SLOT
            and lons % GRAIN == 0
            and columns == 2 * LANES
        )
        if not self.fits:
            return
        self.depth = members // self.step
        self.fits = levels % (self.depth + 1) == 0
        if not self.fits:
            return
        self.groups = levels // (self.depth + 1)
        across = lons // 2
        inner = [i ^ (i >> 1) for i in range(across)]
        if sorted(inner) != list(range(across)):
            inner = list(range(across))
        path = []
        for band in range(bands):
            path += [band * across + c for c in (inner if band % 2 == 0 else inner[::-1])]
        self.path = path
        self.block = -(-(self.rows + 3) // 16) * 16
        self.height = 2 * self.block + GRAIN

    def low_rows(self, k):
        return (self.members - k * self.step) // 2

    def device(self, group, k, core):
        return 2 * self.path[group * self.depth + k] + core

    def owners(self):
        for group in range(self.groups):
            for k in range(self.depth):
                for core in range(2):
                    low = group * (self.depth + 1) + k
                    yield self.device(group, k, core), k, core, low

    def table(self):
        out = np.zeros((self.count, 8), np.int32)
        for device, k, core, low in self.owners():
            last = k == self.depth - 1
            joined = (int(not last), int(k > 0))
            out[device, :5] = (self.low_rows(k), core, int(core == 0), int(core == 1 and last), low)
            out[device, 5:7] = (joined[core], joined[1 - core])
        return out

    def outward(self):
        pairs = []
        for group in range(self.groups):
            for k in range(self.depth):
                pairs.append((self.device(group, k, 0), self.device(group, (k - 1) % self.depth, 0)))
                pairs.append((self.device(group, k, 1), self.device(group, (k + 1) % self.depth, 1)))
        return pairs


def in_three(x):
    high = x.astype(jnp.bfloat16).astype(jnp.float32)
    rest = x - high
    middle = rest.astype(jnp.bfloat16).astype(jnp.float32)
    return [high, middle, rest - middle]


def pack_kernel(plan, tapers, code_hbm, taper_hbm, a_ref, f_hbm, out_ref,
                code_ref, taper_ref, f_ref, near_ref, wide_ref, sent_ref, small_sem, in_sem, out_sem):
    share, size = plan.depth + 1, plan.count // plan.groups

    def fetch(group):
        run = pl.ds(group * share, share)
        return pltpu.make_async_copy(a_ref.at[run], near_ref.at[run], in_sem.at[group])

    small = [
        pltpu.make_async_copy(source, target, small_sem.at[n])
        for n, (source, target) in enumerate(((code_hbm, code_ref), (taper_hbm, taper_ref), (f_hbm, f_ref)))
    ]
    for copy in small:
        copy.start()
    for group in range(plan.groups):
        fetch(group).start()
    for copy in small:
        copy.wait()
    forcing = in_three(f_ref[:, 0, :])
    lane = lax.broadcasted_iota(jnp.int32, (1, LANES), 1)
    weights = jnp.zeros((1, LANES), jnp.float32)
    for k in range(len(DIRECTIONS)):
        code = code_ref[0, 0, k]
        weight = jnp.float32(0)
        for c in range(tapers):
            weight = jnp.where(code == c + 1, taper_ref[c], weight)
        weights = jnp.where(lane == k, weight, weights)
    high, middle, _ = in_three(weights)
    here = 0
    copies = []
    for device, k, core, low in plan.owners():
        if low % share == 0 and core == 0:
            fetch(low // share).wait()
        while here < low + 2:
            wide_ref[here * plan.members : (here + 1) * plan.members, :] = near_ref[here].astype(jnp.float32)
            here += 1
        count, other = plan.low_rows(k), plan.rows - plan.low_rows(k)
        start = low * plan.members + k * plan.step + core * count
        after = (low + 1) * plan.members + core * other
        for half in range(2):
            lanes = slice(half * LANES, (half + 1) * LANES)
            pieces = [wide_ref[start : start + count, lanes], wide_ref[after : after + other, lanes]]
            pieces += [part[low : low + 1, lanes] for part in forcing]
            spare = plan.block - plan.rows - 3
            if spare:
                pieces.append(jnp.zeros((spare, LANES), jnp.float32))
            sent_ref[device, half * plan.block : (half + 1) * plan.block, :] = jnp.concatenate(
                pieces, axis=0
            ).astype(jnp.bfloat16)
        pieces = [part[low + 1 : low + 2, :LANES] for part in forcing]
        pieces += [part[low + 1 : low + 2, LANES:] for part in forcing]
        sent_ref[device, 2 * plan.block :, :] = jnp.concatenate(pieces + [high, middle], axis=0).astype(jnp.bfloat16)
        if k == plan.depth - 1 and core == 1:
            run = pl.ds(len(copies) * size, size)
            copies.append(pltpu.make_async_copy(sent_ref.at[run], out_ref.at[run], out_sem.at[len(copies)]))
            copies[-1].start()
    for copy in copies:
        copy.wait()


def build_maps(side, kernel_ref, lt_ref, by_lat_ref, turned_ref):
    span = 4 * side - 1
    wide = (span + 1) * side
    square = (lax.broadcasted_iota(jnp.int32, (span, span), 0)
              == lax.broadcasted_iota(jnp.int32, (span, span), 1))
    table = kernel_ref[...].astype(jnp.bfloat16)
    flipped = lax.dot_general(
        square.astype(jnp.float32).astype(jnp.bfloat16), table, (((1,), (1,)), ((), ())),
        preferred_element_type=jnp.float32,
    ).astype(jnp.bfloat16)
    block = lax.broadcasted_iota(jnp.int32, (span, wide), 1) // side
    pick = (lax.broadcasted_iota(jnp.int32, (span, wide), 0) == span - 1 - block)
    by_lat_ref[...] = jnp.dot(
        flipped, pick.astype(jnp.float32).astype(jnp.bfloat16), preferred_element_type=jnp.float32
    )
    lane = lax.broadcasted_iota(jnp.int32, (3 * side, wide), 1) % side
    base = jnp.zeros((3 * side, wide), jnp.float32)
    for x in range(side):
        base = jnp.where(lane == x, by_lat_ref[side - 1 - x : 4 * side - 1 - x, :], base)
    turns = LANES // side
    for turn in range(turns):
        moved = base if turn == 0 else pltpu.roll(base, wide - turn * side, 1)
        turned_ref[turn] = moved.astype(jnp.bfloat16)
    for k, (p, q) in enumerate(ALL_STEPS):
        for y in range(side):
            start = (2 * side - 1 - p * side - y) * side
            turn, first = (start % LANES) // side, start // LANES * LANES
            lt_ref[k, y * side : (y + 1) * side, :] = turned_ref[
                turn, (q + 1) * side : (q + 2) * side, first : first + side * side
            ]


def read_extra(plan, got_ref, wide_ref):
    first = plan.rows // 16 * 16
    at = plan.rows - first
    tail = got_ref[:, 2 * plan.block :, :].astype(jnp.float32)
    weights = tail[:, 6, :] + tail[:, 7, :]
    for k in range(len(DIRECTIONS)):
        wide_ref[k] = jnp.broadcast_to(weights[:, k : k + 1], (plan.count, plan.columns))
    low, high = [], []
    for half in range(2):
        slab = got_ref[:, half * plan.block + first : (half + 1) * plan.block, :].astype(jnp.float32)
        low.append(slab[:, at, :] + slab[:, at + 1, :] + slab[:, at + 2, :])
        high.append(tail[:, 3 * half, :] + tail[:, 3 * half + 1, :] + tail[:, 3 * half + 2, :])
    return [jnp.concatenate(low, axis=1), jnp.concatenate(high, axis=1)]


def apply_rows(plan, low, order, got_ref, v_ref, lt_ref, wide_ref, w_ref, s_ref, p_ref):
    bands, lons, rows = plan.bands, plan.lons, plan.block
    place = lax.broadcasted_iota(jnp.int32, (rows, LANES), 0)
    is_low = place < low
    sides = [slice(half * LANES, (half + 1) * LANES) for half in range(2)]

    def block(tile, half):
        return got_ref[tile, half * rows : (half + 1) * rows, :].astype(jnp.float32)

    for tile in range(plan.count):
        v_low, v_high = v_ref[0, tile : tile + 1, :], v_ref[1, tile : tile + 1, :]
        for half, lanes in enumerate(sides):
            v = jnp.where(is_low, v_low[:, lanes], v_high[:, lanes])
            w_ref[tile * rows : (tile + 1) * rows, lanes] = (block(tile, half) * v).astype(jnp.bfloat16)

    scale = jnp.float32(1.0 / (plan.members - 1))
    low_share = jnp.where(is_low, scale, jnp.float32(0))
    high_share = jnp.where(is_low | (place >= plan.rows), jnp.float32(0), scale)
    low_end = min(-(-plan.low_rows(0) // GRAIN) * GRAIN, rows)
    sums = {}

    def finish(tile, spread):
        for half, lanes in enumerate(sides):
            product = block(tile, half) * spread[:, lanes]
            sums[tile, 0, half] = jnp.sum(product[:low_end] * low_share[:low_end], axis=0, keepdims=True)
            sums[tile, 1, half] = jnp.sum(product * high_share, axis=0, keepdims=True)

    touched = set()
    steps = sorted(ALL_STEPS, key=lambda step: (step[0] == 0, step == (0, 0)))
    for start in range(0, bands, CHUNK):
        stop = min(start + CHUNK, bands)
        for p, q in steps:
            first, last = max(0, start + p), min(bands, stop + p)
            if first >= last:
                continue
            k = ALL_STEPS.index((p, q))
            y = jnp.dot(
                w_ref[first * lons * rows : last * lons * rows, :], lt_ref[k], preferred_element_type=jnp.float32
            )
            for band in range(first, last):
                for l in range(lons):
                    tile = (band - p) * lons + (l - q) % lons
                    at = ((band - first) * lons + l) * rows
                    term = y[at : at + rows]
                    if k == 0:
                        finish(tile, s_ref[tile] + term)
                        continue
                    term = term * wide_ref[k - 1, tile : tile + 1, :]
                    if tile in touched:
                        s_ref[tile] += term
                    else:
                        s_ref[tile] = term
                        touched.add(tile)
                if k == 0:
                    for level in range(2):
                        for half, lanes in enumerate(sides):
                            p_ref[order[level], band, :, lanes] = jnp.concatenate(
                                [sums[band * lons + l, level, half] for l in range(lons)], axis=0
                            )


def first_kernel(plan, info_ref, got_ref, lt_ref, p_ref, v_ref, wide_ref, w_ref, s_ref):
    v_ref[0], v_ref[1] = read_extra(plan, got_ref, wide_ref)
    order = (info_ref[1], 1 - info_ref[1])
    apply_rows(plan, info_ref[0], order, got_ref, v_ref, lt_ref, wide_ref, w_ref, s_ref, p_ref)


def total(x):
    return jnp.sum(jnp.sum(x, axis=1, keepdims=True), axis=0, keepdims=True)


def second_kernel(plan, info_ref, got_ref, lt_ref, b_ref, wide_ref, own_ref, other_ref, far_ref, far_other_ref,
                  out_ref, v_ref, w_ref, s_ref, p_ref):
    mine = (own_ref[0] + other_ref[1]) + jnp.where(info_ref[6] > 0, far_other_ref[...], 0.0)
    rest = (own_ref[1] + other_ref[0]) + jnp.where(info_ref[5] > 0, far_ref[...], 0.0)
    first_core = info_ref[1] == 0
    images = (jnp.where(first_core, mine, rest), jnp.where(first_core, rest, mine))
    lane = lax.broadcasted_iota(jnp.int32, (1, LANES), 1)
    first = jnp.zeros((1, LANES), jnp.float32)
    for level in range(2):
        b = b_ref[level]
        u = images[level]
        bb, bu = total(b * b), total(b * u)
        ratio = jnp.where(bb > 0, bu / jnp.where(bb > 0, bb, 1.0), 0.0)
        q = ratio * b - u
        v_ref[level] = q
        values = (bb, total(b * q), total(q * q), ratio)
        speaks = jnp.where(info_ref[2 + level] > 0, jnp.float32(1), jnp.float32(0))
        for n, value in enumerate(values):
            at = lane == info_ref[4] + level + SLOT * n
            first = first + jnp.where(at, value, 0.0) * speaks
    apply_rows(plan, info_ref[0], (0, 1), got_ref, v_ref, lt_ref, wide_ref, w_ref, s_ref, p_ref)
    second = jnp.zeros((1, LANES), jnp.float32)
    for level in range(2):
        b = b_ref[level]
        t = p_ref[level].reshape(plan.count, plan.columns)
        for n, value in enumerate((total(v_ref[level] * t), total(b * t))):
            at = lane == info_ref[4] + level + SLOT * n
            second = second + jnp.where(at, value, 0.0)
    for half in range(2):
        lanes = slice(half * LANES, (half + 1) * LANES)
        out_ref[:, half, :] = mine[:, lanes]
        for level in range(2):
            share = p_ref[level, :, :, lanes].reshape(plan.count, LANES)
            out_ref[:, 2 + 2 * level + half, :] = share
    out_ref[:, 6, :] = jnp.broadcast_to(first, (plan.count, LANES))
    out_ref[:, 7, :] = jnp.broadcast_to(second, (plan.count, LANES))


def last_kernel(plan, f_ref, got_ref, inc_ref, res_ref, u_ref, t_ref):
    depth = plan.depth
    for level in range(plan.levels):
        group, j = divmod(level, depth + 1)
        speaker = plan.device(group, j, 0) if j < depth else plan.device(group, depth - 1, 1)
        for half in range(2):
            lanes = slice(half * LANES, (half + 1) * LANES)
            u_ref[level : level + 1, lanes] = got_ref[speaker, half : half + 1, :]
            t = None
            for core in range(2):
                for part in (0, 1):
                    k = j - part
                    if 0 <= k < depth:
                        row = 2 + 2 * part + half
                        term = got_ref[plan.device(group, k, core), row : row + 1, :]
                        t = term if t is None else t + term
            t_ref[level : level + 1, lanes] = t
    firsts = jnp.zeros((1, LANES), jnp.float32)
    seconds = jnp.zeros((1, LANES), jnp.float32)
    for device, _, _, _ in plan.owners():
        firsts = firsts + got_ref[device, 6:7, :]
        seconds = seconds + got_ref[device, 7:8, :]
    lane = lax.broadcasted_iota(jnp.int32, (1, LANES), 1)
    kept = lane < plan.levels

    def slot(row, n):
        moved = row if n == 0 else pltpu.roll(row, LANES - SLOT * n, 1)
        return jnp.where(kept, moved, 0.0)

    bb, bq, qq, ratio = (slot(firsts, n) for n in range(4))
    qt, bt = (slot(seconds, n) for n in range(2))

    def add(x):
        return jnp.sum(x, axis=1, keepdims=True)

    all_bb = add(bb)
    all_bu = add(ratio * bb - bq)
    whole = all_bu / all_bb
    shift = jnp.where(kept, whole - ratio, 0.0)
    q_q = add(shift * shift * bb + 2 * shift * bq + qq)
    q_bq = add(shift * shift * ratio * bb - shift * shift * bq + shift * bt
               + shift * ratio * bq - shift * qq + qt)
    b_bq = add(shift * ratio * bb - shift * bq + bt)
    q_u = add(shift * ratio * bb - shift * bq + ratio * bq - qq)
    energy = all_bb + all_bu
    step_0 = all_bb / energy
    norm_1 = step_0 * step_0 * q_q
    turn = norm_1 / all_bb
    curve = (step_0 * step_0 * (q_q + q_bq) + turn * step_0 * (q_u + b_bq) + turn * turn * energy)
    step_1 = norm_1 / curve

    rows = lax.broadcasted_iota(jnp.int32, (plan.levels, LANES), 0)
    diagonal = rows == lax.broadcasted_iota(jnp.int32, (plan.levels, LANES), 1)
    ratio_c = add(jnp.where(diagonal, ratio, 0.0))
    shift_c = add(jnp.where(diagonal, shift, 0.0))
    b, u, t = f_ref[:, 0, :], u_ref[...], t_ref[...]
    q = shift_c * b + (ratio_c * b - u)
    b_of_q = shift_c * u + t
    direction = step_0 * q + turn * b
    inc_ref[:, 0, :] = step_0 * b + step_1 * direction
    res_ref[:, 0, :] = step_0 * q - step_1 * (step_0 * (q + b_of_q) + turn * (b + u))


def room(mib):
    return pltpu.CompilerParams(vmem_limit_bytes=mib << 20)


def vmem():
    return pl.BlockSpec(memory_space=pltpu.VMEM)


def smem():
    return pl.BlockSpec(memory_space=pltpu.SMEM)


def by_levels(plan, anomalies, forcing, pair_code, kernel, tile_taper):
    axes = ("band", "tile")
    bf16, f32 = jnp.bfloat16, jnp.float32
    n, rows, columns = plan.count, plan.block, plan.columns
    side = (kernel.shape[0] + 1) // 4
    wide = 4 * side * side
    a, f = anomalies[0, 0], jnp.swapaxes(forcing[0], 0, 1)
    sent = pl.pallas_call(
        functools.partial(pack_kernel, plan, tile_taper.shape[0]),
        out_shape=jax.ShapeDtypeStruct((n, plan.height, LANES), bf16),
        in_specs=[pl.BlockSpec(memory_space=pl.ANY)] * 4,
        out_specs=pl.BlockSpec(memory_space=pl.ANY),
        scratch_shapes=[pltpu.SMEM(pair_code.shape, jnp.int32),
                        pltpu.SMEM(tile_taper.shape, f32),
                        pltpu.VMEM(f.shape, f32),
                        pltpu.VMEM(a.shape, bf16),
                        pltpu.VMEM((plan.levels * plan.members, columns), f32),
                        pltpu.VMEM((n, plan.height, LANES), bf16),
                        pltpu.SemaphoreType.DMA((3,)),
                        pltpu.SemaphoreType.DMA((plan.groups,)),
                        pltpu.SemaphoreType.DMA((plan.groups,))],
        name="pack",
    )(pair_code, tile_taper, a, f)
    got = lax.all_to_all(sent, axes, 0, 0)
    me = lax.axis_index(axes)
    info = lax.dynamic_slice(jnp.asarray(plan.table()), (me, 0), (1, 8))[0]
    both = jax.ShapeDtypeStruct((2, n, columns), f32)
    shares = jax.ShapeDtypeStruct((2, plan.bands, plan.lons, columns), f32)
    weights = jax.ShapeDtypeStruct((len(DIRECTIONS), n, columns), f32)
    work = [pltpu.VMEM((n * rows, columns), bf16), pltpu.VMEM((n, rows, columns), f32)]
    maps = pl.pallas_call(
        functools.partial(build_maps, side),
        out_shape=jax.ShapeDtypeStruct((len(ALL_STEPS), columns, columns), bf16),
        in_specs=[vmem()],
        out_specs=vmem(),
        scratch_shapes=[pltpu.VMEM((4 * side - 1, wide), f32),
                        pltpu.VMEM((LANES // side, 3 * side, wide), bf16)],
        cost_estimate=pl.CostEstimate(flops=200_000_000, bytes_accessed=2_000_000, transcendentals=0),
        compiler_params=room(12),
        name="maps",
    )(kernel)
    part, b, wide_weights = pl.pallas_call(
        functools.partial(first_kernel, plan),
        out_shape=(shares, both, weights),
        in_specs=[smem(), vmem(), vmem()],
        out_specs=(vmem(),) * 3,
        scratch_shapes=work,
        compiler_params=room(20),
        name="first",
    )(info, got, maps)
    part = part.reshape(2, n, columns)
    swap = [(i, i ^ 1) for i in range(plan.lons)]
    other = lax.ppermute(part, "tile", swap)
    far = lax.ppermute(part[0] + other[1], axes, plan.outward())
    far_other = lax.ppermute(far, "tile", swap)
    back = pl.pallas_call(
        functools.partial(second_kernel, plan),
        out_shape=jax.ShapeDtypeStruct((n, 8, LANES), f32),
        in_specs=[smem()] + [vmem()] * 8,
        out_specs=vmem(),
        scratch_shapes=[pltpu.VMEM(both.shape, f32)] + work + [pltpu.VMEM(shares.shape, f32)],
        compiler_params=room(20),
        name="second",
    )(info, got, maps, b, wide_weights, part, other, far, far_other)
    home = lax.all_to_all(back, axes, 0, 0)
    increment, residual = pl.pallas_call(
        functools.partial(last_kernel, plan),
        out_shape=(jax.ShapeDtypeStruct(f.shape, f32),) * 2,
        in_specs=[vmem(), vmem()],
        out_specs=(vmem(), vmem()),
        scratch_shapes=[pltpu.VMEM((plan.levels, columns), f32)] * 2,
        compiler_params=room(8),
        name="last",
    )(f, home)
    return jnp.swapaxes(increment, 0, 1)[None], jnp.swapaxes(residual, 0, 1)[None]


def padded(block, sides, width):
    for axis, dim in sides:
        count = lax.axis_size(axis)
        forward = [(i, i + 1) for i in range(count - 1)]
        forward.append((count - 1, 0))
        backward = [(target, source) for source, target in forward]
        low = lax.ppermute(
            lax.slice_in_dim(block, block.shape[dim] - width, None, axis=dim), axis, forward
        )
        high = lax.ppermute(lax.slice_in_dim(block, 0, width, axis=dim), axis, backward)
        block = jnp.concatenate([low, block, high], axis=dim)
    return block


def selector(tile_side, offset):
    first_index = np.arange(tile_side)[:, None]
    second_index = np.arange(tile_side)[None, :]
    target = 2 * tile_side - 1 + offset * tile_side + second_index - first_index
    return (np.arange(4 * tile_side - 1)[None, None, :] == target[:, :, None]).astype(np.float32)


def local_map(kernel, row_step, col_step):
    by_lat = jnp.einsum(
        "abp,pq->abq", selector(SIDE, row_step), kernel, precision=lax.Precision.HIGHEST
    )
    full_map = jnp.einsum(
        "abq,cdq->acbd", by_lat, selector(SIDE, col_step), precision=lax.Precision.HIGHEST
    )
    return full_map.reshape(SIDE * SIDE, SIDE * SIDE).astype(jnp.bfloat16)


def all_maps(kernel):
    return [local_map(kernel, 0, 0)] + [
        local_map(kernel, row_step, col_step) for row_step, col_step in DIRECTIONS
    ]


def taper_lookup(tile_taper, code):
    entries = jnp.arange(1, tile_taper.shape[0] + 1, dtype=jnp.int32)
    return jnp.sum(jnp.where(entries == code, tile_taper, jnp.zeros_like(tile_taper)))


def weighted_block(block, field):
    return (block.astype(jnp.float32) * field[:, None, :]).astype(jnp.bfloat16)


def pair_term(own_block, weighted, matrix, weight):
    levels, members, columns = weighted.shape
    spread = lax.dot_general(
        weighted.reshape(levels * members, columns),
        matrix,
        (((1,), (1,)), ((), ())),
        preferred_element_type=jnp.float32,
    )
    summed = jnp.sum(
        own_block.astype(jnp.float32) * spread.reshape(levels, members, columns), axis=1
    )
    return summed * (weight / (members - 1))


def masked_term(code, weight, own_block, weighted, matrix):

    def active():
        return pair_term(own_block, weighted, matrix, weight)

    def inactive():
        return jnp.zeros((weighted.shape[0], weighted.shape[2]), jnp.float32)

    return lax.cond(code > 0, active, inactive)


def covariance_all(blocks, neighbours, pair_codes, tile_taper, local_maps):
    own_block = blocks[1, 1]
    summed_terms = pair_term(
        own_block, weighted_block(own_block, neighbours[1, 1]), local_maps[0], 1.0
    )
    for position, (row_step, col_step) in enumerate(DIRECTIONS):
        code = pair_codes[position]
        weight = taper_lookup(tile_taper, code)
        other_weighted = weighted_block(
            blocks[1 + row_step, 1 + col_step], neighbours[1 + row_step, 1 + col_step]
        )
        summed_terms = summed_terms + masked_term(
            code, weight, own_block, other_weighted, local_maps[position + 1]
        )
    return summed_terms


def global_total(factor_one, factor_two):
    return lax.psum(jnp.sum(factor_one * factor_two), ("band", "tile"))


def on_device(anomalies, forcing, pair_code, kernel, tile_taper):
    pair_codes = pair_code[0, 0]
    kept_maps = all_maps(kernel)
    residual = forcing[0, 0]
    increment = jnp.zeros_like(residual)
    direction = residual
    norm_now = global_total(residual, residual)
    for iteration in range(ITERS):
        blocks = padded(anomalies, (("band", 0), ("tile", 1)), 1)
        neighbours = padded(direction[None, None], (("band", 0), ("tile", 1)), 1)
        mapped = direction + covariance_all(blocks, neighbours, pair_codes, tile_taper, kept_maps)
        step_length = norm_now / global_total(direction, mapped)
        increment = increment + step_length * direction
        residual = residual - step_length * mapped
        norm_next = global_total(residual, residual)
        direction = residual + norm_next / norm_now * direction
        norm_now = norm_next
    return (increment[None, None], residual[None, None])


def solution(mesh):
    specs = (
        P("band", "tile", None, None, None),
        P("band", "tile", None, None),
        P("band", "tile", None),
        P(),
        P(),
    )

    def run(anomalies, forcing, pair_code, kernel, tile_taper):
        plan = Plan(mesh.shape["band"], mesh.shape["tile"], *anomalies.shape[2:])
        step = functools.partial(by_levels, plan) if plan.fits else on_device
        return step(anomalies, forcing, pair_code, kernel, tile_taper)

    return jax.shard_map(
        run,
        mesh=mesh,
        in_specs=specs,
        out_specs=(P("band", "tile", None, None), P("band", "tile", None, None)),
        check_vma=False,
    )
```

```python
import functools

import jax
import jax.numpy as jnp
import numpy as np
from jax import lax
from jax.experimental import pallas as pl
from jax.experimental.pallas import tpu as pltpu
from jax.sharding import PartitionSpec as P

SIDE = 16
ITERS = 2
GRAIN = 8
LANES = 128
SLOT = 32
CHUNK = 1

DIRECTIONS = ((-1, -1), (-1, 0), (-1, 1), (0, -1), (0, 1), (1, -1), (1, 0), (1, 1))
ALL_STEPS = ((0, 0),) + DIRECTIONS


class Plan:
    def __init__(self, bands, lons, levels, members, columns):
        self.bands, self.lons = bands, lons
        self.levels, self.members, self.columns = levels, members, columns
        self.count = bands * lons
        self.rows = levels * members // self.count
        self.step = 2 * self.rows - members
        self.fits = (
            levels * members % self.count == 0
            and members % 2 == 0
            and 0 < self.step < members
            and members % self.step == 0
            and levels <= SLOT
            and lons % GRAIN == 0
            and columns == 2 * LANES
        )
        if not self.fits:
            return
        self.depth = members // self.step
        self.fits = levels % (self.depth + 1) == 0
        if not self.fits:
            return
        self.groups = levels // (self.depth + 1)
        across = lons // 2
        inner = [i ^ (i >> 1) for i in range(across)]
        if sorted(inner) != list(range(across)):
            inner = list(range(across))
        path = []
        for band in range(bands):
            path += [band * across + c for c in (inner if band % 2 == 0 else inner[::-1])]
        self.path = path
        self.block = -(-(self.rows + 3) // 16) * 16
        self.height = 2 * self.block + GRAIN

    def low_rows(self, k):
        return (self.members - k * self.step) // 2

    def device(self, group, k, core):
        return 2 * self.path[group * self.depth + k] + core

    def owners(self):
        for group in range(self.groups):
            for k in range(self.depth):
                for core in range(2):
                    low = group * (self.depth + 1) + k
                    yield self.device(group, k, core), k, core, low

    def table(self):
        out = np.zeros((self.count, 8), np.int32)
        for device, k, core, low in self.owners():
            last = k == self.depth - 1
            joined = (int(not last), int(k > 0))
            out[device, :5] = (self.low_rows(k), core, int(core == 0), int(core == 1 and last), low)
            out[device, 5:7] = (joined[core], joined[1 - core])
        return out

    def outward(self):
        pairs = []
        for group in range(self.groups):
            for k in range(self.depth):
                pairs.append((self.device(group, k, 0), self.device(group, (k - 1) % self.depth, 0)))
                pairs.append((self.device(group, k, 1), self.device(group, (k + 1) % self.depth, 1)))
        return pairs


def in_three(x):
    high = x.astype(jnp.bfloat16).astype(jnp.float32)
    rest = x - high
    middle = rest.astype(jnp.bfloat16).astype(jnp.float32)
    return [high, middle, rest - middle]


def pack_kernel(plan, tapers, code_hbm, taper_hbm, a_ref, f_hbm, out_ref,
                code_ref, taper_ref, f_ref, near_ref, wide_ref, sent_ref, small_sem, in_sem, out_sem):
    share, size = plan.depth + 1, plan.count // plan.groups

    def fetch(group):
        run = pl.ds(group * share, share)
        return pltpu.make_async_copy(a_ref.at[run], near_ref.at[run], in_sem.at[group])

    small = [
        pltpu.make_async_copy(source, target, small_sem.at[n])
        for n, (source, target) in enumerate(((code_hbm, code_ref), (taper_hbm, taper_ref), (f_hbm, f_ref)))
    ]
    for copy in small:
        copy.start()
    for group in range(plan.groups):
        fetch(group).start()
    for copy in small:
        copy.wait()
    forcing = in_three(f_ref[:, 0, :])
    lane = lax.broadcasted_iota(jnp.int32, (1, LANES), 1)
    weights = jnp.zeros((1, LANES), jnp.float32)
    for k in range(len(DIRECTIONS)):
        code = code_ref[0, 0, k]
        weight = jnp.float32(0)
        for c in range(tapers):
            weight = jnp.where(code == c + 1, taper_ref[c], weight)
        weights = jnp.where(lane == k, weight, weights)
    high, middle, _ = in_three(weights)
    here = 0
    copies = []
    for device, k, core, low in plan.owners():
        if low % share == 0 and core == 0:
            fetch(low // share).wait()
        while here < low + 2:
            wide_ref[here * plan.members : (here + 1) * plan.members, :] = near_ref[here].astype(jnp.float32)
            here += 1
        count, other = plan.low_rows(k), plan.rows - plan.low_rows(k)
        start = low * plan.members + k * plan.step + core * count
        after = (low + 1) * plan.members + core * other
        for half in range(2):
            lanes = slice(half * LANES, (half + 1) * LANES)
            pieces = [wide_ref[start : start + count, lanes], wide_ref[after : after + other, lanes]]
            pieces += [part[low : low + 1, lanes] for part in forcing]
            spare = plan.block - plan.rows - 3
            if spare:
                pieces.append(jnp.zeros((spare, LANES), jnp.float32))
            sent_ref[device, half * plan.block : (half + 1) * plan.block, :] = jnp.concatenate(
                pieces, axis=0
            ).astype(jnp.bfloat16)
        pieces = [part[low + 1 : low + 2, :LANES] for part in forcing]
        pieces += [part[low + 1 : low + 2, LANES:] for part in forcing]
        sent_ref[device, 2 * plan.block :, :] = jnp.concatenate(pieces + [high, middle], axis=0).astype(jnp.bfloat16)
        if k == plan.depth - 1 and core == 1:
            run = pl.ds(len(copies) * size, size)
            copies.append(pltpu.make_async_copy(sent_ref.at[run], out_ref.at[run], out_sem.at[len(copies)]))
            copies[-1].start()
    for copy in copies:
        copy.wait()


def build_maps(side, kernel_ref, lt_ref, by_lat_ref, turned_ref):
    span = 4 * side - 1
    wide = (span + 1) * side
    square = (lax.broadcasted_iota(jnp.int32, (span, span), 0)
              == lax.broadcasted_iota(jnp.int32, (span, span), 1))
    table = kernel_ref[...].astype(jnp.bfloat16)
    flipped = lax.dot_general(
        square.astype(jnp.float32).astype(jnp.bfloat16), table, (((1,), (1,)), ((), ())),
        preferred_element_type=jnp.float32,
    ).astype(jnp.bfloat16)
    block = lax.broadcasted_iota(jnp.int32, (span, wide), 1) // side
    pick = (lax.broadcasted_iota(jnp.int32, (span, wide), 0) == span - 1 - block)
    by_lat_ref[...] = jnp.dot(
        flipped, pick.astype(jnp.float32).astype(jnp.bfloat16), preferred_element_type=jnp.float32
    )
    lane = lax.broadcasted_iota(jnp.int32, (3 * side, wide), 1) % side
    base = jnp.zeros((3 * side, wide), jnp.float32)
    for x in range(side):
        base = jnp.where(lane == x, by_lat_ref[side - 1 - x : 4 * side - 1 - x, :], base)
    turns = LANES // side
    for turn in range(turns):
        moved = base if turn == 0 else pltpu.roll(base, wide - turn * side, 1)
        turned_ref[turn] = moved.astype(jnp.bfloat16)
    for k, (p, q) in enumerate(ALL_STEPS):
        for y in range(side):
            start = (2 * side - 1 - p * side - y) * side
            turn, first = (start % LANES) // side, start // LANES * LANES
            lt_ref[k, y * side : (y + 1) * side, :] = turned_ref[
                turn, (q + 1) * side : (q + 2) * side, first : first + side * side
            ]


def read_extra(plan, got_ref, wide_ref):
    first = plan.rows // 16 * 16
    at = plan.rows - first
    tail = got_ref[:, 2 * plan.block :, :].astype(jnp.float32)
    weights = tail[:, 6, :] + tail[:, 7, :]
    for k in range(len(DIRECTIONS)):
        wide_ref[k] = jnp.broadcast_to(weights[:, k : k + 1], (plan.count, plan.columns))
    low, high = [], []
    for half in range(2):
        slab = got_ref[:, half * plan.block + first : (half + 1) * plan.block, :].astype(jnp.float32)
        low.append(slab[:, at, :] + slab[:, at + 1, :] + slab[:, at + 2, :])
        high.append(tail[:, 3 * half, :] + tail[:, 3 * half + 1, :] + tail[:, 3 * half + 2, :])
    return [jnp.concatenate(low, axis=1), jnp.concatenate(high, axis=1)]


def apply_rows(plan, low, order, got_ref, v_ref, lt_ref, wide_ref, w_ref, s_ref, p_ref):
    bands, lons, rows = plan.bands, plan.lons, plan.block
    place = lax.broadcasted_iota(jnp.int32, (rows, LANES), 0)
    is_low = place < low
    sides = [slice(half * LANES, (half + 1) * LANES) for half in range(2)]

    def block(tile, half):
        return got_ref[tile, half * rows : (half + 1) * rows, :].astype(jnp.float32)

    for tile in range(plan.count):
        v_low, v_high = v_ref[0, tile : tile + 1, :], v_ref[1, tile : tile + 1, :]
        for half, lanes in enumerate(sides):
            v = jnp.where(is_low, v_low[:, lanes], v_high[:, lanes])
            w_ref[tile * rows : (tile + 1) * rows, lanes] = (block(tile, half) * v).astype(jnp.bfloat16)

    scale = jnp.float32(1.0 / (plan.members - 1))
    low_share = jnp.where(is_low, scale, jnp.float32(0))
    high_share = jnp.where(is_low | (place >= plan.rows), jnp.float32(0), scale)
    low_end = min(-(-plan.low_rows(0) // GRAIN) * GRAIN, rows)
    sums = {}

    def finish(tile, spread):
        for half, lanes in enumerate(sides):
            product = block(tile, half) * spread[:, lanes]
            sums[tile, 0, half] = jnp.sum(product[:low_end] * low_share[:low_end], axis=0, keepdims=True)
            sums[tile, 1, half] = jnp.sum(product * high_share, axis=0, keepdims=True)

    touched = set()
    steps = sorted(ALL_STEPS, key=lambda step: (step[0] == 0, step == (0, 0)))
    for start in range(0, bands, CHUNK):
        stop = min(start + CHUNK, bands)
        for p, q in steps:
            first, last = max(0, start + p), min(bands, stop + p)
            if first >= last:
                continue
            k = ALL_STEPS.index((p, q))
            y = jnp.dot(
                w_ref[first * lons * rows : last * lons * rows, :], lt_ref[k], preferred_element_type=jnp.float32
            )
            for band in range(first, last):
                for l in range(lons):
                    tile = (band - p) * lons + (l - q) % lons
                    at = ((band - first) * lons + l) * rows
                    term = y[at : at + rows]
                    if k == 0:
                        finish(tile, s_ref[tile] + term)
                        continue
                    term = term * wide_ref[k - 1, tile : tile + 1, :]
                    if tile in touched:
                        s_ref[tile] += term
                    else:
                        s_ref[tile] = term
                        touched.add(tile)
                if k == 0:
                    for level in range(2):
                        for half, lanes in enumerate(sides):
                            p_ref[order[level], band, :, lanes] = jnp.concatenate(
                                [sums[band * lons + l, level, half] for l in range(lons)], axis=0
                            )


def first_kernel(plan, info_ref, got_ref, lt_ref, p_ref, v_ref, wide_ref, w_ref, s_ref):
    v_ref[0], v_ref[1] = read_extra(plan, got_ref, wide_ref)
    order = (info_ref[1], 1 - info_ref[1])
    apply_rows(plan, info_ref[0], order, got_ref, v_ref, lt_ref, wide_ref, w_ref, s_ref, p_ref)


def total(x):
    return jnp.sum(jnp.sum(x, axis=1, keepdims=True), axis=0, keepdims=True)


def second_kernel(plan, info_ref, got_ref, lt_ref, b_ref, wide_ref, own_ref, other_ref, far_ref, far_other_ref,
                  out_ref, v_ref, w_ref, s_ref, p_ref):
    mine = (own_ref[0] + other_ref[1]) + jnp.where(info_ref[6] > 0, far_other_ref[...], 0.0)
    rest = (own_ref[1] + other_ref[0]) + jnp.where(info_ref[5] > 0, far_ref[...], 0.0)
    first_core = info_ref[1] == 0
    images = (jnp.where(first_core, mine, rest), jnp.where(first_core, rest, mine))
    lane = lax.broadcasted_iota(jnp.int32, (1, LANES), 1)
    first = jnp.zeros((1, LANES), jnp.float32)
    for level in range(2):
        b = b_ref[level]
        u = images[level]
        bb, bu = total(b * b), total(b * u)
        ratio = jnp.where(bb > 0, bu / jnp.where(bb > 0, bb, 1.0), 0.0)
        q = ratio * b - u
        v_ref[level] = q
        values = (bb, total(b * q), total(q * q), ratio)
        speaks = jnp.where(info_ref[2 + level] > 0, jnp.float32(1), jnp.float32(0))
        for n, value in enumerate(values):
            at = lane == info_ref[4] + level + SLOT * n
            first = first + jnp.where(at, value, 0.0) * speaks
    apply_rows(plan, info_ref[0], (0, 1), got_ref, v_ref, lt_ref, wide_ref, w_ref, s_ref, p_ref)
    second = jnp.zeros((1, LANES), jnp.float32)
    for level in range(2):
        b = b_ref[level]
        t = p_ref[level].reshape(plan.count, plan.columns)
        for n, value in enumerate((total(v_ref[level] * t), total(b * t))):
            at = lane == info_ref[4] + level + SLOT * n
            second = second + jnp.where(at, value, 0.0)
    for half in range(2):
        lanes = slice(half * LANES, (half + 1) * LANES)
        out_ref[:, half, :] = mine[:, lanes]
        for level in range(2):
            share = p_ref[level, :, :, lanes].reshape(plan.count, LANES)
            out_ref[:, 2 + 2 * level + half, :] = share
    out_ref[:, 6, :] = jnp.broadcast_to(first, (plan.count, LANES))
    out_ref[:, 7, :] = jnp.broadcast_to(second, (plan.count, LANES))


def last_kernel(plan, f_ref, got_ref, inc_ref, res_ref, u_ref, t_ref):
    depth = plan.depth
    for level in range(plan.levels):
        group, j = divmod(level, depth + 1)
        speaker = plan.device(group, j, 0) if j < depth else plan.device(group, depth - 1, 1)
        for half in range(2):
            lanes = slice(half * LANES, (half + 1) * LANES)
            u_ref[level : level + 1, lanes] = got_ref[speaker, half : half + 1, :]
            t = None
            for core in range(2):
                for part in (0, 1):
                    k = j - part
                    if 0 <= k < depth:
                        row = 2 + 2 * part + half
                        term = got_ref[plan.device(group, k, core), row : row + 1, :]
                        t = term if t is None else t + term
            t_ref[level : level + 1, lanes] = t
    firsts = jnp.zeros((1, LANES), jnp.float32)
    seconds = jnp.zeros((1, LANES), jnp.float32)
    for device, _, _, _ in plan.owners():
        firsts = firsts + got_ref[device, 6:7, :]
        seconds = seconds + got_ref[device, 7:8, :]
    lane = lax.broadcasted_iota(jnp.int32, (1, LANES), 1)
    kept = lane < plan.levels

    def slot(row, n):
        moved = row if n == 0 else pltpu.roll(row, LANES - SLOT * n, 1)
        return jnp.where(kept, moved, 0.0)

    bb, bq, qq, ratio = (slot(firsts, n) for n in range(4))
    qt, bt = (slot(seconds, n) for n in range(2))

    def add(x):
        return jnp.sum(x, axis=1, keepdims=True)

    all_bb = add(bb)
    all_bu = add(ratio * bb - bq)
    whole = all_bu / all_bb
    shift = jnp.where(kept, whole - ratio, 0.0)
    q_q = add(shift * shift * bb + 2 * shift * bq + qq)
    q_bq = add(shift * shift * ratio * bb - shift * shift * bq + shift * bt
               + shift * ratio * bq - shift * qq + qt)
    b_bq = add(shift * ratio * bb - shift * bq + bt)
    q_u = add(shift * ratio * bb - shift * bq + ratio * bq - qq)
    energy = all_bb + all_bu
    step_0 = all_bb / energy
    norm_1 = step_0 * step_0 * q_q
    turn = norm_1 / all_bb
    curve = (step_0 * step_0 * (q_q + q_bq) + turn * step_0 * (q_u + b_bq) + turn * turn * energy)
    step_1 = norm_1 / curve

    rows = lax.broadcasted_iota(jnp.int32, (plan.levels, LANES), 0)
    diagonal = rows == lax.broadcasted_iota(jnp.int32, (plan.levels, LANES), 1)
    ratio_c = add(jnp.where(diagonal, ratio, 0.0))
    shift_c = add(jnp.where(diagonal, shift, 0.0))
    b, u, t = f_ref[:, 0, :], u_ref[...], t_ref[...]
    q = shift_c * b + (ratio_c * b - u)
    b_of_q = shift_c * u + t
    direction = step_0 * q + turn * b
    inc_ref[:, 0, :] = step_0 * b + step_1 * direction
    res_ref[:, 0, :] = step_0 * q - step_1 * (step_0 * (q + b_of_q) + turn * (b + u))


def room(mib):
    return pltpu.CompilerParams(vmem_limit_bytes=mib << 20)


def vmem():
    return pl.BlockSpec(memory_space=pltpu.VMEM)


def smem():
    return pl.BlockSpec(memory_space=pltpu.SMEM)


def by_levels(plan, anomalies, forcing, pair_code, kernel, tile_taper):
    axes = ("band", "tile")
    bf16, f32 = jnp.bfloat16, jnp.float32
    n, rows, columns = plan.count, plan.block, plan.columns
    side = (kernel.shape[0] + 1) // 4
    wide = 4 * side * side
    a, f = anomalies[0, 0], jnp.swapaxes(forcing[0], 0, 1)
    sent = pl.pallas_call(
        functools.partial(pack_kernel, plan, tile_taper.shape[0]),
        out_shape=jax.ShapeDtypeStruct((n, plan.height, LANES), bf16),
        in_specs=[pl.BlockSpec(memory_space=pl.ANY)] * 4,
        out_specs=pl.BlockSpec(memory_space=pl.ANY),
        scratch_shapes=[pltpu.SMEM(pair_code.shape, jnp.int32),
                        pltpu.SMEM(tile_taper.shape, f32),
                        pltpu.VMEM(f.shape, f32),
                        pltpu.VMEM(a.shape, bf16),
                        pltpu.VMEM((plan.levels * plan.members, columns), f32),
                        pltpu.VMEM((n, plan.height, LANES), bf16),
                        pltpu.SemaphoreType.DMA((3,)),
                        pltpu.SemaphoreType.DMA((plan.groups,)),
                        pltpu.SemaphoreType.DMA((plan.groups,))],
        name="pack",
    )(pair_code, tile_taper, a, f)
    got = lax.all_to_all(sent, axes, 0, 0)
    me = lax.axis_index(axes)
    info = lax.dynamic_slice(jnp.asarray(plan.table()), (me, 0), (1, 8))[0]
    both = jax.ShapeDtypeStruct((2, n, columns), f32)
    shares = jax.ShapeDtypeStruct((2, plan.bands, plan.lons, columns), f32)
    weights = jax.ShapeDtypeStruct((len(DIRECTIONS), n, columns), f32)
    work = [pltpu.VMEM((n * rows, columns), bf16), pltpu.VMEM((n, rows, columns), f32)]
    maps = pl.pallas_call(
        functools.partial(build_maps, side),
        out_shape=jax.ShapeDtypeStruct((len(ALL_STEPS), columns, columns), bf16),
        in_specs=[vmem()],
        out_specs=vmem(),
        scratch_shapes=[pltpu.VMEM((4 * side - 1, wide), f32),
                        pltpu.VMEM((LANES // side, 3 * side, wide), bf16)],
        cost_estimate=pl.CostEstimate(flops=200_000_000, bytes_accessed=2_000_000, transcendentals=0),
        compiler_params=room(12),
        name="maps",
    )(kernel)
    part, b, wide_weights = pl.pallas_call(
        functools.partial(first_kernel, plan),
        out_shape=(shares, both, weights),
        in_specs=[smem(), vmem(), vmem()],
        out_specs=(vmem(),) * 3,
        scratch_shapes=work,
        compiler_params=room(20),
        name="first",
    )(info, got, maps)
    part = part.reshape(2, n, columns)
    swap = [(i, i ^ 1) for i in range(plan.lons)]
    other = lax.ppermute(part, "tile", swap)
    outward = plan.outward()
    far = lax.ppermute(part[0] + other[1], axes, outward)
    far_other = lax.ppermute(part[1] + other[0], axes, [(target, source) for source, target in outward])
    back = pl.pallas_call(
        functools.partial(second_kernel, plan),
        out_shape=jax.ShapeDtypeStruct((n, 8, LANES), f32),
        in_specs=[smem()] + [vmem()] * 8,
        out_specs=vmem(),
        scratch_shapes=[pltpu.VMEM(both.shape, f32)] + work + [pltpu.VMEM(shares.shape, f32)],
        compiler_params=room(20),
        name="second",
    )(info, got, maps, b, wide_weights, part, other, far, far_other)
    home = lax.all_to_all(back, axes, 0, 0)
    increment, residual = pl.pallas_call(
        functools.partial(last_kernel, plan),
        out_shape=(jax.ShapeDtypeStruct(f.shape, f32),) * 2,
        in_specs=[vmem(), vmem()],
        out_specs=(vmem(), vmem()),
        scratch_shapes=[pltpu.VMEM((plan.levels, columns), f32)] * 2,
        compiler_params=room(8),
        name="last",
    )(f, home)
    return jnp.swapaxes(increment, 0, 1)[None], jnp.swapaxes(residual, 0, 1)[None]


def padded(block, sides, width):
    for axis, dim in sides:
        count = lax.axis_size(axis)
        forward = [(i, i + 1) for i in range(count - 1)]
        forward.append((count - 1, 0))
        backward = [(target, source) for source, target in forward]
        low = lax.ppermute(
            lax.slice_in_dim(block, block.shape[dim] - width, None, axis=dim), axis, forward
        )
        high = lax.ppermute(lax.slice_in_dim(block, 0, width, axis=dim), axis, backward)
        block = jnp.concatenate([low, block, high], axis=dim)
    return block


def selector(tile_side, offset):
    first_index = np.arange(tile_side)[:, None]
    second_index = np.arange(tile_side)[None, :]
    target = 2 * tile_side - 1 + offset * tile_side + second_index - first_index
    return (np.arange(4 * tile_side - 1)[None, None, :] == target[:, :, None]).astype(np.float32)


def local_map(kernel, row_step, col_step):
    by_lat = jnp.einsum(
        "abp,pq->abq", selector(SIDE, row_step), kernel, precision=lax.Precision.HIGHEST
    )
    full_map = jnp.einsum(
        "abq,cdq->acbd", by_lat, selector(SIDE, col_step), precision=lax.Precision.HIGHEST
    )
    return full_map.reshape(SIDE * SIDE, SIDE * SIDE).astype(jnp.bfloat16)


def all_maps(kernel):
    return [local_map(kernel, 0, 0)] + [
        local_map(kernel, row_step, col_step) for row_step, col_step in DIRECTIONS
    ]


def taper_lookup(tile_taper, code):
    entries = jnp.arange(1, tile_taper.shape[0] + 1, dtype=jnp.int32)
    return jnp.sum(jnp.where(entries == code, tile_taper, jnp.zeros_like(tile_taper)))


def weighted_block(block, field):
    return (block.astype(jnp.float32) * field[:, None, :]).astype(jnp.bfloat16)


def pair_term(own_block, weighted, matrix, weight):
    levels, members, columns = weighted.shape
    spread = lax.dot_general(
        weighted.reshape(levels * members, columns),
        matrix,
        (((1,), (1,)), ((), ())),
        preferred_element_type=jnp.float32,
    )
    summed = jnp.sum(
        own_block.astype(jnp.float32) * spread.reshape(levels, members, columns), axis=1
    )
    return summed * (weight / (members - 1))


def masked_term(code, weight, own_block, weighted, matrix):

    def active():
        return pair_term(own_block, weighted, matrix, weight)

    def inactive():
        return jnp.zeros((weighted.shape[0], weighted.shape[2]), jnp.float32)

    return lax.cond(code > 0, active, inactive)


def covariance_all(blocks, neighbours, pair_codes, tile_taper, local_maps):
    own_block = blocks[1, 1]
    summed_terms = pair_term(
        own_block, weighted_block(own_block, neighbours[1, 1]), local_maps[0], 1.0
    )
    for position, (row_step, col_step) in enumerate(DIRECTIONS):
        code = pair_codes[position]
        weight = taper_lookup(tile_taper, code)
        other_weighted = weighted_block(
            blocks[1 + row_step, 1 + col_step], neighbours[1 + row_step, 1 + col_step]
        )
        summed_terms = summed_terms + masked_term(
            code, weight, own_block, other_weighted, local_maps[position + 1]
        )
    return summed_terms


def global_total(factor_one, factor_two):
    return lax.psum(jnp.sum(factor_one * factor_two), ("band", "tile"))


def on_device(anomalies, forcing, pair_code, kernel, tile_taper):
    pair_codes = pair_code[0, 0]
    kept_maps = all_maps(kernel)
    residual = forcing[0, 0]
    increment = jnp.zeros_like(residual)
    direction = residual
    norm_now = global_total(residual, residual)
    for iteration in range(ITERS):
        blocks = padded(anomalies, (("band", 0), ("tile", 1)), 1)
        neighbours = padded(direction[None, None], (("band", 0), ("tile", 1)), 1)
        mapped = direction + covariance_all(blocks, neighbours, pair_codes, tile_taper, kept_maps)
        step_length = norm_now / global_total(direction, mapped)
        increment = increment + step_length * direction
        residual = residual - step_length * mapped
        norm_next = global_total(residual, residual)
        direction = residual + norm_next / norm_now * direction
        norm_now = norm_next
    return (increment[None, None], residual[None, None])


def solution(mesh):
    specs = (
        P("band", "tile", None, None, None),
        P("band", "tile", None, None),
        P("band", "tile", None),
        P(),
        P(),
    )

    def run(anomalies, forcing, pair_code, kernel, tile_taper):
        plan = Plan(mesh.shape["band"], mesh.shape["tile"], *anomalies.shape[2:])
        step = functools.partial(by_levels, plan) if plan.fits else on_device
        return step(anomalies, forcing, pair_code, kernel, tile_taper)

    return jax.shard_map(
        run,
        mesh=mesh,
        in_specs=specs,
        out_specs=(P("band", "tile", None, None), P("band", "tile", None, None)),
        check_vma=False,
    )
```

```python
import functools

import jax
import jax.numpy as jnp
import numpy as np
from jax import lax
from jax.experimental import pallas as pl
from jax.experimental.pallas import tpu as pltpu
from jax.sharding import PartitionSpec as P

SIDE = 16
ITERS = 2
GRAIN = 8
LANES = 128
SLOT = 32
CHUNK = 1

DIRECTIONS = ((-1, -1), (-1, 0), (-1, 1), (0, -1), (0, 1), (1, -1), (1, 0), (1, 1))
ALL_STEPS = ((0, 0),) + DIRECTIONS


class Plan:
    def __init__(self, bands, lons, levels, members, columns):
        self.bands, self.lons = bands, lons
        self.levels, self.members, self.columns = levels, members, columns
        self.count = bands * lons
        self.rows = levels * members // self.count
        self.step = 2 * self.rows - members
        self.fits = (
            levels * members % self.count == 0
            and members % 2 == 0
            and 0 < self.step < members
            and members % self.step == 0
            and levels <= SLOT
            and lons % GRAIN == 0
            and columns == 2 * LANES
        )
        if not self.fits:
            return
        self.depth = members // self.step
        self.fits = levels % (self.depth + 1) == 0
        if not self.fits:
            return
        self.groups = levels // (self.depth + 1)
        across = lons // 2
        inner = [i ^ (i >> 1) for i in range(across)]
        if sorted(inner) != list(range(across)):
            inner = list(range(across))
        path = []
        for band in range(bands):
            path += [band * across + c for c in (inner if band % 2 == 0 else inner[::-1])]
        self.path = path
        self.block = -(-(self.rows + 3) // 16) * 16
        self.height = 2 * self.block + GRAIN

    def low_rows(self, k):
        return (self.members - k * self.step) // 2

    def device(self, group, k, core):
        return 2 * self.path[group * self.depth + k] + core

    def owners(self):
        for group in range(self.groups):
            for k in range(self.depth):
                for core in range(2):
                    low = group * (self.depth + 1) + k
                    yield self.device(group, k, core), k, core, low

    def table(self):
        out = np.zeros((self.count, 8), np.int32)
        for device, k, core, low in self.owners():
            last = k == self.depth - 1
            joined = (int(not last), int(k > 0))
            out[device, :5] = (self.low_rows(k), core, int(core == 0), int(core == 1 and last), low)
            out[device, 5:7] = (joined[core], joined[1 - core])
        return out

    def outward(self):
        pairs = []
        for group in range(self.groups):
            for k in range(self.depth):
                pairs.append((self.device(group, k, 0), self.device(group, (k - 1) % self.depth, 0)))
                pairs.append((self.device(group, k, 1), self.device(group, (k + 1) % self.depth, 1)))
        return pairs


def in_three(x):
    high = x.astype(jnp.bfloat16).astype(jnp.float32)
    rest = x - high
    middle = rest.astype(jnp.bfloat16).astype(jnp.float32)
    return [high, middle, rest - middle]


def pack_kernel(plan, tapers, code_hbm, taper_hbm, a_ref, f_hbm, out_ref,
                code_ref, taper_ref, f_ref, near_ref, sent_ref, small_sem, in_sem, out_sem):
    share, size = plan.depth + 1, plan.count // plan.groups

    def fetch(group):
        run = pl.ds(group * share, share)
        return pltpu.make_async_copy(a_ref.at[run], near_ref.at[run], in_sem.at[group])

    small = [
        pltpu.make_async_copy(source, target, small_sem.at[n])
        for n, (source, target) in enumerate(((code_hbm, code_ref), (taper_hbm, taper_ref), (f_hbm, f_ref)))
    ]
    for copy in small:
        copy.start()
    for group in range(plan.groups):
        fetch(group).start()
    for copy in small:
        copy.wait()
    forcing = in_three(f_ref[:, 0, :])
    lane = lax.broadcasted_iota(jnp.int32, (1, LANES), 1)
    weights = jnp.zeros((1, LANES), jnp.float32)
    for k in range(len(DIRECTIONS)):
        code = code_ref[0, 0, k]
        weight = jnp.float32(0)
        for c in range(tapers):
            weight = jnp.where(code == c + 1, taper_ref[c], weight)
        weights = jnp.where(lane == k, weight, weights)
    high, middle, _ = in_three(weights)
    copies = []
    for device, k, core, low in plan.owners():
        if low % share == 0 and core == 0:
            fetch(low // share).wait()
        count, other = plan.low_rows(k), plan.rows - plan.low_rows(k)
        start, after = k * plan.step + core * count, core * other
        for half in range(2):
            lanes = slice(half * LANES, (half + 1) * LANES)
            pieces = [
                near_ref[low, start : start + count, lanes].astype(jnp.float32),
                near_ref[low + 1, after : after + other, lanes].astype(jnp.float32),
            ]
            pieces += [part[low : low + 1, lanes] for part in forcing]
            spare = plan.block - plan.rows - 3
            if spare:
                pieces.append(jnp.zeros((spare, LANES), jnp.float32))
            sent_ref[device, half * plan.block : (half + 1) * plan.block, :] = jnp.concatenate(
                pieces, axis=0
            ).astype(jnp.bfloat16)
        pieces = [part[low + 1 : low + 2, :LANES] for part in forcing]
        pieces += [part[low + 1 : low + 2, LANES:] for part in forcing]
        sent_ref[device, 2 * plan.block :, :] = jnp.concatenate(pieces + [high, middle], axis=0).astype(jnp.bfloat16)
        if k == plan.depth - 1 and core == 1:
            run = pl.ds(len(copies) * size, size)
            copies.append(pltpu.make_async_copy(sent_ref.at[run], out_ref.at[run], out_sem.at[len(copies)]))
            copies[-1].start()
    for copy in copies:
        copy.wait()


def build_maps(side, kernel_ref, lt_ref, by_lat_ref, turned_ref):
    span = 4 * side - 1
    wide = (span + 1) * side
    square = (lax.broadcasted_iota(jnp.int32, (span, span), 0)
              == lax.broadcasted_iota(jnp.int32, (span, span), 1))
    table = kernel_ref[...].astype(jnp.bfloat16)
    flipped = lax.dot_general(
        square.astype(jnp.float32).astype(jnp.bfloat16), table, (((1,), (1,)), ((), ())),
        preferred_element_type=jnp.float32,
    ).astype(jnp.bfloat16)
    block = lax.broadcasted_iota(jnp.int32, (span, wide), 1) // side
    pick = (lax.broadcasted_iota(jnp.int32, (span, wide), 0) == span - 1 - block)
    by_lat_ref[...] = jnp.dot(
        flipped, pick.astype(jnp.float32).astype(jnp.bfloat16), preferred_element_type=jnp.float32
    )
    lane = lax.broadcasted_iota(jnp.int32, (3 * side, wide), 1) % side
    base = jnp.zeros((3 * side, wide), jnp.float32)
    for x in range(side):
        base = jnp.where(lane == x, by_lat_ref[side - 1 - x : 4 * side - 1 - x, :], base)
    turns = LANES // side
    for turn in range(turns):
        moved = base if turn == 0 else pltpu.roll(base, wide - turn * side, 1)
        turned_ref[turn] = moved.astype(jnp.bfloat16)
    for k, (p, q) in enumerate(ALL_STEPS):
        for y in range(side):
            start = (2 * side - 1 - p * side - y) * side
            turn, first = (start % LANES) // side, start // LANES * LANES
            lt_ref[k, y * side : (y + 1) * side, :] = turned_ref[
                turn, (q + 1) * side : (q + 2) * side, first : first + side * side
            ]


def read_extra(plan, got_ref, wide_ref):
    first = plan.rows // 16 * 16
    at = plan.rows - first
    tail = got_ref[:, 2 * plan.block :, :].astype(jnp.float32)
    weights = tail[:, 6, :] + tail[:, 7, :]
    for k in range(len(DIRECTIONS)):
        wide_ref[k] = jnp.broadcast_to(weights[:, k : k + 1], (plan.count, plan.columns))
    low, high = [], []
    for half in range(2):
        slab = got_ref[:, half * plan.block + first : (half + 1) * plan.block, :].astype(jnp.float32)
        low.append(slab[:, at, :] + slab[:, at + 1, :] + slab[:, at + 2, :])
        high.append(tail[:, 3 * half, :] + tail[:, 3 * half + 1, :] + tail[:, 3 * half + 2, :])
    return [jnp.concatenate(low, axis=1), jnp.concatenate(high, axis=1)]


def apply_rows(plan, low, order, got_ref, v_ref, lt_ref, wide_ref, w_ref, s_ref, p_ref):
    bands, lons, rows = plan.bands, plan.lons, plan.block
    place = lax.broadcasted_iota(jnp.int32, (rows, LANES), 0)
    is_low = place < low
    sides = [slice(half * LANES, (half + 1) * LANES) for half in range(2)]

    def block(tile, half):
        return got_ref[tile, half * rows : (half + 1) * rows, :].astype(jnp.float32)

    for tile in range(plan.count):
        v_low, v_high = v_ref[0, tile : tile + 1, :], v_ref[1, tile : tile + 1, :]
        for half, lanes in enumerate(sides):
            v = jnp.where(is_low, v_low[:, lanes], v_high[:, lanes])
            w_ref[tile * rows : (tile + 1) * rows, lanes] = (block(tile, half) * v).astype(jnp.bfloat16)

    scale = jnp.float32(1.0 / (plan.members - 1))
    low_share = jnp.where(is_low, scale, jnp.float32(0))
    high_share = jnp.where(is_low | (place >= plan.rows), jnp.float32(0), scale)
    low_end = min(-(-plan.low_rows(0) // GRAIN) * GRAIN, rows)
    sums = {}

    def finish(tile, spread):
        for half, lanes in enumerate(sides):
            product = block(tile, half) * spread[:, lanes]
            sums[tile, 0, half] = jnp.sum(product[:low_end] * low_share[:low_end], axis=0, keepdims=True)
            sums[tile, 1, half] = jnp.sum(product * high_share, axis=0, keepdims=True)

    touched = set()
    steps = sorted(ALL_STEPS, key=lambda step: (step[0] == 0, step == (0, 0)))
    for start in range(0, bands, CHUNK):
        stop = min(start + CHUNK, bands)
        for p, q in steps:
            first, last = max(0, start + p), min(bands, stop + p)
            if first >= last:
                continue
            k = ALL_STEPS.index((p, q))
            y = jnp.dot(
                w_ref[first * lons * rows : last * lons * rows, :], lt_ref[k], preferred_element_type=jnp.float32
            )
            for band in range(first, last):
                for l in range(lons):
                    tile = (band - p) * lons + (l - q) % lons
                    at = ((band - first) * lons + l) * rows
                    term = y[at : at + rows]
                    if k == 0:
                        finish(tile, s_ref[tile] + term)
                        continue
                    term = term * wide_ref[k - 1, tile : tile + 1, :]
                    if tile in touched:
                        s_ref[tile] += term
                    else:
                        s_ref[tile] = term
                        touched.add(tile)
                if k == 0:
                    for level in range(2):
                        for half, lanes in enumerate(sides):
                            p_ref[order[level], band, :, lanes] = jnp.concatenate(
                                [sums[band * lons + l, level, half] for l in range(lons)], axis=0
                            )


def first_kernel(plan, info_ref, got_ref, lt_ref, p_ref, v_ref, wide_ref, w_ref, s_ref):
    v_ref[0], v_ref[1] = read_extra(plan, got_ref, wide_ref)
    order = (info_ref[1], 1 - info_ref[1])
    apply_rows(plan, info_ref[0], order, got_ref, v_ref, lt_ref, wide_ref, w_ref, s_ref, p_ref)


def total(x):
    return jnp.sum(jnp.sum(x, axis=1, keepdims=True), axis=0, keepdims=True)


def second_kernel(plan, info_ref, got_ref, lt_ref, b_ref, wide_ref, own_ref, other_ref, far_ref, far_other_ref,
                  out_ref, v_ref, w_ref, s_ref, p_ref):
    mine = (own_ref[0] + other_ref[1]) + jnp.where(info_ref[6] > 0, far_other_ref[...], 0.0)
    rest = (own_ref[1] + other_ref[0]) + jnp.where(info_ref[5] > 0, far_ref[...], 0.0)
    first_core = info_ref[1] == 0
    images = (jnp.where(first_core, mine, rest), jnp.where(first_core, rest, mine))
    lane = lax.broadcasted_iota(jnp.int32, (1, LANES), 1)
    first = jnp.zeros((1, LANES), jnp.float32)
    for level in range(2):
        b = b_ref[level]
        u = images[level]
        bb, bu = total(b * b), total(b * u)
        ratio = jnp.where(bb > 0, bu / jnp.where(bb > 0, bb, 1.0), 0.0)
        q = ratio * b - u
        v_ref[level] = q
        values = (bb, total(b * q), total(q * q), ratio)
        speaks = jnp.where(info_ref[2 + level] > 0, jnp.float32(1), jnp.float32(0))
        for n, value in enumerate(values):
            at = lane == info_ref[4] + level + SLOT * n
            first = first + jnp.where(at, value, 0.0) * speaks
    apply_rows(plan, info_ref[0], (0, 1), got_ref, v_ref, lt_ref, wide_ref, w_ref, s_ref, p_ref)
    second = jnp.zeros((1, LANES), jnp.float32)
    for level in range(2):
        b = b_ref[level]
        t = p_ref[level].reshape(plan.count, plan.columns)
        for n, value in enumerate((total(v_ref[level] * t), total(b * t))):
            at = lane == info_ref[4] + level + SLOT * n
            second = second + jnp.where(at, value, 0.0)
    for half in range(2):
        lanes = slice(half * LANES, (half + 1) * LANES)
        out_ref[:, half, :] = mine[:, lanes]
        for level in range(2):
            share = p_ref[level, :, :, lanes].reshape(plan.count, LANES)
            out_ref[:, 2 + 2 * level + half, :] = share
    out_ref[:, 6, :] = jnp.broadcast_to(first, (plan.count, LANES))
    out_ref[:, 7, :] = jnp.broadcast_to(second, (plan.count, LANES))


def last_kernel(plan, f_ref, got_ref, inc_ref, res_ref, u_ref, t_ref):
    depth = plan.depth
    for level in range(plan.levels):
        group, j = divmod(level, depth + 1)
        speaker = plan.device(group, j, 0) if j < depth else plan.device(group, depth - 1, 1)
        for half in range(2):
            lanes = slice(half * LANES, (half + 1) * LANES)
            u_ref[level : level + 1, lanes] = got_ref[speaker, half : half + 1, :]
            t = None
            for core in range(2):
                for part in (0, 1):
                    k = j - part
                    if 0 <= k < depth:
                        row = 2 + 2 * part + half
                        term = got_ref[plan.device(group, k, core), row : row + 1, :]
                        t = term if t is None else t + term
            t_ref[level : level + 1, lanes] = t
    firsts = jnp.zeros((1, LANES), jnp.float32)
    seconds = jnp.zeros((1, LANES), jnp.float32)
    for device, _, _, _ in plan.owners():
        firsts = firsts + got_ref[device, 6:7, :]
        seconds = seconds + got_ref[device, 7:8, :]
    lane = lax.broadcasted_iota(jnp.int32, (1, LANES), 1)
    kept = lane < plan.levels

    def slot(row, n):
        moved = row if n == 0 else pltpu.roll(row, LANES - SLOT * n, 1)
        return jnp.where(kept, moved, 0.0)

    bb, bq, qq, ratio = (slot(firsts, n) for n in range(4))
    qt, bt = (slot(seconds, n) for n in range(2))

    def add(x):
        return jnp.sum(x, axis=1, keepdims=True)

    all_bb = add(bb)
    all_bu = add(ratio * bb - bq)
    whole = all_bu / all_bb
    shift = jnp.where(kept, whole - ratio, 0.0)
    q_q = add(shift * shift * bb + 2 * shift * bq + qq)
    q_bq = add(shift * shift * ratio * bb - shift * shift * bq + shift * bt
               + shift * ratio * bq - shift * qq + qt)
    b_bq = add(shift * ratio * bb - shift * bq + bt)
    q_u = add(shift * ratio * bb - shift * bq + ratio * bq - qq)
    energy = all_bb + all_bu
    step_0 = all_bb / energy
    norm_1 = step_0 * step_0 * q_q
    turn = norm_1 / all_bb
    curve = (step_0 * step_0 * (q_q + q_bq) + turn * step_0 * (q_u + b_bq) + turn * turn * energy)
    step_1 = norm_1 / curve

    rows = lax.broadcasted_iota(jnp.int32, (plan.levels, LANES), 0)
    diagonal = rows == lax.broadcasted_iota(jnp.int32, (plan.levels, LANES), 1)
    ratio_c = add(jnp.where(diagonal, ratio, 0.0))
    shift_c = add(jnp.where(diagonal, shift, 0.0))
    b, u, t = f_ref[:, 0, :], u_ref[...], t_ref[...]
    q = shift_c * b + (ratio_c * b - u)
    b_of_q = shift_c * u + t
    direction = step_0 * q + turn * b
    inc_ref[:, 0, :] = step_0 * b + step_1 * direction
    res_ref[:, 0, :] = step_0 * q - step_1 * (step_0 * (q + b_of_q) + turn * (b + u))


def room(mib):
    return pltpu.CompilerParams(vmem_limit_bytes=mib << 20)


def vmem():
    return pl.BlockSpec(memory_space=pltpu.VMEM)


def smem():
    return pl.BlockSpec(memory_space=pltpu.SMEM)


def by_levels(plan, anomalies, forcing, pair_code, kernel, tile_taper):
    axes = ("band", "tile")
    bf16, f32 = jnp.bfloat16, jnp.float32
    n, rows, columns = plan.count, plan.block, plan.columns
    side = (kernel.shape[0] + 1) // 4
    wide = 4 * side * side
    a, f = anomalies[0, 0], jnp.swapaxes(forcing[0], 0, 1)
    sent = pl.pallas_call(
        functools.partial(pack_kernel, plan, tile_taper.shape[0]),
        out_shape=jax.ShapeDtypeStruct((n, plan.height, LANES), bf16),
        in_specs=[pl.BlockSpec(memory_space=pl.ANY)] * 4,
        out_specs=pl.BlockSpec(memory_space=pl.ANY),
        scratch_shapes=[pltpu.SMEM(pair_code.shape, jnp.int32),
                        pltpu.SMEM(tile_taper.shape, f32),
                        pltpu.VMEM(f.shape, f32),
                        pltpu.VMEM(a.shape, bf16),
                        pltpu.VMEM((n, plan.height, LANES), bf16),
                        pltpu.SemaphoreType.DMA((3,)),
                        pltpu.SemaphoreType.DMA((plan.groups,)),
                        pltpu.SemaphoreType.DMA((plan.groups,))],
        name="pack",
    )(pair_code, tile_taper, a, f)
    got = lax.all_to_all(sent, axes, 0, 0)
    me = lax.axis_index(axes)
    info = lax.dynamic_slice(jnp.asarray(plan.table()), (me, 0), (1, 8))[0]
    both = jax.ShapeDtypeStruct((2, n, columns), f32)
    shares = jax.ShapeDtypeStruct((2, plan.bands, plan.lons, columns), f32)
    weights = jax.ShapeDtypeStruct((len(DIRECTIONS), n, columns), f32)
    work = [pltpu.VMEM((n * rows, columns), bf16), pltpu.VMEM((n, rows, columns), f32)]
    maps = pl.pallas_call(
        functools.partial(build_maps, side),
        out_shape=jax.ShapeDtypeStruct((len(ALL_STEPS), columns, columns), bf16),
        in_specs=[vmem()],
        out_specs=vmem(),
        scratch_shapes=[pltpu.VMEM((4 * side - 1, wide), f32),
                        pltpu.VMEM((LANES // side, 3 * side, wide), bf16)],
        cost_estimate=pl.CostEstimate(flops=200_000_000, bytes_accessed=2_000_000, transcendentals=0),
        compiler_params=room(12),
        name="maps",
    )(kernel)
    part, b, wide_weights = pl.pallas_call(
        functools.partial(first_kernel, plan),
        out_shape=(shares, both, weights),
        in_specs=[smem(), vmem(), vmem()],
        out_specs=(vmem(),) * 3,
        scratch_shapes=work,
        compiler_params=room(20),
        name="first",
    )(info, got, maps)
    part = part.reshape(2, n, columns)
    swap = [(i, i ^ 1) for i in range(plan.lons)]
    other = lax.ppermute(part, "tile", swap)
    outward = plan.outward()
    far = lax.ppermute(part[0] + other[1], axes, outward)
    far_other = lax.ppermute(part[1] + other[0], axes, [(target, source) for source, target in outward])
    back = pl.pallas_call(
        functools.partial(second_kernel, plan),
        out_shape=jax.ShapeDtypeStruct((n, 8, LANES), f32),
        in_specs=[smem()] + [vmem()] * 8,
        out_specs=vmem(),
        scratch_shapes=[pltpu.VMEM(both.shape, f32)] + work + [pltpu.VMEM(shares.shape, f32)],
        compiler_params=room(20),
        name="second",
    )(info, got, maps, b, wide_weights, part, other, far, far_other)
    home = lax.all_to_all(back, axes, 0, 0)
    increment, residual = pl.pallas_call(
        functools.partial(last_kernel, plan),
        out_shape=(jax.ShapeDtypeStruct(f.shape, f32),) * 2,
        in_specs=[vmem(), vmem()],
        out_specs=(vmem(), vmem()),
        scratch_shapes=[pltpu.VMEM((plan.levels, columns), f32)] * 2,
        compiler_params=room(8),
        name="last",
    )(f, home)
    return jnp.swapaxes(increment, 0, 1)[None], jnp.swapaxes(residual, 0, 1)[None]


def padded(block, sides, width):
    for axis, dim in sides:
        count = lax.axis_size(axis)
        forward = [(i, i + 1) for i in range(count - 1)]
        forward.append((count - 1, 0))
        backward = [(target, source) for source, target in forward]
        low = lax.ppermute(
            lax.slice_in_dim(block, block.shape[dim] - width, None, axis=dim), axis, forward
        )
        high = lax.ppermute(lax.slice_in_dim(block, 0, width, axis=dim), axis, backward)
        block = jnp.concatenate([low, block, high], axis=dim)
    return block


def selector(tile_side, offset):
    first_index = np.arange(tile_side)[:, None]
    second_index = np.arange(tile_side)[None, :]
    target = 2 * tile_side - 1 + offset * tile_side + second_index - first_index
    return (np.arange(4 * tile_side - 1)[None, None, :] == target[:, :, None]).astype(np.float32)


def local_map(kernel, row_step, col_step):
    by_lat = jnp.einsum(
        "abp,pq->abq", selector(SIDE, row_step), kernel, precision=lax.Precision.HIGHEST
    )
    full_map = jnp.einsum(
        "abq,cdq->acbd", by_lat, selector(SIDE, col_step), precision=lax.Precision.HIGHEST
    )
    return full_map.reshape(SIDE * SIDE, SIDE * SIDE).astype(jnp.bfloat16)


def all_maps(kernel):
    return [local_map(kernel, 0, 0)] + [
        local_map(kernel, row_step, col_step) for row_step, col_step in DIRECTIONS
    ]


def taper_lookup(tile_taper, code):
    entries = jnp.arange(1, tile_taper.shape[0] + 1, dtype=jnp.int32)
    return jnp.sum(jnp.where(entries == code, tile_taper, jnp.zeros_like(tile_taper)))


def weighted_block(block, field):
    return (block.astype(jnp.float32) * field[:, None, :]).astype(jnp.bfloat16)


def pair_term(own_block, weighted, matrix, weight):
    levels, members, columns = weighted.shape
    spread = lax.dot_general(
        weighted.reshape(levels * members, columns),
        matrix,
        (((1,), (1,)), ((), ())),
        preferred_element_type=jnp.float32,
    )
    summed = jnp.sum(
        own_block.astype(jnp.float32) * spread.reshape(levels, members, columns), axis=1
    )
    return summed * (weight / (members - 1))


def masked_term(code, weight, own_block, weighted, matrix):

    def active():
        return pair_term(own_block, weighted, matrix, weight)

    def inactive():
        return jnp.zeros((weighted.shape[0], weighted.shape[2]), jnp.float32)

    return lax.cond(code > 0, active, inactive)


def covariance_all(blocks, neighbours, pair_codes, tile_taper, local_maps):
    own_block = blocks[1, 1]
    summed_terms = pair_term(
        own_block, weighted_block(own_block, neighbours[1, 1]), local_maps[0], 1.0
    )
    for position, (row_step, col_step) in enumerate(DIRECTIONS):
        code = pair_codes[position]
        weight = taper_lookup(tile_taper, code)
        other_weighted = weighted_block(
            blocks[1 + row_step, 1 + col_step], neighbours[1 + row_step, 1 + col_step]
        )
        summed_terms = summed_terms + masked_term(
            code, weight, own_block, other_weighted, local_maps[position + 1]
        )
    return summed_terms


def global_total(factor_one, factor_two):
    return lax.psum(jnp.sum(factor_one * factor_two), ("band", "tile"))


def on_device(anomalies, forcing, pair_code, kernel, tile_taper):
    pair_codes = pair_code[0, 0]
    kept_maps = all_maps(kernel)
    residual = forcing[0, 0]
    increment = jnp.zeros_like(residual)
    direction = residual
    norm_now = global_total(residual, residual)
    for iteration in range(ITERS):
        blocks = padded(anomalies, (("band", 0), ("tile", 1)), 1)
        neighbours = padded(direction[None, None], (("band", 0), ("tile", 1)), 1)
        mapped = direction + covariance_all(blocks, neighbours, pair_codes, tile_taper, kept_maps)
        step_length = norm_now / global_total(direction, mapped)
        increment = increment + step_length * direction
        residual = residual - step_length * mapped
        norm_next = global_total(residual, residual)
        direction = residual + norm_next / norm_now * direction
        norm_now = norm_next
    return (increment[None, None], residual[None, None])


def solution(mesh):
    specs = (
        P("band", "tile", None, None, None),
        P("band", "tile", None, None),
        P("band", "tile", None),
        P(),
        P(),
    )

    def run(anomalies, forcing, pair_code, kernel, tile_taper):
        plan = Plan(mesh.shape["band"], mesh.shape["tile"], *anomalies.shape[2:])
        step = functools.partial(by_levels, plan) if plan.fits else on_device
        return step(anomalies, forcing, pair_code, kernel, tile_taper)

    return jax.shard_map(
        run,
        mesh=mesh,
        in_specs=specs,
        out_specs=(P("band", "tile", None, None), P("band", "tile", None, None)),
        check_vma=False,
    )
```
